256 devices in a mesh: row: 4 (over x), col: 64 (over y, z, core).
Axes of the slice: x: 4, y: 4, z: 8, core: 2. Of those that a mesh axis runs over, the one named last changes fastest.
Arguments:
- state: float32 [3, 10, 1048576], P(None, None, ('row', 'col')), may hold values from -6 to 6
- depth: float32 [1048576], P(('row', 'col')), may hold values from 1 to 18
- metric: float32 [4, 1048576], P(None, ('row', 'col')), may hold values from -4 to 4, as said below
- partner: int32 [1048576], P(('row', 'col')), may hold values from -63 to 63, as said below
- refine: int32 [1048576], P(('row', 'col')), may hold values from 0 to 1, as said below
- diff_ops: float32 [2, 10, 10], replicated, may hold values from -2 to 2
- lift: float32 [10, 12], replicated, may hold values from -1.75 to 1.75
- prolong: float32 [2, 10, 10], replicated, may hold values from -2 to 2
Outputs:
- refined: float32 [3, 10, 1572864], P(None, None, ('row', 'col'))
The draws below stay inside these ranges and needn't reach their ends.
Inputs may be any that keep to these rules, and one draw needn't show every extreme that they name: `metric`: (r_x, r_y) and (s_x, s_y) are orthogonal and of equal length, between 1 and 4. Where partner[i] is not 0, j = i + partner[i] is a triangle with partner[j] = -partner[i]; an offset of size 63 occurs in every draw. `refine`: split the curve into sections of 4096 consecutive triangles. The refinements before section k number k * 2048 plus an offset between -1024 and 1024, and both ends of that range occur in every draw; all refinements together number 1048576 / 2.
All inputs are finite; a program needn't handle non-finite values.
Results may differ from the reference program's by a relative error of at most 0.000076.
Values sent between devices are 32-bit elements; how exact they have to be, the bound alone decides.
A program may use at most 64 MiB of HBM per device.

```python
import jax
import jax.numpy as jnp
import numpy as np
from jax import lax

E_DEV = 4096
RIM = 64
NE = 1048576
NEW = 1572864


def draw_depth(key, part):
    total = NE
    keys = jax.random.split(key, 3)
    position = jnp.arange(total, dtype=jnp.float32) / total
    center = jax.random.uniform(keys[1], (), jnp.float32, 0.0, 1.0)
    height = jax.random.uniform(keys[2], (), jnp.float32, 4.0, 8.0)
    bump = jnp.maximum(0.0, 1.0 - 8.0 * jnp.abs(position - center))
    trend = 1.0 + height * bump
    rough = jnp.exp(jax.random.uniform(keys[0], (total,), jnp.float32, 0.0, jnp.log(2.0)))
    return (trend * rough).astype(jnp.float32)


def draw_metric(key, part):
    total = NE
    keys = jax.random.split(key, 3)
    size = jnp.exp(jax.random.uniform(keys[0], (total,), jnp.float32, 0.0, jnp.log(4.0)))
    turn = jax.random.randint(keys[1], (total,), 0, 8).astype(jnp.float32) * (jnp.pi / 4.0)
    mirror = 1.0 - 2.0 * jax.random.randint(keys[2], (total,), 0, 2).astype(jnp.float32)
    cosine = size * jnp.cos(turn)
    sine = size * jnp.sin(turn)
    return jnp.stack([cosine, sine, -sine * mirror, cosine * mirror]).astype(jnp.float32)


def draw_partner(key, part):
    total = NE
    sections = NE // E_DEV
    keys = jax.random.split(key, 6)
    index = jnp.arange(total, dtype=jnp.int32)
    back_all = jax.random.randint(keys[0], (sections + 1,), 1, RIM)
    high = jax.random.randint(keys[1], (), 1, sections)
    low = 1 + (high - 1 + jax.random.randint(keys[2], (), 1, sections - 1)) % (sections - 1)
    back_all = back_all.at[high].set(1).at[low].set(RIM - 1)
    nearest = ((index + E_DEV // 2) // E_DEV).astype(jnp.int32)
    real_end = (nearest >= 1) & (nearest <= sections - 1)
    back = jnp.take(back_all, nearest)
    cross_start = nearest * E_DEV - back
    in_cross = real_end & (index >= cross_start) & (index < cross_start + RIM)
    after_cross = real_end & (index == cross_start + RIM)
    grid = (index % RIM == 0) & ~in_cross
    windows = total // RIM + 1
    quiet = jax.random.randint(keys[4], (windows,), 0, 8) == 0
    loose = (jax.random.randint(keys[3], (total,), 0, 3) == 0) & (index % 2 == 0) & (index % RIM != 0) & ~in_cross & ~quiet[index // RIM]
    mark = grid | in_cross & (index == cross_start) | after_cross | loose | (index == 0)
    start = lax.cummax(jnp.where(mark, index, 0))
    marked = jnp.where(mark, index, total)
    after = jnp.concatenate([marked[1:], jnp.full((1,), total, jnp.int32)])
    finish = lax.cummin(after, reverse=True)
    paired = start + finish - 1 - index
    coast_bits = jax.random.randint(keys[5], (total,), 0, 4) == 0
    coast = jnp.take(coast_bits, start) & ~in_cross
    return jnp.where(coast, 0, paired - index).astype(jnp.int32)


def shuffled(subkey):
    return jax.random.permutation(subkey, E_DEV)


def draw_refine(key, part):
    sections = NE // E_DEV
    keys = jax.random.split(key, 4)
    quarter = E_DEV // 4
    drift = jax.random.randint(keys[0], (sections + 1,), -quarter, quarter + 1)
    high = jax.random.randint(keys[1], (), 1, sections)
    low = 1 + (high - 1 + jax.random.randint(keys[2], (), 1, sections - 1)) % (sections - 1)
    drift = drift.at[high].set(quarter).at[low].set(-quarter)
    drift = drift.at[0].set(0).at[sections].set(0)
    amount = E_DEV // 2 + drift[1:] - drift[:-1]
    order = jax.vmap(shuffled)(jax.random.split(keys[3], sections))
    return (order < amount[:, None]).astype(jnp.int32).reshape(-1)


def block_levels(stream_key, shape, cuts, smallest, largest):
    loudness = 1.0
    for dim, blocks in cuts:
        draws = jax.random.uniform(jax.random.fold_in(jax.random.fold_in(stream_key, 6), dim), (blocks,), jnp.float32, smallest / len(cuts), largest / len(cuts))
        loudness = loudness * jnp.repeat(jnp.exp(draws), shape[dim] // blocks).reshape((-1,) + (1,) * (len(shape) - 1 - dim))
    return loudness


def scatter_about(stream_key, dims, spread, bound, pieces=(), kind=jnp.bfloat16):
    loudness = block_levels(stream_key, dims, pieces, -0.22, 0.18) if pieces else 1.0
    entries = jax.random.normal(stream_key, dims, jnp.float32) * spread * loudness
    return jnp.minimum(jnp.maximum(entries, -bound), bound).astype(kind)


def setup_inputs(seed: int = 0) -> dict:
    arg_keys = jax.random.split(jax.random.key(seed), 9)
    return {
        "state": scatter_about(arg_keys[0], (3, 10, NE), 1.0, 6.0, ((2, 256),), jnp.float32),
        "depth": draw_depth(jax.random.fold_in(arg_keys[8], 71), 0),
        "metric": draw_metric(jax.random.fold_in(arg_keys[8], 71), 0),
        "partner": draw_partner(jax.random.fold_in(arg_keys[8], 71), 0),
        "refine": draw_refine(jax.random.fold_in(arg_keys[8], 71), 0),
        "diff_ops": scatter_about(arg_keys[5], (2, 10, 10), 10 ** -0.5, 2.0, (), jnp.float32),
        "lift": scatter_about(arg_keys[6], (10, 12), 12 ** -0.5, 1.75, (), jnp.float32),
        "prolong": scatter_about(arg_keys[7], (2, 10, 10), 10 ** -0.5, 2.0, (), jnp.float32),
    }


GRAVITY = 9.81
COURANT = 0.5
FACE_NODES = (0, 1, 2, 3, 3, 6, 8, 9, 9, 7, 4, 0)
HIGH = lax.Precision.HIGHEST

def apply_ops(matrix, field):
    return jnp.einsum('ab,fbx->fax', matrix, field, precision=HIGH)

def normal_flux(values, speed_sq, normal_x, normal_y):
    return jnp.stack([values[1] * normal_x + values[2] * normal_y, speed_sq * values[0] * normal_x, speed_sq * values[0] * normal_y])

def face_vectors(metric):
    grad_rx, grad_ry, grad_sx, grad_sy = (metric[0], metric[1], metric[2], metric[3])
    return ((-grad_sx, -grad_sy), (grad_rx + grad_sx, grad_ry + grad_sy), (-grad_rx, -grad_ry))

def wave_rate(depth, metric):
    lengths = [jnp.sqrt(vx * vx + vy * vy) for vx, vy in face_vectors(metric)]
    return jnp.sqrt(GRAVITY * depth) * jnp.maximum(jnp.maximum(lengths[0], lengths[1]), lengths[2])

def tendency(state, depth, metric, outer, outer_depth, walls, diff_ops, lift):
    speed_sq = GRAVITY * depth
    grad_rx, grad_ry, grad_sx, grad_sy = (metric[0], metric[1], metric[2], metric[3])
    moved = jnp.stack([state[1], state[2], state[0]])
    along_r = apply_ops(diff_ops[0], moved)
    along_s = apply_ops(diff_ops[1], moved)
    vol_eta = -(grad_rx * along_r[0] + grad_sx * along_s[0] + grad_ry * along_r[1] + grad_sy * along_s[1])
    vol_mx = -speed_sq * (grad_rx * along_r[2] + grad_sx * along_s[2])
    vol_my = -speed_sq * (grad_ry * along_r[2] + grad_sy * along_s[2])
    inner = jnp.take(state, np.array(FACE_NODES), axis=1)
    jumps = []
    for edge_num, (vec_x, vec_y) in enumerate(face_vectors(metric)):
        length = jnp.sqrt(vec_x * vec_x + vec_y * vec_y)
        normal_x = vec_x / length
        normal_y = vec_y / length
        inside = inner[:, 4 * edge_num:4 * edge_num + 4, :]
        normal_m = inside[1] * normal_x + inside[2] * normal_y
        ghost = jnp.stack([inside[0], inside[1] - 2.0 * normal_m * normal_x, inside[2] - 2.0 * normal_m * normal_y])
        closed = walls[edge_num]
        outside = jnp.where(closed, ghost, outer[edge_num])
        outside_sq = jnp.where(closed, speed_sq, GRAVITY * outer_depth[edge_num])
        flux_in = normal_flux(inside, speed_sq, normal_x, normal_y)
        flux_out = normal_flux(outside, outside_sq, normal_x, normal_y)
        wave_top = jnp.sqrt(jnp.maximum(speed_sq, outside_sq))
        common = 0.5 * (flux_in + flux_out) - 0.5 * wave_top * (outside - inside)
        jumps.append(length * (flux_in - common))
    surface = apply_ops(lift, jnp.concatenate(jumps, axis=1))
    return jnp.stack([vol_eta, vol_mx, vol_my]) + surface

def neighbour_values(current, depth, partner):
    total = current.shape[2]
    index = jnp.arange(total, dtype=jnp.int32)
    traces = jnp.take(current, np.array(FACE_NODES), axis=1)
    zero_col = jnp.zeros((3, 4, 1), current.dtype)
    from_prev = jnp.concatenate([zero_col, traces[:, 7:3:-1, :-1]], axis=2)
    from_next = jnp.concatenate([traces[:, 3::-1, 1:], zero_col], axis=2)
    safe = jnp.clip(index + partner.astype(jnp.int32), 0, total - 1).astype(jnp.int32)
    from_pair = jnp.take(traces[:, 11:7:-1, :], safe, axis=2)
    depth_prev = jnp.concatenate([depth[:1], depth[:-1]])
    depth_next = jnp.concatenate([depth[1:], depth[-1:]])
    depth_pair = jnp.take(depth, safe)
    walls = (index == 0, index == total - 1, partner == 0)
    return ((from_prev, from_next, from_pair), (depth_prev, depth_next, depth_pair), walls)

def reference(state, depth, metric, partner, refine, diff_ops, lift, prolong):
    step = COURANT / jnp.max(wave_rate(depth, metric))

    def rhs(current):
        outer, outer_depth, walls = neighbour_values(current, depth, partner)
        return tendency(current, depth, metric, outer, outer_depth, walls, diff_ops, lift)
    first = state + step * rhs(state)
    second = 0.5 * state + 0.5 * (first + step * rhs(first))
    counts = (1 + refine).astype(jnp.int32)
    ends = jnp.cumsum(counts).astype(jnp.int32)
    starts = ends - counts
    slots = jnp.arange(NEW, dtype=jnp.int32)
    parent = jnp.searchsorted(ends, slots, side='right').astype(jnp.int32)
    which = slots - jnp.take(starts, parent)
    child_one = jnp.where(refine == 1, apply_ops(prolong[0], second), second)
    child_two = apply_ops(prolong[1], second)
    return jnp.where(which == 0, jnp.take(child_one, parent, axis=2), jnp.take(child_two, parent, axis=2))
```

```python
import functools

import jax
import jax.numpy as jnp
from jax import lax
from jax.experimental import pallas as pl
from jax.experimental.pallas import tpu as pltpu
from jax.sharding import PartitionSpec as P

GRAVITY = 9.81
COURANT = 0.5
MESH = pl.DeviceIdType.MESH

OWN = 32
HALO = 9
WIDE = HALO * 128
BASE = 24
MEM = 72
QP = 40
RP = 32
XP = 96

FACES = ((0, 1, 2, 3), (3, 6, 8, 9), (9, 7, 4, 0))
MEET = ((9, 8, 6, 3), (3, 2, 1, 0), (0, 4, 7, 9))

f32 = jnp.float32
bf16 = jnp.bfloat16
i32 = jnp.int32


def lanes_of(shape):
    return lax.broadcasted_iota(i32, shape, len(shape) - 1)


def state_row(f, n):
    return 4 * n + f


def result_row(f, n):
    return 10 * f + n


def spread(ref, v, tile, pitch):
    return ref[pl.ds(tile * pitch + v, 8, stride=pitch), :]


def put(ref, v, tile, pitch, value):
    ref[pl.ds(tile * pitch + v, 8, stride=pitch), :] = value


def pick(x, idx):
    return jnp.take_along_axis(x, idx, axis=1, mode="promise_in_bounds")


def split(x):
    hi = x.astype(bf16)
    return hi, (x - hi.astype(f32)).astype(bf16)


def exchange(
    rows, cols, low,
    state, metric, depth, partner, refine,
    ls, lm, ld, lp, lr, rs, rm, rd, rp, rr, stat,
    mt, mine, box1, pair2, box2, send, recv, send1, recv1, send2, recv2,
):
    total = rows * cols
    high = total // low
    me = lax.axis_index("row") * cols + lax.axis_index("col")
    lo, hi = lax.rem(me, low), me // low

    def at(flat):
        return (flat // cols, lax.rem(flat, cols))

    right = at(lax.rem(me + 1, total))
    left = at(lax.rem(me + total - 1, total))
    peers1 = [at(hi * low + lax.rem(lo + d, low)) for d in range(1, low)]
    peers2 = [at(lax.rem(hi + d, high) * low + lo) for d in range(1, high)]

    barrier = pltpu.get_barrier_semaphore()
    everyone = [left, right] + peers1 + peers2
    for peer in everyone:
        pl.semaphore_signal(barrier, inc=1, device_id=peer, device_id_type=MESH)

    for t in range(OWN):
        mt[t * 8 : t * 8 + 4, :] = metric[:, t * 128 : (t + 1) * 128]
    grads = [mt[pl.ds(k, OWN, stride=8), :] for k in range(4)]
    rate = wave_rate(depth[...], grads)
    top = jnp.max(jnp.max(rate, axis=1, keepdims=True), axis=0, keepdims=True)
    count = refine[...].astype(f32)
    count = jnp.sum(jnp.sum(count, axis=1, keepdims=True), axis=0, keepdims=True)
    first_row = lax.broadcasted_iota(i32, (8, 128), 0) == 0
    mine[...] = jnp.where(first_row, top, count)

    pl.semaphore_wait(barrier, len(everyone))

    copies = []
    sides = (
        (right, (state.at[:, :, pl.ds((OWN - HALO) * 128, WIDE)], metric.at[:, pl.ds((OWN - HALO) * 128, WIDE)],
                 depth.at[pl.ds(16, 16)], partner.at[pl.ds(16, 16)], refine.at[pl.ds(16, 16)]), (ls, lm, ld, lp, lr)),
        (left, (state.at[:, :, pl.ds(0, WIDE)], metric.at[:, pl.ds(0, WIDE)],
                depth.at[pl.ds(0, 16)], partner.at[pl.ds(0, 16)], refine.at[pl.ds(0, 16)]), (rs, rm, rd, rp, rr)),
    )
    for peer, sources, targets in sides:
        for source, target in zip(sources, targets):
            k = len(copies)
            copies.append(pltpu.make_async_remote_copy(
                src_ref=source, dst_ref=target, send_sem=send.at[k], recv_sem=recv.at[k],
                device_id=peer, device_id_type=MESH))
    for copy in copies:
        copy.start()

    def round_of(source, box, peers, sems, rems):
        batch = [
            pltpu.make_async_remote_copy(
                src_ref=source, dst_ref=box.at[d], send_sem=sems.at[d], recv_sem=rems.at[d],
                device_id=peer, device_id_type=MESH)
            for d, peer in enumerate(peers)
        ]
        for copy in batch:
            copy.start()
        for copy in batch:
            copy.wait()

    def joined(own, box, size, position):
        best, both, before = own, own, jnp.zeros_like(own)
        for d in range(size - 1):
            part = box[d]
            best = jnp.maximum(best, part)
            both = both + part
            before = before + jnp.where(d + 1 <= position, part, 0.0)
        return best, both, before

    round_of(mine, box1, peers1, send1, recv1)
    best, both, before1 = joined(mine[...], box1, low, lo)
    pair2[...] = jnp.where(first_row, best, both)
    round_of(pair2, box2, peers2, send2, recv2)
    best, _, before2 = joined(pair2[...], box2, high, hi)
    offset = before1 + before2 - (me * (OWN * 64)).astype(f32)
    stat[...] = jnp.where(first_row, best, offset)
    for copy in copies:
        copy.wait()


def wave_rate(depth, grads):
    gx, gy, hx, hy = grads
    lengths = [jnp.sqrt(vx * vx + vy * vy) for vx, vy in ((hx, hy), (gx + hx, gy + hy), (gx, gy))]
    return jnp.sqrt(GRAVITY * depth) * jnp.maximum(jnp.maximum(lengths[0], lengths[1]), lengths[2])


def load_tiles(own, left, right, qt, mt, cv, pv, ends):
    state, metric, depth, partner = own
    ls, lm, ld, lp = left
    rs, rm, rd, rp = right

    def lay(m, s, g, t):
        here = slice(t * 128, (t + 1) * 128)
        for n in range(10):
            qt[m * QP + 4 * n : m * QP + 4 * n + 3, :] = s[n, :, here]
        mt[m * 8 : m * 8 + 4, :] = g[:, here]

    for t in range(OWN):
        lay(BASE + t, state, metric, t)
    for t in range(HALO):
        lay(BASE - HALO + t, ls, lm, t)
        if t < HALO - 1:
            lay(BASE + OWN + t, rs, rm, t)
    lay(8, rs, rm, HALO - 1)
    lay(64, rs, rm, HALO - 1)
    lay(7, rs, rm, HALO - 2)
    for into, mid, before, after in ((cv, depth, ld, rd), (pv, partner, lp, rp)):
        into[BASE : BASE + OWN, :] = mid[...]
        into[BASE - HALO : BASE, :] = before[16 - HALO : 16, :]
        into[BASE + OWN : BASE + OWN + 8, :] = after[0:8, :]
        into[7:8, :] = after[7:8, :]
        into[8:9, :] = after[8:9, :]
        into[64:65, :] = after[8:9, :]
    first, last = ends

    @pl.when(first)
    def _():
        cv[BASE - 1 : BASE, :] = pltpu.roll(cv[BASE : BASE + 1, :], 127, 1)

    @pl.when(last)
    def _():
        cv[BASE + OWN : BASE + OWN + 1, :] = pltpu.roll(cv[BASE + OWN - 1 : BASE + OWN, :], 1, 1)

    cv[...] = GRAVITY * cv[...]


def mirror(src, pitch, at, mt, ends):
    lane = lanes_of((1, 128))

    def row(tile, v):
        return src[tile * pitch + v : tile * pitch + v + 1, :]

    def grads(tile):
        return [mt[tile * 8 + k : tile * 8 + k + 1, :] for k in range(4)]

    def write(tile, rim, nodes, meet, gx, gy, shift, target):
        length = jnp.sqrt(gx * gx + gy * gy)
        nx, ny = gx / length, gy / length
        for j in range(4):
            eta, mx, my = (row(tile, at(f, nodes[j])) for f in range(3))
            normal = mx * nx + my * ny
            for f, value in enumerate((eta, mx - 2.0 * normal * nx, my - 2.0 * normal * ny)):
                v = at(f, meet[j])
                old = row(rim, v)
                src[rim * pitch + v : rim * pitch + v + 1, :] = jnp.where(
                    lane == target, pltpu.roll(value, shift, 1), old)

    first, last = ends

    @pl.when(first)
    def _():
        _, _, sx, sy = grads(BASE)
        write(BASE, BASE - 1, FACES[0], MEET[0], -sx, -sy, 127, 127)

    @pl.when(last)
    def _():
        rx, ry, sx, sy = grads(BASE + OWN - 1)
        write(BASE + OWN - 1, BASE + OWN, FACES[1], MEET[1], rx + sx, ry + sy, 1, 0)


def shifts(partner):
    lane = lanes_of((8, 128))
    j = lane + partner
    idx, inside = j & 127, (j >= 0) & (j < 128)

    def before(own, prv, nxt):
        return pltpu.roll(jnp.where(lane == 127, prv, own), 1, 1)

    def after(own, prv, nxt):
        return pltpu.roll(jnp.where(lane == 0, nxt, own), 127, 1)

    def across(own, prv, nxt):
        return jnp.where(inside, pick(own, idx), pick(jnp.where(lane < 64, nxt, prv), idx))

    return before, after, across


def coefficients(m, mt, cv, pv, co):
    rx, ry, sx, sy = (spread(mt, k, m, 8) for k in range(4))
    partner = pv[m : m + 8, :]
    three = [cv[m + s : m + s + 8, :] for s in (0, -1, 1)]
    c = three[0]
    outer = [move(*three) for move in shifts(partner)]
    outer[2] = jnp.where(partner == 0, c, outer[2])
    for k, (gx, gy) in enumerate(((sx, sy), (rx + sx, ry + sy), (rx, ry))):
        length = jnp.sqrt(gx * gx + gy * gy)
        co[k, m : m + 8, :] = outer[k]
        co[3 + k, m : m + 8, :] = length * jnp.sqrt(jnp.maximum(c, outer[k]))
        if k == 2:
            co[6, m : m + 8, :] = gx / length
            co[7, m : m + 8, :] = gy / length


def flux(m, src, pitch, at, mt, cv, pv, co, xt, slot):
    rx, ry, sx, sy = (spread(mt, k, m, 8) for k in range(4))
    c = cv[m : m + 8, :]
    partner = pv[m : m + 8, :]
    wall = partner == 0
    moves = shifts(partner)

    def value(f, n, step=0):
        return spread(src, at(f, n), m + step, pitch)

    def store(f, k, x):
        put(xt, f * 32 + k, slot, XP, x)

    crx, cry, csx, csy = -c * rx, -c * ry, -c * sx, -c * sy
    for n in range(10):
        eta, mx, my = (value(f, n) for f in range(3))
        store(0, n, -(rx * mx + ry * my))
        store(0, 10 + n, -(sx * mx + sy * my))
        store(1, n, crx * eta)
        store(1, 10 + n, csx * eta)
        store(2, n, cry * eta)
        store(2, 10 + n, csy * eta)
    vectors = ((-sx, -sy), (rx + sx, ry + sy), (-rx, -ry))
    for k in range(3):
        gx, gy = vectors[k]
        ce = co[k, m : m + 8, :]
        scale = co[3 + k, m : m + 8, :]
        for j in range(4):
            inner = [value(f, FACES[k][j]) for f in range(3)]
            outer = []
            for f in range(3):
                node = MEET[k][j]
                own = value(f, node)
                prv = value(f, node, -1) if k != 1 else None
                nxt = value(f, node, 1) if k != 0 else None
                outer.append(moves[k](own, prv, nxt))
            if k == 2:
                outer[0] = jnp.where(wall, inner[0], outer[0])
            d_eta, d_mx, d_my = (b - a for a, b in zip(inner, outer))
            if k == 2:
                nx, ny = co[6, m : m + 8, :], co[7, m : m + 8, :]
                twice = -2.0 * (inner[1] * nx + inner[2] * ny)
                d_mx = jnp.where(wall, twice * nx, d_mx)
                d_my = jnp.where(wall, twice * ny, d_my)
            drop = c * inner[0] - ce * outer[0]
            row = 20 + 4 * k + j
            store(0, row, scale * d_eta - gx * d_mx - gy * d_my)
            store(1, row, gx * drop + scale * d_mx)
            store(2, row, gy * drop + scale * d_my)


def product(m, slot, xt, wl, out):
    for pair in range(4):
        parts = []
        for t in (2 * pair, 2 * pair + 1):
            hi, lo = split(xt[(slot + t) * XP : (slot + t + 1) * XP, :])
            parts.append(jnp.concatenate([hi, lo], axis=0))
        both = jnp.concatenate(parts, axis=1)
        res = jnp.dot(wl[:, 0 : 2 * XP], both, preferred_element_type=f32)
        res = res[0:32] + res[32:64]
        tile = m + 2 * pair
        out[tile * RP : (tile + 1) * RP, :] = res[:, 0:128]
        out[(tile + 1) * RP : (tile + 2) * RP, :] = res[:, 128:256]


def weights(diff_ops, lift, wl, tmp, wf):
    wf[...] = jnp.zeros_like(wf)
    base = jnp.zeros((16, 128), f32)
    for i, shift in ((0, 0), (1, 10), (2, 20)):
        tmp[...] = jnp.zeros_like(tmp)
        if i == 2:
            tmp[0:10, 0:12] = 0.5 * lift[...]
        else:
            for n in range(10):
                tmp[n : n + 1, 0:10] = diff_ops[n, i : i + 1, :]
        base = base + (tmp[...] if shift == 0 else pltpu.roll(tmp[...], shift, 1))
    for f in range(3):
        turned = base if f == 0 else pltpu.roll(base, 32 * f, 1)
        wf[f * 10 : f * 10 + 10, :] = turned[0:10]
    w = wf[0:32, :]
    hi = w.astype(bf16).astype(f32)
    low = w - hi
    turned = pltpu.roll(hi, XP, 1)
    lane = lanes_of((32, 128))
    wl[0:32, 0:128] = (hi + jnp.where(lane >= XP, turned, 0.0)).astype(bf16)
    wl[0:32, 128:256] = jnp.where(lane < 64, turned, 0.0).astype(bf16)
    wl[32:64, 0:128] = low.astype(bf16)
    wl[32:64, 128:256] = jnp.zeros((32, 128), bf16)


def child_weights(prolong, pw, tmp, wf):
    for i in range(3):
        wf[...] = jnp.zeros_like(wf)
        tmp[...] = jnp.zeros_like(tmp)
        if i == 0:
            eye = lax.broadcasted_iota(i32, (16, 128), 0) == lanes_of((16, 128))
            tmp[0:10, :] = jnp.where(eye, 1.0, 0.0)[0:10]
        else:
            for n in range(10):
                tmp[n : n + 1, 0:10] = prolong[n, i - 1 : i, :]
        for f in range(3):
            turned = tmp[...] if f == 0 else pltpu.roll(tmp[...], 10 * f, 1)
            wf[pl.ds(f, 10, stride=4), :] = turned[0:10]
        w = wf[...]
        hi = w.astype(bf16).astype(f32)
        low = w - hi
        pw[i * 48 : i * 48 + 48, :] = (hi + pltpu.roll(hi, 32, 1) + pltpu.roll(low, 64, 1)).astype(bf16)


def combine(m, step, qt, r1, r2, st):
    half = 0.5 * step * step
    for f in range(3):
        for n in range(10):
            v = f * 10 + n
            x = spread(qt, state_row(f, n), m, QP) + (step * spread(r1, v, m, RP) + half * spread(r2, v, m, RP))
            put(st, v, m - 16, RP, x)
    put(st, 30, m - 16, RP, jnp.zeros((8, 128), f32))
    put(st, 31, m - 16, RP, jnp.zeros((8, 128), f32))


def place_tables(offset, refine, lr, rr, rv, pk, near, code, lidx, pkw):
    rv[0:8, :] = lr[8:16, :]
    rv[8:40, :] = refine[...]
    rv[40:48, :] = rr[0:8, :]
    bits = rv[...]
    counts = (1 + bits).astype(f32)
    upper = lax.broadcasted_iota(i32, (128, 128), 0) <= lanes_of((128, 128))
    within = jnp.dot(counts.astype(bf16), upper.astype(f32).astype(bf16), preferred_element_type=f32)
    sums = jnp.broadcast_to(within[:, 127:128], (48, 128))
    lower = lanes_of((48, 48)) < lax.broadcasted_iota(i32, (48, 48), 0)
    before = jnp.dot(lower.astype(f32).astype(bf16), sums.astype(bf16), preferred_element_type=f32)
    ends = within + before - before[8:9, :] + offset
    ends = ends.astype(i32)
    pk[0:48, :] = 2 * (ends - 1 - bits) + bits
    pk[48:56, :] = jnp.full((8, 128), 2 * (1 << 20), i32)
    last = jnp.broadcast_to(ends[:, 127:128], (48, 128))
    reached = (last <= lanes_of((48, 128)) * 128).astype(f32)
    first = jnp.sum(reached, axis=0, keepdims=True).astype(i32)
    near[...] = jnp.broadcast_to(first, (8, 128))
    tiles = [near[0, r] for r in range(48)]
    for r in range(48):
        pkw[0, r : r + 1, :] = pk[pl.ds(tiles[r], 1), :]
        pkw[1, r : r + 1, :] = pk[pl.ds(tiles[r] + 1, 1), :]
    for g in range(6):
        rows = slice(8 * g, 8 * g + 8)
        p0, p1 = pkw[0, rows, :], pkw[1, rows, :]
        e0 = (p0 >> 1) + 1 + (p0 & 1)
        e1 = (p1 >> 1) + 1 + (p1 & 1)
        slot = (8 * g + lax.broadcasted_iota(i32, (8, 128), 0)) * 128 + lanes_of((8, 128))
        over = jnp.broadcast_to(e0[:, 127:128], (8, 128)) <= slot
        pos = jnp.zeros((8, 128), i32)
        for s in (64, 32, 16, 8, 4, 2, 1):
            probe = pos + (s - 1)
            e = jnp.where(over, pick(e1, probe), pick(e0, probe))
            pos = jnp.where(e <= slot, pos + s, pos)
        got = jnp.where(over, pick(p1, pos), pick(p0, pos))
        which = slot - (got >> 1)
        lidx[rows, :] = jnp.where(over, pos + 128, pos)
        code[rows, :] = jnp.where((got & 1) == 0, 0, 1 + which)
    return tiles


def place(tiles, st, pw, lidx, code, out):
    for pair in range(24):
        parts = []
        for r in (2 * pair, 2 * pair + 1):
            begin = pl.multiple_of(tiles[r] * RP, RP)
            near = st[pl.ds(begin, RP), :]
            far = st[pl.ds(pl.multiple_of(begin + RP, RP), RP), :]
            idx = jnp.broadcast_to(lidx[r : r + 1, :], (RP, 128))
            low = idx & 127
            s = jnp.where(idx < 128, pick(near, low), pick(far, low))
            hi, lo = split(s)
            parts.append(jnp.concatenate([hi, lo, hi], axis=0))
        res = jnp.dot(pw[:, 0:96], jnp.concatenate(parts, axis=1), preferred_element_type=f32)
        for i in range(2):
            r = 2 * pair + i
            one = res[:, 128 * i : 128 * i + 128]
            kind = jnp.broadcast_to(code[r : r + 1, :], (48, 128))
            new = jnp.where(kind == 0, one[0:48], jnp.where(kind == 1, one[48:96], one[96:144]))
            for n in range(10):
                out[n, :, r * 128 : (r + 1) * 128] = new[4 * n : 4 * n + 3]


def local(
    total, cols,
    state, metric, depth, partner, refine, diff_ops, lift, prolong,
    ls, lm, ld, lp, lr, rs, rm, rd, rp, rr, stat,
    out,
    qt, mt, cv, pv, co, xt, r1, r2, st, wl, pw, tmp, wf, rv, pk, near, code, lidx, pkw,
):
    me = lax.axis_index("row") * cols + lax.axis_index("col")
    ends = (me == 0, me == total - 1)
    weights(diff_ops, lift, wl, tmp, wf)
    child_weights(prolong, pw, tmp, wf)
    load_tiles((state, metric, depth, partner), (ls, lm, ld, lp), (rs, rm, rd, rp), qt, mt, cv, pv, ends)
    mirror(qt, QP, state_row, mt, ends)
    for g in range(7):
        m = 8 + 8 * g
        coefficients(m, mt, cv, pv, co)
        flux(m, qt, QP, state_row, mt, cv, pv, co, xt, 8 * (g % 2))
        product(m, 8 * (g % 2), xt, wl, r1)
    r1[64 * RP : 65 * RP, :] = r1[8 * RP : 9 * RP, :]
    mirror(r1, RP, result_row, mt, ends)
    step = COURANT / stat[0:1, :]
    for g in range(1, 7):
        m = 8 + 8 * g
        flux(m, r1, RP, result_row, mt, cv, pv, co, xt, 8 * (g % 2))
        product(m, 8 * (g % 2), xt, wl, r2)
        combine(m, step, qt, r1, r2, st)
    tiles = place_tables(stat[1:2, :], refine, lr, rr, rv, pk, near, code, lidx, pkw)
    place(tiles, st, pw, lidx, code, out)


def solution(mesh):
    rows, cols = mesh.shape["row"], mesh.shape["col"]
    total = rows * cols
    low = 16 if total % 256 == 0 else max(total // 2, 1)
    high = total // low

    def shards(state, depth, metric, partner, refine, diff_ops, lift, prolong):
        depth, partner, refine = (a.reshape(OWN, 128) for a in (depth, partner, refine))
        state, diff_ops, prolong = (a.transpose(1, 0, 2) for a in (state, diff_ops, prolong))
        vm = pl.BlockSpec(memory_space=pltpu.VMEM)
        side = [
            jax.ShapeDtypeStruct((10, 3, WIDE), f32),
            jax.ShapeDtypeStruct((4, WIDE), f32),
            jax.ShapeDtypeStruct((16, 128), f32),
            jax.ShapeDtypeStruct((16, 128), i32),
            jax.ShapeDtypeStruct((16, 128), i32),
        ]
        got = pl.pallas_call(
            functools.partial(exchange, rows, cols, low),
            out_shape=side + side + [jax.ShapeDtypeStruct((8, 128), f32)],
            in_specs=[vm] * 5,
            out_specs=[vm] * 11,
            scratch_shapes=[
                pltpu.VMEM((OWN * 8, 128), f32),
                pltpu.VMEM((8, 128), f32),
                pltpu.VMEM((low - 1, 8, 128), f32),
                pltpu.VMEM((8, 128), f32),
                pltpu.VMEM((high - 1, 8, 128), f32),
                pltpu.SemaphoreType.DMA((10,)),
                pltpu.SemaphoreType.DMA((10,)),
                pltpu.SemaphoreType.DMA((low - 1,)),
                pltpu.SemaphoreType.DMA((low - 1,)),
                pltpu.SemaphoreType.DMA((high - 1,)),
                pltpu.SemaphoreType.DMA((high - 1,)),
            ],
            compiler_params=pltpu.CompilerParams(collective_id=0, has_side_effects=True),
            name="exchange",
        )(state, metric, depth, partner, refine)
        new = pl.pallas_call(
            functools.partial(local, total, cols),
            out_shape=jax.ShapeDtypeStruct((10, 3, OWN * 192), f32),
            in_specs=[vm] * 19,
            out_specs=vm,
            scratch_shapes=[
                pltpu.VMEM((MEM * QP, 128), f32),
                pltpu.VMEM((MEM * 8, 128), f32),
                pltpu.VMEM((MEM, 128), f32),
                pltpu.VMEM((MEM, 128), i32),
                pltpu.VMEM((8, MEM, 128), f32),
                pltpu.VMEM((16 * XP, 128), f32),
                pltpu.VMEM((MEM * RP, 128), f32),
                pltpu.VMEM((MEM * RP, 128), f32),
                pltpu.VMEM((49 * RP, 128), f32),
                pltpu.VMEM((64, 256), bf16),
                pltpu.VMEM((144, 128), bf16),
                pltpu.VMEM((16, 128), f32),
                pltpu.VMEM((48, 128), f32),
                pltpu.VMEM((48, 128), i32),
                pltpu.VMEM((56, 128), i32),
                pltpu.VMEM((8, 128), i32),
                pltpu.VMEM((48, 128), i32),
                pltpu.VMEM((48, 128), i32),
                pltpu.VMEM((2, 48, 128), i32),
            ],
            name="local",
        )(state, metric, depth, partner, refine, diff_ops, lift, prolong, *got)
        return new.transpose(1, 0, 2)

    halves = ("row", "col")
    return jax.shard_map(
        shards,
        mesh=mesh,
        in_specs=(P(None, None, halves), P(halves), P(None, halves), P(halves), P(halves), P(), P(), P()),
        out_specs=P(None, None, halves),
        check_vma=False,
    )
```

```python
import functools

import jax
import jax.numpy as jnp
from jax import lax
from jax.experimental import pallas as pl
from jax.experimental.pallas import tpu as pltpu
from jax.sharding import PartitionSpec as P

GRAVITY = 9.81
COURANT = 0.5
MESH = pl.DeviceIdType.MESH

OWN = 32
HALO = 9
WIDE = HALO * 128
BASE = 24
MEM = 72
QP = 41
RR = 32
RP = 33
MP = 9
XP = 96
XS = 97

FACES = ((0, 1, 2, 3), (3, 6, 8, 9), (9, 7, 4, 0))
MEET = ((9, 8, 6, 3), (3, 2, 1, 0), (0, 4, 7, 9))

f32 = jnp.float32
bf16 = jnp.bfloat16
i32 = jnp.int32


def lanes_of(shape):
    return lax.broadcasted_iota(i32, shape, len(shape) - 1)


def state_row(f, n):
    return 4 * n + f


def result_row(f, n):
    return 10 * f + n


def spread(ref, v, tile, pitch):
    return ref[pl.ds(tile * pitch + v, 8, stride=pitch), :]


def put(ref, v, tile, pitch, value):
    ref[pl.ds(tile * pitch + v, 8, stride=pitch), :] = value


def pick(x, idx):
    return jnp.take_along_axis(x, idx, axis=1, mode="promise_in_bounds")


def split(x):
    hi = x.astype(bf16)
    return hi, (x - hi.astype(f32)).astype(bf16)


def joined(own, box, size, position):
    part = box[0 : size - 1, :]
    member = lax.broadcasted_iota(i32, part.shape, 0) + 1
    best = jnp.maximum(own, jnp.max(part, axis=0, keepdims=True))
    both = own + jnp.sum(part, axis=0, keepdims=True)
    before = jnp.sum(jnp.where(member <= position, part, 0.0), axis=0, keepdims=True)
    return jnp.where(lanes_of((1, 128)) < 64, best, both), before


def advance(
    rows, cols, low,
    state, metric, depth, partner, refine, diff_ops, lift, prolong,
    st, pk, pw, stat,
    sv, gv, dv, av, bv, wd, wt, wc,
    ls, lm, ld, lp, lr, rs, rm, rd, rp, rr,
    qt, mt, cv, pv, co, xt, r1, r2, wl, tmp, wf, rv,
    mine, box1, mine2, box2,
    here, send, recv, send1, recv1, send2, recv2,
):
    total = rows * cols
    high = total // low
    me = lax.axis_index("row") * cols + lax.axis_index("col")
    lo, hi = lax.rem(me, low), me // low

    def at(flat):
        return (flat // cols, lax.rem(flat, cols))

    right = at(lax.rem(me + 1, total))
    left = at(lax.rem(me + total - 1, total))
    peers1 = [at(hi * low + lax.rem(lo + d, low)) for d in range(1, low)]
    peers2 = [at(lax.rem(hi + d, high) * low + lo) for d in range(1, high)]

    barrier = pltpu.get_barrier_semaphore()
    everyone = [left, right] + peers1 + peers2
    for peer in everyone:
        pl.semaphore_signal(barrier, inc=1, device_id=peer, device_id_type=MESH)

    pairs = (
        (metric, gv), (depth, dv), (refine, bv), (state, sv), (partner, av), (diff_ops, wd), (lift, wt), (prolong, wc))
    loads = [pltpu.make_async_copy(a, b, here.at[k]) for k, (a, b) in enumerate(pairs)]
    for load in loads:
        load.start()
    for load in loads[:3]:
        load.wait()
    for t in range(OWN):
        lay_metric(mt, BASE + t, gv, t)
    grads = [mt[pl.ds(BASE * MP + k, OWN, stride=MP), :] for k in range(4)]
    rate = wave_rate(dv[...], grads)
    top = jnp.max(jnp.max(rate, axis=0, keepdims=True), axis=1, keepdims=True)
    count = jnp.sum(bv[...].astype(f32), axis=0, keepdims=True)
    count = jnp.sum(count, axis=1, keepdims=True)
    half = lanes_of((1, 128)) < 64
    own = jnp.where(half, top, count)
    mine[0:1, :] = own

    def round_of(source, box, peers, sems, rems):
        return [
            pltpu.make_async_remote_copy(
                src_ref=source.at[pl.ds(0, 1)], dst_ref=box.at[pl.ds(d, 1)], send_sem=sems.at[d], recv_sem=rems.at[d],
                device_id=peer, device_id_type=MESH)
            for d, peer in enumerate(peers)
        ]

    round1 = round_of(mine, box1, peers1, send1, recv1)
    round2 = round_of(mine2, box2, peers2, send2, recv2)
    tail, head = pl.ds((OWN - HALO) * 128, WIDE), pl.ds(0, WIDE)
    copies = []
    for peer, wide, short, targets in (
        (right, tail, pl.ds(16, 16), (ls, lm, ld, lp, lr)),
        (left, head, pl.ds(0, 16), (rs, rm, rd, rp, rr)),
    ):
        sources = (state.at[:, :, wide], metric.at[:, wide], depth.at[short], partner.at[short], refine.at[short])
        for source, target in zip(sources, targets):
            k = len(copies)
            copies.append(pltpu.make_async_remote_copy(
                src_ref=source, dst_ref=target, send_sem=send.at[k], recv_sem=recv.at[k],
                device_id=peer, device_id_type=MESH))

    pl.semaphore_wait(barrier, len(everyone))
    for copy in round1 + copies:
        copy.start()

    for load in loads[3:]:
        load.wait()
    ends = (me == 0, me == total - 1)
    weights(wd, wt, wl, tmp, wf)
    for t in range(OWN):
        lay_state(qt, BASE + t, sv, t)
    cv[BASE : BASE + OWN, :] = GRAVITY * dv[...]
    pv[BASE : BASE + OWN, :] = av[...]

    def first_rate(g):
        m = 8 + 8 * g
        coefficients(m, mt, cv, pv, co)
        flux(m, qt, QP, state_row, mt, cv, pv, co, xt, 8 * (g % 2))
        product(m, 8 * (g % 2), xt, wl, r1)

    for g in (3, 4):
        first_rate(g)
    child_weights(wc, pw, tmp, wf)
    for copy in copies:
        copy.wait_recv()
    load_rims((ls, lm, ld, lp), (rs, rm, rd, rp), qt, mt, cv, pv, ends)
    mirror(qt, QP, state_row, mt, ends)
    for g in (2, 5, 6, 1, 0):
        first_rate(g)
    for copy in round1:
        copy.wait_recv()
    own, before1 = joined(own, box1, low, lo)
    mine2[0:1, :] = own
    for copy in round2:
        copy.start()
    r1[64 * RP : 65 * RP, :] = r1[8 * RP : 9 * RP, :]
    mirror(r1, RP, result_row, mt, ends)
    for g in range(1, 7):
        m = 8 + 8 * g
        flux(m, r1, RP, result_row, mt, cv, pv, co, xt, 8 * (g % 2))
        product(m, 8 * (g % 2), xt, wl, r2)
    prefix(lr, bv, rr, rv, pk)
    for copy in round2:
        copy.wait_recv()
    own, before2 = joined(own, box2, high, hi)
    best = jnp.where(half, own, pltpu.roll(own, 64, 1))
    before = before1 + before2
    before = jnp.where(half, pltpu.roll(before, 64, 1), before)
    stat[0:1, :] = before - (me * (OWN * 64)).astype(f32)
    step = COURANT / best
    for g in range(1, 7):
        combine(8 + 8 * g, step, qt, r1, r2, st)
    for copy in round1 + round2 + copies:
        copy.wait_send()


def wave_rate(depth, grads):
    gx, gy, hx, hy = grads
    lengths = [jnp.sqrt(vx * vx + vy * vy) for vx, vy in ((hx, hy), (gx + hx, gy + hy), (gx, gy))]
    return jnp.sqrt(GRAVITY * depth) * jnp.maximum(jnp.maximum(lengths[0], lengths[1]), lengths[2])


def lay_state(qt, m, s, t):
    for n in range(10):
        qt[m * QP + 4 * n : m * QP + 4 * n + 3, :] = s[n, :, t * 128 : (t + 1) * 128]


def lay_metric(mt, m, g, t):
    mt[m * MP : m * MP + 4, :] = g[:, t * 128 : (t + 1) * 128]


def load_rims(left, right, qt, mt, cv, pv, ends):
    ls, lm, ld, lp = left
    rs, rm, rd, rp = right

    def lay(m, s, g, t):
        lay_state(qt, m, s, t)
        lay_metric(mt, m, g, t)

    for t in range(HALO):
        lay(BASE - HALO + t, ls, lm, t)
        if t < HALO - 1:
            lay(BASE + OWN + t, rs, rm, t)
    lay(8, rs, rm, HALO - 1)
    lay(64, rs, rm, HALO - 1)
    lay(7, rs, rm, HALO - 2)
    for into, before, after, scale in ((cv, ld, rd, GRAVITY), (pv, lp, rp, 1)):
        into[BASE - HALO : BASE, :] = scale * before[16 - HALO : 16, :]
        into[BASE + OWN : BASE + OWN + 8, :] = scale * after[0:8, :]
        into[7:8, :] = scale * after[7:8, :]
        into[8:9, :] = scale * after[8:9, :]
        into[64:65, :] = scale * after[8:9, :]
    first, last = ends

    @pl.when(first)
    def _():
        cv[BASE - 1 : BASE, :] = pltpu.roll(cv[BASE : BASE + 1, :], 127, 1)

    @pl.when(last)
    def _():
        cv[BASE + OWN : BASE + OWN + 1, :] = pltpu.roll(cv[BASE + OWN - 1 : BASE + OWN, :], 1, 1)


def mirror(src, pitch, at, mt, ends):
    lane = lanes_of((1, 128))

    def row(tile, v):
        return src[tile * pitch + v : tile * pitch + v + 1, :]

    def grads(tile):
        return [mt[tile * MP + k : tile * MP + k + 1, :] for k in range(4)]

    def write(tile, rim, nodes, meet, gx, gy, shift, target):
        length = jnp.sqrt(gx * gx + gy * gy)
        nx, ny = gx / length, gy / length
        for j in range(4):
            eta, mx, my = (row(tile, at(f, nodes[j])) for f in range(3))
            normal = mx * nx + my * ny
            for f, value in enumerate((eta, mx - 2.0 * normal * nx, my - 2.0 * normal * ny)):
                v = at(f, meet[j])
                old = row(rim, v)
                src[rim * pitch + v : rim * pitch + v + 1, :] = jnp.where(
                    lane == target, pltpu.roll(value, shift, 1), old)

    first, last = ends

    @pl.when(first)
    def _():
        _, _, sx, sy = grads(BASE)
        write(BASE, BASE - 1, FACES[0], MEET[0], -sx, -sy, 127, 127)

    @pl.when(last)
    def _():
        rx, ry, sx, sy = grads(BASE + OWN - 1)
        write(BASE + OWN - 1, BASE + OWN, FACES[1], MEET[1], rx + sx, ry + sy, 1, 0)


def shifts(partner):
    lane = lanes_of((8, 128))
    j = lane + partner
    idx, inside = j & 127, (j >= 0) & (j < 128)

    def before(own, prv, nxt):
        return pltpu.roll(jnp.where(lane == 127, prv, own), 1, 1)

    def after(own, prv, nxt):
        return pltpu.roll(jnp.where(lane == 0, nxt, own), 127, 1)

    def across(own, prv, nxt):
        return jnp.where(inside, pick(own, idx), pick(jnp.where(lane < 64, nxt, prv), idx))

    return before, after, across


def coefficients(m, mt, cv, pv, co):
    rx, ry, sx, sy = (spread(mt, k, m, MP) for k in range(4))
    partner = pv[m : m + 8, :]
    three = [cv[m + s : m + s + 8, :] for s in (0, -1, 1)]
    c = three[0]
    outer = [move(*three) for move in shifts(partner)]
    outer[2] = jnp.where(partner == 0, c, outer[2])
    for k, (gx, gy) in enumerate(((sx, sy), (rx + sx, ry + sy), (rx, ry))):
        length = jnp.sqrt(gx * gx + gy * gy)
        co[k, m : m + 8, :] = outer[k]
        co[3 + k, m : m + 8, :] = length * jnp.sqrt(jnp.maximum(c, outer[k]))
        if k == 2:
            co[6, m : m + 8, :] = gx / length
            co[7, m : m + 8, :] = gy / length


def flux(m, src, pitch, at, mt, cv, pv, co, xt, slot):
    rx, ry, sx, sy = (spread(mt, k, m, MP) for k in range(4))
    c = cv[m : m + 8, :]
    partner = pv[m : m + 8, :]
    wall = partner == 0
    moves = shifts(partner)

    def value(f, n, step=0):
        return spread(src, at(f, n), m + step, pitch)

    def store(f, k, x):
        put(xt, f * 32 + k, slot, XS, x)

    crx, cry, csx, csy = -c * rx, -c * ry, -c * sx, -c * sy
    for n in range(10):
        eta, mx, my = (value(f, n) for f in range(3))
        store(0, n, -(rx * mx + ry * my))
        store(0, 10 + n, -(sx * mx + sy * my))
        store(1, n, crx * eta)
        store(1, 10 + n, csx * eta)
        store(2, n, cry * eta)
        store(2, 10 + n, csy * eta)
    vectors = ((-sx, -sy), (rx + sx, ry + sy), (-rx, -ry))
    for k in range(3):
        gx, gy = vectors[k]
        ce = co[k, m : m + 8, :]
        scale = co[3 + k, m : m + 8, :]
        for j in range(4):
            inner = [value(f, FACES[k][j]) for f in range(3)]
            outer = []
            for f in range(3):
                node = MEET[k][j]
                own = value(f, node)
                prv = value(f, node, -1) if k != 1 else None
                nxt = value(f, node, 1) if k != 0 else None
                outer.append(moves[k](own, prv, nxt))
            if k == 2:
                outer[0] = jnp.where(wall, inner[0], outer[0])
            d_eta, d_mx, d_my = (b - a for a, b in zip(inner, outer))
            if k == 2:
                nx, ny = co[6, m : m + 8, :], co[7, m : m + 8, :]
                twice = -2.0 * (inner[1] * nx + inner[2] * ny)
                d_mx = jnp.where(wall, twice * nx, d_mx)
                d_my = jnp.where(wall, twice * ny, d_my)
            drop = c * inner[0] - ce * outer[0]
            row = 20 + 4 * k + j
            store(0, row, scale * d_eta - gx * d_mx - gy * d_my)
            store(1, row, gx * drop + scale * d_mx)
            store(2, row, gy * drop + scale * d_my)


def product(m, slot, xt, wl, out):
    for pair in range(4):
        parts = []
        for t in (2 * pair, 2 * pair + 1):
            hi, lo = split(xt[(slot + t) * XS : (slot + t) * XS + XP, :])
            parts.append(jnp.concatenate([hi, lo], axis=0))
        both = jnp.concatenate(parts, axis=1)
        res = jnp.dot(wl[:, 0 : 2 * XP], both, preferred_element_type=f32)
        res = res[0:32] + res[32:64]
        tile = m + 2 * pair
        out[tile * RP : tile * RP + RR, :] = res[:, 0:128]
        out[(tile + 1) * RP : (tile + 1) * RP + RR, :] = res[:, 128:256]


def weights(diff_ops, lift, wl, tmp, wf):
    wf[...] = jnp.zeros_like(wf)
    base = jnp.zeros((16, 128), f32)
    for i, shift in ((0, 0), (1, 10), (2, 20)):
        tmp[...] = jnp.zeros_like(tmp)
        if i == 2:
            tmp[0:10, 0:12] = 0.5 * lift[...]
        else:
            for n in range(10):
                tmp[n : n + 1, 0:10] = diff_ops[n, i : i + 1, :]
        base = base + (tmp[...] if shift == 0 else pltpu.roll(tmp[...], shift, 1))
    for f in range(3):
        turned = base if f == 0 else pltpu.roll(base, 32 * f, 1)
        wf[f * 10 : f * 10 + 10, :] = turned[0:10]
    w = wf[0:32, :]
    hi = w.astype(bf16).astype(f32)
    low = w - hi
    turned = pltpu.roll(hi, XP, 1)
    lane = lanes_of((32, 128))
    wl[0:32, 0:128] = (hi + jnp.where(lane >= XP, turned, 0.0)).astype(bf16)
    wl[0:32, 128:256] = jnp.where(lane < 64, turned, 0.0).astype(bf16)
    wl[32:64, 0:128] = low.astype(bf16)
    wl[32:64, 128:256] = jnp.zeros((32, 128), bf16)


def child_weights(prolong, pw, tmp, wf):
    for i in range(3):
        wf[...] = jnp.zeros_like(wf)
        tmp[...] = jnp.zeros_like(tmp)
        if i == 0:
            eye = lax.broadcasted_iota(i32, (16, 128), 0) == lanes_of((16, 128))
            tmp[0:10, :] = jnp.where(eye, 1.0, 0.0)[0:10]
        else:
            for n in range(10):
                tmp[n : n + 1, 0:10] = prolong[n, i - 1 : i, :]
        for f in range(3):
            turned = tmp[...] if f == 0 else pltpu.roll(tmp[...], 10 * f, 1)
            wf[pl.ds(f, 10, stride=4), :] = turned[0:10]
        w = wf[...]
        hi = w.astype(bf16).astype(f32)
        low = w - hi
        pw[i * 48 : i * 48 + 48, :] = (hi + pltpu.roll(hi, 32, 1) + pltpu.roll(low, 64, 1)).astype(bf16)


def combine(m, step, qt, r1, r2, st):
    half = 0.5 * step * step
    for f in range(3):
        for n in range(10):
            v = f * 10 + n
            x = spread(qt, state_row(f, n), m, QP) + (step * spread(r1, v, m, RP) + half * spread(r2, v, m, RP))
            put(st, v, m - 16, RP, x)
    put(st, 30, m - 16, RP, jnp.zeros((8, 128), f32))
    put(st, 31, m - 16, RP, jnp.zeros((8, 128), f32))


def prefix(lr, refine, rr, rv, pk):
    rv[0:8, :] = lr[8:16, :]
    rv[8:40, :] = refine[...]
    rv[40:48, :] = rr[0:8, :]
    bits = rv[...]
    counts = (1 + bits).astype(f32)
    upper = lax.broadcasted_iota(i32, (128, 128), 0) <= lanes_of((128, 128))
    within = jnp.dot(counts.astype(bf16), upper.astype(f32).astype(bf16), preferred_element_type=f32)
    sums = jnp.broadcast_to(within[:, 127:128], (48, 128))
    lower = lanes_of((48, 48)) < lax.broadcasted_iota(i32, (48, 48), 0)
    before = jnp.dot(lower.astype(f32).astype(bf16), sums.astype(bf16), preferred_element_type=f32)
    ends = (within + before - before[8:9, :]).astype(i32)
    pk[0:48, :] = 2 * (ends - 1 - bits) + bits
    pk[48:56, :] = jnp.full((8, 128), 1 << 21, i32)


def tables(offset, rel, pk, near, code, lidx, pkw):
    pk[...] = rel[...] + 2 * offset.astype(i32)
    ends = (pk[0:48, :] >> 1) + 1 + (pk[0:48, :] & 1)
    last = jnp.broadcast_to(ends[:, 127:128], (48, 128))
    reached = (last <= lanes_of((48, 128)) * 128).astype(f32)
    first = jnp.sum(reached, axis=0, keepdims=True).astype(i32)
    near[...] = jnp.broadcast_to(first, (8, 128))
    tiles = [near[0, r] for r in range(48)]
    for r in range(48):
        pkw[0, r : r + 1, :] = pk[pl.ds(tiles[r], 1), :]
        pkw[1, r : r + 1, :] = pk[pl.ds(tiles[r] + 1, 1), :]
    for g in range(6):
        rows = slice(8 * g, 8 * g + 8)
        p0, p1 = pkw[0, rows, :], pkw[1, rows, :]
        e0 = (p0 >> 1) + 1 + (p0 & 1)
        e1 = (p1 >> 1) + 1 + (p1 & 1)
        slot = (8 * g + lax.broadcasted_iota(i32, (8, 128), 0)) * 128 + lanes_of((8, 128))
        over = jnp.broadcast_to(e0[:, 127:128], (8, 128)) <= slot
        pos = jnp.zeros((8, 128), i32)
        for s in (64, 32, 16, 8, 4, 2, 1):
            probe = pos + (s - 1)
            e = jnp.where(over, pick(e1, probe), pick(e0, probe))
            pos = jnp.where(e <= slot, pos + s, pos)
        got = jnp.where(over, pick(p1, pos), pick(p0, pos))
        which = slot - (got >> 1)
        lidx[rows, :] = jnp.where(over, pos + 128, pos)
        code[rows, :] = jnp.where((got & 1) == 0, 0, 1 + which)
    return tiles


def place(rel, pw, stat, st_in, out, st, new_tiles, pk, near, code, lidx, pkw, sems):
    load = pltpu.make_async_copy(st_in, st, sems.at[0])
    load.start()
    tiles = tables(stat[0:1, :], rel, pk, near, code, lidx, pkw)
    load.wait()
    weight = pw[:, 0:96]
    stores = []
    for pair in range(24):
        parts = []
        for r in (2 * pair, 2 * pair + 1):
            begin = tiles[r] * RP
            near_tile = st[pl.ds(begin, RR), :]
            far_tile = st[pl.ds(begin + RP, RR), :]
            idx = jnp.broadcast_to(lidx[r : r + 1, :], (RR, 128))
            low = idx & 127
            s = jnp.where(idx < 128, pick(near_tile, low), pick(far_tile, low))
            hi, lo = split(s)
            parts.append(jnp.concatenate([hi, lo, hi], axis=0))
        res = jnp.dot(weight, jnp.concatenate(parts, axis=1), preferred_element_type=f32)
        for i in range(2):
            r = 2 * pair + i
            one = res[:, 128 * i : 128 * i + 128]
            kind = jnp.broadcast_to(code[r : r + 1, :], (48, 128))
            new = jnp.where(kind == 0, one[0:48], jnp.where(kind == 1, one[48:96], one[96:144]))
            for n in range(10):
                new_tiles[n, :, r * 128 : (r + 1) * 128] = new[4 * n : 4 * n + 3]
        if pair % 6 == 5:
            part = pl.ds((pair // 6) * 1536, 1536)
            store = pltpu.make_async_copy(new_tiles.at[:, :, part], out.at[:, :, part], sems.at[1 + pair // 6])
            store.start()
            stores.append(store)
    for store in stores:
        store.wait()


def solution(mesh):
    rows, cols = mesh.shape["row"], mesh.shape["col"]
    total = rows * cols
    low = 16 if total % 256 == 0 else max(total // 2, 1)
    high = total // low
    placed = OWN + OWN // 2

    def shards(state, depth, metric, partner, refine, diff_ops, lift, prolong):
        depth, partner, refine = (a.reshape(OWN, 128) for a in (depth, partner, refine))
        state, diff_ops, prolong = (a.transpose(1, 0, 2) for a in (state, diff_ops, prolong))
        args = (state, metric, depth, partner, refine, diff_ops, lift, prolong)
        vm, hbm = pl.BlockSpec(memory_space=pltpu.VMEM), pl.BlockSpec(memory_space=pl.ANY)
        side = [
            pltpu.VMEM((10, 3, WIDE), f32),
            pltpu.VMEM((4, WIDE), f32),
            pltpu.VMEM((16, 128), f32),
            pltpu.VMEM((16, 128), i32),
            pltpu.VMEM((16, 128), i32),
        ]
        st, pk, pw, stat = pl.pallas_call(
            functools.partial(advance, rows, cols, low),
            out_shape=[
                jax.ShapeDtypeStruct((((placed + 1) * RP + 7) // 8 * 8, 128), f32),
                jax.ShapeDtypeStruct((56, 128), i32),
                jax.ShapeDtypeStruct((144, 128), bf16),
                jax.ShapeDtypeStruct((8, 128), f32),
            ],
            in_specs=[hbm] * 8,
            out_specs=[vm] * 4,
            scratch_shapes=[pltpu.VMEM(a.shape, a.dtype) for a in args]
            + side
            + side
            + [
                pltpu.VMEM((MEM * QP, 128), f32),
                pltpu.VMEM((MEM * MP, 128), f32),
                pltpu.VMEM((MEM, 128), f32),
                pltpu.VMEM((MEM, 128), i32),
                pltpu.VMEM((8, MEM, 128), f32),
                pltpu.VMEM((16 * XS, 128), f32),
                pltpu.VMEM((MEM * RP, 128), f32),
                pltpu.VMEM((MEM * RP, 128), f32),
                pltpu.VMEM((64, 256), bf16),
                pltpu.VMEM((16, 128), f32),
                pltpu.VMEM((48, 128), f32),
                pltpu.VMEM((48, 128), i32),
                pltpu.VMEM((8, 128), f32),
                pltpu.VMEM((low, 128), f32),
                pltpu.VMEM((8, 128), f32),
                pltpu.VMEM((high, 128), f32),
                pltpu.SemaphoreType.DMA((8,)),
                pltpu.SemaphoreType.DMA((10,)),
                pltpu.SemaphoreType.DMA((10,)),
                pltpu.SemaphoreType.DMA((low - 1,)),
                pltpu.SemaphoreType.DMA((low - 1,)),
                pltpu.SemaphoreType.DMA((high - 1,)),
                pltpu.SemaphoreType.DMA((high - 1,)),
            ],
            compiler_params=pltpu.CompilerParams(collective_id=0, has_side_effects=True),
            name="advance",
        )(*args)
        new = pl.pallas_call(
            place,
            out_shape=jax.ShapeDtypeStruct((10, 3, placed * 128), f32),
            in_specs=[vm] * 3 + [hbm],
            out_specs=hbm,
            scratch_shapes=[
                pltpu.VMEM(st.shape, f32),
                pltpu.VMEM((10, 3, placed * 128), f32),
                pltpu.VMEM((56, 128), i32),
                pltpu.VMEM((8, 128), i32),
                pltpu.VMEM((48, 128), i32),
                pltpu.VMEM((48, 128), i32),
                pltpu.VMEM((2, 48, 128), i32),
                pltpu.SemaphoreType.DMA((5,)),
            ],
            name="place",
        )(pk, pw, stat, st)
        return new.transpose(1, 0, 2)

    halves = ("row", "col")
    return jax.shard_map(
        shards,
        mesh=mesh,
        in_specs=(P(None, None, halves), P(halves), P(None, halves), P(halves), P(halves), P(), P(), P()),
        out_specs=P(None, None, halves),
        check_vma=False,
    )
```

```python
import functools

import jax
import jax.numpy as jnp
from jax import lax
from jax.experimental import pallas as pl
from jax.experimental.pallas import tpu as pltpu
from jax.sharding import PartitionSpec as P

GRAVITY = 9.81
COURANT = 0.5
MESH = pl.DeviceIdType.MESH

OWN = 32
HALO = 9
WIDE = HALO * 128
BASE = 24
MEM = 72
QP = 41
RR = 32
RP = 33
MP = 9
XP = 96
XS = 97

FACES = ((0, 1, 2, 3), (3, 6, 8, 9), (9, 7, 4, 0))
MEET = ((9, 8, 6, 3), (3, 2, 1, 0), (0, 4, 7, 9))

f32 = jnp.float32
bf16 = jnp.bfloat16
i32 = jnp.int32


def lanes_of(shape):
    return lax.broadcasted_iota(i32, shape, len(shape) - 1)


def state_row(f, n):
    return 4 * n + f


def result_row(f, n):
    return 10 * f + n


def spread(ref, v, tile, pitch):
    return ref[pl.ds(tile * pitch + v, 8, stride=pitch), :]


def put(ref, v, tile, pitch, value):
    ref[pl.ds(tile * pitch + v, 8, stride=pitch), :] = value


def pick(x, idx):
    return jnp.take_along_axis(x, idx, axis=1, mode="promise_in_bounds")


def split(x):
    hi = x.astype(bf16)
    return hi, (x - hi.astype(f32)).astype(bf16)


def joined(own, box, size, position):
    part = box[0 : size - 1, :]
    member = lax.broadcasted_iota(i32, part.shape, 0) + 1
    best = jnp.maximum(own, jnp.max(part, axis=0, keepdims=True))
    both = own + jnp.sum(part, axis=0, keepdims=True)
    before = jnp.sum(jnp.where(member <= position, part, 0.0), axis=0, keepdims=True)
    return jnp.where(lanes_of((1, 128)) < 64, best, both), before


def advance(
    rows, cols, low,
    state, metric, depth, partner, refine, diff_ops, lift, prolong,
    st, pk, pw, stat,
    sv, gv, dv, av, bv, wd, wt, wc,
    ls, lm, ld, lp, lr, rs, rm, rd, rp, rr,
    qt, mt, cv, pv, co, xt, r1, r2, wl, tmp, wf, rv,
    mine, box1, mine2, box2,
    here, send, recv, send1, recv1, send2, recv2,
):
    total = rows * cols
    high = total // low
    me = lax.axis_index("row") * cols + lax.axis_index("col")
    lo, hi = lax.rem(me, low), me // low

    def at(flat):
        return (flat // cols, lax.rem(flat, cols))

    right = at(lax.rem(me + 1, total))
    left = at(lax.rem(me + total - 1, total))
    peers1 = [at(hi * low + lax.rem(lo + d, low)) for d in range(1, low)]
    peers2 = [at(lax.rem(hi + d, high) * low + lo) for d in range(1, high)]

    barrier = pltpu.get_barrier_semaphore()
    everyone = [left, right] + peers1 + peers2
    for peer in everyone:
        pl.semaphore_signal(barrier, inc=1, device_id=peer, device_id_type=MESH)

    pairs = (
        (metric, gv), (depth, dv), (refine, bv), (state, sv), (partner, av), (diff_ops, wd), (lift, wt), (prolong, wc))
    loads = [pltpu.make_async_copy(a, b, here.at[k]) for k, (a, b) in enumerate(pairs)]
    for load in loads:
        load.start()
    for load in loads[:3]:
        load.wait()
    for t in range(OWN):
        lay_metric(mt, BASE + t, gv, t)
    grads = [mt[pl.ds(BASE * MP + k, OWN, stride=MP), :] for k in range(4)]
    rate = wave_rate(dv[...], grads)
    top = jnp.max(jnp.max(rate, axis=0, keepdims=True), axis=1, keepdims=True)
    count = jnp.sum(bv[...].astype(f32), axis=0, keepdims=True)
    count = jnp.sum(count, axis=1, keepdims=True)
    half = lanes_of((1, 128)) < 64
    own = jnp.where(half, top, count)
    mine[0:1, :] = own

    def round_of(source, box, peers, sems, rems):
        return [
            pltpu.make_async_remote_copy(
                src_ref=source.at[pl.ds(0, 1)], dst_ref=box.at[pl.ds(d, 1)], send_sem=sems.at[d], recv_sem=rems.at[d],
                device_id=peer, device_id_type=MESH)
            for d, peer in enumerate(peers)
        ]

    round1 = round_of(mine, box1, peers1, send1, recv1)
    round2 = round_of(mine2, box2, peers2, send2, recv2)
    tail, head = pl.ds((OWN - HALO) * 128, WIDE), pl.ds(0, WIDE)
    copies = []
    for peer, wide, short, targets in (
        (right, tail, pl.ds(16, 16), (ls, lm, ld, lp, lr)),
        (left, head, pl.ds(0, 16), (rs, rm, rd, rp, rr)),
    ):
        sources = (state.at[:, :, wide], metric.at[:, wide], depth.at[short], partner.at[short], refine.at[short])
        for source, target in zip(sources, targets):
            k = len(copies)
            copies.append(pltpu.make_async_remote_copy(
                src_ref=source, dst_ref=target, send_sem=send.at[k], recv_sem=recv.at[k],
                device_id=peer, device_id_type=MESH))

    pl.semaphore_wait(barrier, len(everyone))
    for copy in round1 + copies:
        copy.start()

    for load in loads[3:]:
        load.wait()
    ends = (me == 0, me == total - 1)
    weights(wd, wt, wl, tmp, wf)
    for t in range(OWN):
        lay_state(qt, BASE + t, sv, t)
    cv[BASE : BASE + OWN, :] = GRAVITY * dv[...]
    pv[BASE : BASE + OWN, :] = av[...]

    def first_rate(g):
        m = 8 + 8 * g
        coefficients(m, mt, cv, pv, co)
        flux(m, qt, QP, state_row, mt, cv, pv, co, xt, 8 * (g % 2))
        product(m, 8 * (g % 2), xt, wl, r1)

    for g in (3, 4):
        first_rate(g)
    child_weights(wc, pw, tmp, wf)
    for copy in copies:
        copy.wait_recv()
    load_rims((ls, lm, ld, lp), (rs, rm, rd, rp), qt, mt, cv, pv, ends)
    mirror(qt, QP, state_row, mt, ends)
    for g in (2, 5, 6, 1, 0):
        first_rate(g)
    for copy in round1:
        copy.wait_recv()
    own, before1 = joined(own, box1, low, lo)
    mine2[0:1, :] = own
    for copy in round2:
        copy.start()
    r1[64 * RP : 65 * RP, :] = r1[8 * RP : 9 * RP, :]
    mirror(r1, RP, result_row, mt, ends)
    for g in range(1, 7):
        m = 8 + 8 * g
        flux(m, r1, RP, result_row, mt, cv, pv, co, xt, 8 * (g % 2))
        product(m, 8 * (g % 2), xt, wl, r2)
    prefix(lr, bv, rr, rv, pk)
    for copy in round2:
        copy.wait_recv()
    own, before2 = joined(own, box2, high, hi)
    best = jnp.where(half, own, pltpu.roll(own, 64, 1))
    before = before1 + before2
    before = jnp.where(half, pltpu.roll(before, 64, 1), before)
    stat[0:1, :] = before - (me * (OWN * 64)).astype(f32)
    step = COURANT / best
    for g in range(1, 7):
        combine(8 + 8 * g, step, qt, r1, r2, st)
    for copy in round1 + round2 + copies:
        copy.wait_send()


def wave_rate(depth, grads):
    gx, gy, hx, hy = grads
    lengths = [jnp.sqrt(vx * vx + vy * vy) for vx, vy in ((hx, hy), (gx + hx, gy + hy), (gx, gy))]
    return jnp.sqrt(GRAVITY * depth) * jnp.maximum(jnp.maximum(lengths[0], lengths[1]), lengths[2])


def lay_state(qt, m, s, t):
    for n in range(10):
        qt[m * QP + 4 * n : m * QP + 4 * n + 3, :] = s[n, :, t * 128 : (t + 1) * 128]


def lay_metric(mt, m, g, t):
    mt[m * MP : m * MP + 4, :] = g[:, t * 128 : (t + 1) * 128]


def load_rims(left, right, qt, mt, cv, pv, ends):
    ls, lm, ld, lp = left
    rs, rm, rd, rp = right

    def lay(m, s, g, t):
        lay_state(qt, m, s, t)
        lay_metric(mt, m, g, t)

    for t in range(HALO):
        lay(BASE - HALO + t, ls, lm, t)
        if t < HALO - 1:
            lay(BASE + OWN + t, rs, rm, t)
    lay(8, rs, rm, HALO - 1)
    lay(64, rs, rm, HALO - 1)
    lay(7, rs, rm, HALO - 2)
    for into, before, after, scale in ((cv, ld, rd, GRAVITY), (pv, lp, rp, 1)):
        into[BASE - HALO : BASE, :] = scale * before[16 - HALO : 16, :]
        into[BASE + OWN : BASE + OWN + 8, :] = scale * after[0:8, :]
        into[7:8, :] = scale * after[7:8, :]
        into[8:9, :] = scale * after[8:9, :]
        into[64:65, :] = scale * after[8:9, :]
    first, last = ends

    @pl.when(first)
    def _():
        cv[BASE - 1 : BASE, :] = pltpu.roll(cv[BASE : BASE + 1, :], 127, 1)

    @pl.when(last)
    def _():
        cv[BASE + OWN : BASE + OWN + 1, :] = pltpu.roll(cv[BASE + OWN - 1 : BASE + OWN, :], 1, 1)


def mirror(src, pitch, at, mt, ends):
    lane = lanes_of((1, 128))

    def row(tile, v):
        return src[tile * pitch + v : tile * pitch + v + 1, :]

    def grads(tile):
        return [mt[tile * MP + k : tile * MP + k + 1, :] for k in range(4)]

    def write(tile, rim, nodes, meet, gx, gy, shift, target):
        length = jnp.sqrt(gx * gx + gy * gy)
        nx, ny = gx / length, gy / length
        for j in range(4):
            eta, mx, my = (row(tile, at(f, nodes[j])) for f in range(3))
            normal = mx * nx + my * ny
            for f, value in enumerate((eta, mx - 2.0 * normal * nx, my - 2.0 * normal * ny)):
                v = at(f, meet[j])
                old = row(rim, v)
                src[rim * pitch + v : rim * pitch + v + 1, :] = jnp.where(
                    lane == target, pltpu.roll(value, shift, 1), old)

    first, last = ends

    @pl.when(first)
    def _():
        _, _, sx, sy = grads(BASE)
        write(BASE, BASE - 1, FACES[0], MEET[0], -sx, -sy, 127, 127)

    @pl.when(last)
    def _():
        rx, ry, sx, sy = grads(BASE + OWN - 1)
        write(BASE + OWN - 1, BASE + OWN, FACES[1], MEET[1], rx + sx, ry + sy, 1, 0)


def shifts(partner):
    lane = lanes_of((8, 128))
    j = lane + partner
    idx, inside = j & 127, (j >= 0) & (j < 128)

    def before(own, prv, nxt):
        return pltpu.roll(jnp.where(lane == 127, prv, own), 1, 1)

    def after(own, prv, nxt):
        return pltpu.roll(jnp.where(lane == 0, nxt, own), 127, 1)

    def across(own, prv, nxt):
        return jnp.where(inside, pick(own, idx), pick(jnp.where(lane < 64, nxt, prv), idx))

    return before, after, across


def coefficients(m, mt, cv, pv, co):
    rx, ry, sx, sy = (spread(mt, k, m, MP) for k in range(4))
    partner = pv[m : m + 8, :]
    three = [cv[m + s : m + s + 8, :] for s in (0, -1, 1)]
    c = three[0]
    outer = [move(*three) for move in shifts(partner)]
    outer[2] = jnp.where(partner == 0, c, outer[2])
    for k, (gx, gy) in enumerate(((sx, sy), (rx + sx, ry + sy), (rx, ry))):
        length = jnp.sqrt(gx * gx + gy * gy)
        co[k, m : m + 8, :] = outer[k]
        co[3 + k, m : m + 8, :] = length * jnp.sqrt(jnp.maximum(c, outer[k]))
        if k == 2:
            co[6, m : m + 8, :] = gx / length
            co[7, m : m + 8, :] = gy / length


def flux(m, src, pitch, at, mt, cv, pv, co, xt, slot):
    rx, ry, sx, sy = (spread(mt, k, m, MP) for k in range(4))
    c = cv[m : m + 8, :]
    partner = pv[m : m + 8, :]
    wall = partner == 0
    moves = shifts(partner)

    def value(f, n, step=0):
        return spread(src, at(f, n), m + step, pitch)

    def store(f, k, x):
        put(xt, f * 32 + k, slot, XS, x)

    crx, cry, csx, csy = -c * rx, -c * ry, -c * sx, -c * sy
    for n in range(10):
        eta, mx, my = (value(f, n) for f in range(3))
        store(0, n, -(rx * mx + ry * my))
        store(0, 10 + n, -(sx * mx + sy * my))
        store(1, n, crx * eta)
        store(1, 10 + n, csx * eta)
        store(2, n, cry * eta)
        store(2, 10 + n, csy * eta)
    vectors = ((-sx, -sy), (rx + sx, ry + sy), (-rx, -ry))
    for k in range(3):
        gx, gy = vectors[k]
        ce = co[k, m : m + 8, :]
        scale = co[3 + k, m : m + 8, :]
        for j in range(4):
            inner = [value(f, FACES[k][j]) for f in range(3)]
            outer = []
            for f in range(3):
                node = MEET[k][j]
                own = value(f, node)
                prv = value(f, node, -1) if k != 1 else None
                nxt = value(f, node, 1) if k != 0 else None
                outer.append(moves[k](own, prv, nxt))
            if k == 2:
                outer[0] = jnp.where(wall, inner[0], outer[0])
            d_eta, d_mx, d_my = (b - a for a, b in zip(inner, outer))
            if k == 2:
                nx, ny = co[6, m : m + 8, :], co[7, m : m + 8, :]
                twice = -2.0 * (inner[1] * nx + inner[2] * ny)
                d_mx = jnp.where(wall, twice * nx, d_mx)
                d_my = jnp.where(wall, twice * ny, d_my)
            drop = c * inner[0] - ce * outer[0]
            row = 20 + 4 * k + j
            store(0, row, scale * d_eta - gx * d_mx - gy * d_my)
            store(1, row, gx * drop + scale * d_mx)
            store(2, row, gy * drop + scale * d_my)


def product(m, slot, xt, wl, out):
    for pair in range(4):
        parts = []
        for t in (2 * pair, 2 * pair + 1):
            hi, lo = split(xt[(slot + t) * XS : (slot + t) * XS + XP, :])
            parts.append(jnp.concatenate([hi, lo], axis=0))
        both = jnp.concatenate(parts, axis=1)
        res = jnp.dot(wl[:, 0 : 2 * XP], both, preferred_element_type=f32)
        res = res[0:32] + res[32:64]
        tile = m + 2 * pair
        out[tile * RP : tile * RP + RR, :] = res[:, 0:128]
        out[(tile + 1) * RP : (tile + 1) * RP + RR, :] = res[:, 128:256]


def weights(diff_ops, lift, wl, tmp, wf):
    wf[...] = jnp.zeros_like(wf)
    base = jnp.zeros((16, 128), f32)
    for i, shift in ((0, 0), (1, 10), (2, 20)):
        tmp[...] = jnp.zeros_like(tmp)
        if i == 2:
            tmp[0:10, 0:12] = 0.5 * lift[...]
        else:
            for n in range(10):
                tmp[n : n + 1, 0:10] = diff_ops[n, i : i + 1, :]
        base = base + (tmp[...] if shift == 0 else pltpu.roll(tmp[...], shift, 1))
    for f in range(3):
        turned = base if f == 0 else pltpu.roll(base, 32 * f, 1)
        wf[f * 10 : f * 10 + 10, :] = turned[0:10]
    w = wf[0:32, :]
    hi = w.astype(bf16).astype(f32)
    low = w - hi
    turned = pltpu.roll(hi, XP, 1)
    lane = lanes_of((32, 128))
    wl[0:32, 0:128] = (hi + jnp.where(lane >= XP, turned, 0.0)).astype(bf16)
    wl[0:32, 128:256] = jnp.where(lane < 64, turned, 0.0).astype(bf16)
    wl[32:64, 0:128] = low.astype(bf16)
    wl[32:64, 128:256] = jnp.zeros((32, 128), bf16)


def child_weights(prolong, pw, tmp, wf):
    for i in range(3):
        wf[...] = jnp.zeros_like(wf)
        tmp[...] = jnp.zeros_like(tmp)
        if i == 0:
            eye = lax.broadcasted_iota(i32, (16, 128), 0) == lanes_of((16, 128))
            tmp[0:10, :] = jnp.where(eye, 1.0, 0.0)[0:10]
        else:
            for n in range(10):
                tmp[n : n + 1, 0:10] = prolong[n, i - 1 : i, :]
        for f in range(3):
            turned = tmp[...] if f == 0 else pltpu.roll(tmp[...], 10 * f, 1)
            wf[pl.ds(f, 10, stride=4), :] = turned[0:10]
        w = wf[...]
        hi = w.astype(bf16).astype(f32)
        low = w - hi
        pw[i * 48 : i * 48 + 48, :] = (hi + pltpu.roll(hi, 32, 1) + pltpu.roll(low, 64, 1)).astype(bf16)


def combine(m, step, qt, r1, r2, st):
    half = 0.5 * step * step
    for f in range(3):
        for n in range(10):
            v = f * 10 + n
            x = spread(qt, state_row(f, n), m, QP) + (step * spread(r1, v, m, RP) + half * spread(r2, v, m, RP))
            put(st, v, m - 16, RP, x)
    put(st, 30, m - 16, RP, jnp.zeros((8, 128), f32))
    put(st, 31, m - 16, RP, jnp.zeros((8, 128), f32))


def prefix(lr, refine, rr, rv, pk):
    rv[0:8, :] = lr[8:16, :]
    rv[8:40, :] = refine[...]
    rv[40:48, :] = rr[0:8, :]
    bits = rv[...]
    counts = (1 + bits).astype(f32)
    upper = lax.broadcasted_iota(i32, (128, 128), 0) <= lanes_of((128, 128))
    within = jnp.dot(counts.astype(bf16), upper.astype(f32).astype(bf16), preferred_element_type=f32)
    sums = jnp.broadcast_to(within[:, 127:128], (48, 128))
    lower = lanes_of((48, 48)) < lax.broadcasted_iota(i32, (48, 48), 0)
    before = jnp.dot(lower.astype(f32).astype(bf16), sums.astype(bf16), preferred_element_type=f32)
    ends = (within + before - before[8:9, :]).astype(i32)
    pk[0:48, :] = 2 * (ends - 1 - bits) + bits
    pk[48:56, :] = jnp.full((8, 128), 1 << 21, i32)


def tables(offset, rel, pk, near, code, lidx, pkw):
    pk[...] = rel[...] + 2 * offset.astype(i32)
    ends = (pk[0:48, :] >> 1) + 1 + (pk[0:48, :] & 1)
    last = jnp.broadcast_to(ends[:, 127:128], (48, 128))
    reached = (last <= lanes_of((48, 128)) * 128).astype(f32)
    first = jnp.sum(reached, axis=0, keepdims=True).astype(i32)
    near[...] = jnp.broadcast_to(first, (8, 128))
    tiles = [near[0, r] for r in range(48)]
    for r in range(48):
        pkw[0, r : r + 1, :] = pk[pl.ds(tiles[r], 1), :]
        pkw[1, r : r + 1, :] = pk[pl.ds(tiles[r] + 1, 1), :]
    for g in range(6):
        rows = slice(8 * g, 8 * g + 8)
        p0, p1 = pkw[0, rows, :], pkw[1, rows, :]
        e0 = (p0 >> 1) + 1 + (p0 & 1)
        e1 = (p1 >> 1) + 1 + (p1 & 1)
        slot = (8 * g + lax.broadcasted_iota(i32, (8, 128), 0)) * 128 + lanes_of((8, 128))
        over = jnp.broadcast_to(e0[:, 127:128], (8, 128)) <= slot
        pos = jnp.zeros((8, 128), i32)
        for s in (64, 32, 16, 8, 4, 2, 1):
            probe = pos + (s - 1)
            e = jnp.where(over, pick(e1, probe), pick(e0, probe))
            pos = jnp.where(e <= slot, pos + s, pos)
        got = jnp.where(over, pick(p1, pos), pick(p0, pos))
        which = slot - (got >> 1)
        lidx[rows, :] = jnp.where(over, pos + 128, pos)
        code[rows, :] = jnp.where((got & 1) == 0, 0, 1 + which)
    return tiles


def place(rel, pw, stat, st, out, new_tiles, pk, near, code, lidx, pkw, sems):
    tiles = tables(stat[0:1, :], rel, pk, near, code, lidx, pkw)
    weight = pw[:, 0:96]
    stores = []
    for pair in range(24):
        parts = []
        for r in (2 * pair, 2 * pair + 1):
            begin = tiles[r] * RP
            near_tile = st[pl.ds(begin, RR), :]
            far_tile = st[pl.ds(begin + RP, RR), :]
            idx = jnp.broadcast_to(lidx[r : r + 1, :], (RR, 128))
            low = idx & 127
            s = jnp.where(idx < 128, pick(near_tile, low), pick(far_tile, low))
            hi, lo = split(s)
            parts.append(jnp.concatenate([hi, lo, hi], axis=0))
        res = jnp.dot(weight, jnp.concatenate(parts, axis=1), preferred_element_type=f32)
        for i in range(2):
            r = 2 * pair + i
            one = res[:, 128 * i : 128 * i + 128]
            kind = jnp.broadcast_to(code[r : r + 1, :], (48, 128))
            new = jnp.where(kind == 0, one[0:48], jnp.where(kind == 1, one[48:96], one[96:144]))
            for n in range(10):
                new_tiles[n, :, r * 128 : (r + 1) * 128] = new[4 * n : 4 * n + 3]
        if pair % 6 == 5:
            part = pl.ds((pair // 6) * 1536, 1536)
            store = pltpu.make_async_copy(new_tiles.at[:, :, part], out.at[:, :, part], sems.at[pair // 6])
            store.start()
            stores.append(store)
    for store in stores:
        store.wait()


def solution(mesh):
    rows, cols = mesh.shape["row"], mesh.shape["col"]
    total = rows * cols
    low = 16 if total % 256 == 0 else max(total // 2, 1)
    high = total // low
    placed = OWN + OWN // 2

    def shards(state, depth, metric, partner, refine, diff_ops, lift, prolong):
        depth, partner, refine = (a.reshape(OWN, 128) for a in (depth, partner, refine))
        state, diff_ops, prolong = (a.transpose(1, 0, 2) for a in (state, diff_ops, prolong))
        args = (state, metric, depth, partner, refine, diff_ops, lift, prolong)
        vm, hbm = pl.BlockSpec(memory_space=pltpu.VMEM), pl.BlockSpec(memory_space=pl.ANY)
        side = [
            pltpu.VMEM((10, 3, WIDE), f32),
            pltpu.VMEM((4, WIDE), f32),
            pltpu.VMEM((16, 128), f32),
            pltpu.VMEM((16, 128), i32),
            pltpu.VMEM((16, 128), i32),
        ]
        st, pk, pw, stat = pl.pallas_call(
            functools.partial(advance, rows, cols, low),
            out_shape=[
                pltpu.VMEM((((placed + 1) * RP + 7) // 8 * 8, 128), f32),
                pltpu.VMEM((56, 128), i32),
                pltpu.VMEM((144, 128), bf16),
                pltpu.VMEM((8, 128), f32),
            ],
            in_specs=[hbm] * 8,
            out_specs=[vm] * 4,
            scratch_shapes=[pltpu.VMEM(a.shape, a.dtype) for a in args]
            + side
            + side
            + [
                pltpu.VMEM((MEM * QP, 128), f32),
                pltpu.VMEM((MEM * MP, 128), f32),
                pltpu.VMEM((MEM, 128), f32),
                pltpu.VMEM((MEM, 128), i32),
                pltpu.VMEM((8, MEM, 128), f32),
                pltpu.VMEM((16 * XS, 128), f32),
                pltpu.VMEM((MEM * RP, 128), f32),
                pltpu.VMEM((MEM * RP, 128), f32),
                pltpu.VMEM((64, 256), bf16),
                pltpu.VMEM((16, 128), f32),
                pltpu.VMEM((48, 128), f32),
                pltpu.VMEM((48, 128), i32),
                pltpu.VMEM((8, 128), f32),
                pltpu.VMEM((low, 128), f32),
                pltpu.VMEM((8, 128), f32),
                pltpu.VMEM((high, 128), f32),
                pltpu.SemaphoreType.DMA((8,)),
                pltpu.SemaphoreType.DMA((10,)),
                pltpu.SemaphoreType.DMA((10,)),
                pltpu.SemaphoreType.DMA((low - 1,)),
                pltpu.SemaphoreType.DMA((low - 1,)),
                pltpu.SemaphoreType.DMA((high - 1,)),
                pltpu.SemaphoreType.DMA((high - 1,)),
            ],
            compiler_params=pltpu.CompilerParams(collective_id=0, has_side_effects=True),
            name="advance",
        )(*args)
        new = pl.pallas_call(
            place,
            out_shape=jax.ShapeDtypeStruct((10, 3, placed * 128), f32),
            in_specs=[vm] * 4,
            out_specs=hbm,
            scratch_shapes=[
                pltpu.VMEM((10, 3, placed * 128), f32),
                pltpu.VMEM((56, 128), i32),
                pltpu.VMEM((8, 128), i32),
                pltpu.VMEM((48, 128), i32),
                pltpu.VMEM((48, 128), i32),
                pltpu.VMEM((2, 48, 128), i32),
                pltpu.SemaphoreType.DMA((4,)),
            ],
            name="place",
        )(*(pltpu.with_memory_space_constraint(a, pltpu.VMEM) for a in (pk, pw, stat, st)))
        return new.transpose(1, 0, 2)

    halves = ("row", "col")
    return jax.shard_map(
        shards,
        mesh=mesh,
        in_specs=(P(None, None, halves), P(halves), P(None, halves), P(halves), P(halves), P(), P(), P()),
        out_specs=P(None, None, halves),
        check_vma=False,
    )
```

```python
import functools

import jax
import jax.numpy as jnp
from jax import lax
from jax.experimental import pallas as pl
from jax.experimental.pallas import tpu as pltpu
from jax.sharding import PartitionSpec as P

GRAVITY = 9.81
COURANT = 0.5
MESH = pl.DeviceIdType.MESH

OWN = 32
HALO = 9
WIDE = HALO * 128
BASE = 24
MEM = 72
QP = 41
RR = 32
RP = 33
MP = 9
XP = 96
XS = 97

FACES = ((0, 1, 2, 3), (3, 6, 8, 9), (9, 7, 4, 0))
MEET = ((9, 8, 6, 3), (3, 2, 1, 0), (0, 4, 7, 9))

f32 = jnp.float32
bf16 = jnp.bfloat16
i32 = jnp.int32


def lanes_of(shape):
    return lax.broadcasted_iota(i32, shape, len(shape) - 1)


def state_row(f, n):
    return 4 * n + f


def result_row(f, n):
    return 10 * f + n


def spread(ref, v, tile, pitch):
    return ref[pl.ds(tile * pitch + v, 8, stride=pitch), :]


def put(ref, v, tile, pitch, value):
    ref[pl.ds(tile * pitch + v, 8, stride=pitch), :] = value


def pick(x, idx):
    return jnp.take_along_axis(x, idx, axis=1, mode="promise_in_bounds")


def split(x):
    hi = x.astype(bf16)
    return hi, (x - hi.astype(f32)).astype(bf16)


def joined(own, box, members, earlier):
    part = box[0:members, :]
    best = jnp.maximum(own, jnp.max(part, axis=0, keepdims=True))
    both = own + jnp.sum(part, axis=0, keepdims=True)
    d = lax.broadcasted_iota(i32, part.shape, 0) + 1
    before = jnp.sum(jnp.where(earlier(d), part, 0.0), axis=0, keepdims=True)
    return jnp.where(lanes_of((1, 128)) < 64, best, both), before


def advance(
    rows, cols, low,
    state, metric, depth, partner, refine, diff_ops, lift, prolong,
    st, pk, pw, stat,
    sv, gv, dv, av, bv, wd, wt, wc,
    ls, lm, ld, lp, lr, rs, rm, rd, rp, rr,
    qt, mt, cv, pv, co, xt, r1, r2, wl, tmp, wf, rv,
    mine, box1, mine2, box2,
    here, send, recv, send1, recv1, send2, recv2,
):
    total = rows * cols
    part, deep = cols // low, rows * (cols // low)
    row, col = lax.axis_index("row"), lax.axis_index("col")
    me = row * cols + col
    block, lo = col // low, lax.rem(col, low)

    def wrapped(x, n):
        return jnp.where(x >= n, x - n, x)

    def hops(d, n):
        return min(d, n - d)

    over = wrapped(col + 1, cols)
    under = wrapped(col + cols - 1, cols)
    right = (jnp.where(over == 0, wrapped(row + 1, rows), row), over)
    left = (jnp.where(col == 0, wrapped(row + rows - 1, rows), row), under)
    near = sorted(range(1, low), key=lambda d: -hops(d // 2, low // 2))
    peers1 = {d: (row, block * low + wrapped(lo + d, low)) for d in near}
    row_at = [wrapped(row + d, rows) for d in range(rows)]
    col_at = [wrapped(block + d, part) * low + lo for d in range(part)]
    far = sorted(range(1, deep), key=lambda d: -hops(d // part, rows) - hops(d % part, part))
    peers2 = {d: (row_at[d // part], col_at[d % part]) for d in far}
    everyone = [peers1[d] for d in near] + [peers2[d] for d in far] + [left, right]

    pairs = (
        (metric, gv), (depth, dv), (refine, bv), (state, sv), (partner, av), (diff_ops, wd), (lift, wt), (prolong, wc))
    loads = [pltpu.make_async_copy(a, b, here.at[k]) for k, (a, b) in enumerate(pairs)]
    for load in loads[:3]:
        load.start()
    barrier = pltpu.get_barrier_semaphore()
    for peer in everyone:
        pl.semaphore_signal(barrier, inc=1, device_id=peer, device_id_type=MESH)
    for load in loads[3:]:
        load.start()
    for load in loads[:3]:
        load.wait()
    for t in range(OWN):
        lay_metric(mt, BASE + t, gv, t)
    grads = [mt[pl.ds(BASE * MP + k, OWN, stride=MP), :] for k in range(4)]
    rate = wave_rate(dv[...], grads)
    top = jnp.max(jnp.max(rate, axis=0, keepdims=True), axis=1, keepdims=True)
    count = jnp.sum(bv[...].astype(f32), axis=0, keepdims=True)
    count = jnp.sum(count, axis=1, keepdims=True)
    half = lanes_of((1, 128)) < 64
    own = jnp.where(half, top, count)
    mine[0:1, :] = own

    def round_of(source, box, peers, sems, rems):
        return [
            pltpu.make_async_remote_copy(
                src_ref=source.at[pl.ds(0, 1)], dst_ref=box.at[pl.ds(d - 1, 1)],
                send_sem=sems.at[d - 1], recv_sem=rems.at[d - 1], device_id=peer, device_id_type=MESH)
            for d, peer in peers.items()
        ]

    round1 = round_of(mine, box1, peers1, send1, recv1)
    round2 = round_of(mine2, box2, peers2, send2, recv2)
    tail, head = pl.ds((OWN - HALO) * 128, WIDE), pl.ds(0, WIDE)
    copies = []
    for peer, wide, short, targets in (
        (right, tail, pl.ds(16, 16), (ls, lm, ld, lp, lr)),
        (left, head, pl.ds(0, 16), (rs, rm, rd, rp, rr)),
    ):
        sources = (state.at[:, :, wide], metric.at[:, wide], depth.at[short], partner.at[short], refine.at[short])
        for source, target in zip(sources, targets):
            k = len(copies)
            copies.append(pltpu.make_async_remote_copy(
                src_ref=source, dst_ref=target, send_sem=send.at[k], recv_sem=recv.at[k],
                device_id=peer, device_id_type=MESH))

    pl.semaphore_wait(barrier, len(everyone))
    for copy in round1 + copies:
        copy.start()

    for load in loads[3:]:
        load.wait()
    ends = (me == 0, me == total - 1)
    weights(wd, wt, wl, tmp, wf)
    for t in range(OWN):
        lay_state(qt, BASE + t, sv, t)
    cv[BASE : BASE + OWN, :] = GRAVITY * dv[...]
    pv[BASE : BASE + OWN, :] = av[...]

    def first_rate(g):
        m = 8 + 8 * g
        coefficients(m, mt, cv, pv, co)
        flux(m, qt, QP, state_row, mt, cv, pv, co, xt, 8 * (g % 2))
        product(m, 8 * (g % 2), xt, wl, r1)

    for g in (3, 4):
        first_rate(g)
    child_weights(wc, pw, tmp, wf)

    def earlier2(d):
        r, b = row - d // part, block - d % part
        r, b = jnp.where(r < 0, r + rows, r), jnp.where(b < 0, b + part, b)
        return r * part + b < row * part + block

    for copy in round1:
        copy.wait_recv()
    own, before1 = joined(own, box1, low - 1, lambda d: d <= lo)
    mine2[0:1, :] = own
    for copy in round2:
        copy.start()
    for copy in copies:
        copy.wait_recv()
    load_rims((ls, lm, ld, lp), (rs, rm, rd, rp), qt, mt, cv, pv, ends)
    mirror(qt, QP, state_row, mt, ends)
    for g in (2, 5, 6, 1, 0):
        first_rate(g)
    r1[64 * RP : 65 * RP, :] = r1[8 * RP : 9 * RP, :]
    mirror(r1, RP, result_row, mt, ends)
    for g in range(1, 7):
        m = 8 + 8 * g
        flux(m, r1, RP, result_row, mt, cv, pv, co, xt, 8 * (g % 2))
        product(m, 8 * (g % 2), xt, wl, r2)
    prefix(lr, bv, rr, rv, pk)
    for copy in round1 + round2 + copies:
        copy.wait_send()
    for copy in round2:
        copy.wait_recv()
    own, before2 = joined(own, box2, deep - 1, earlier2)
    best = jnp.where(half, own, pltpu.roll(own, 64, 1))
    before = before1 + before2
    before = jnp.where(half, pltpu.roll(before, 64, 1), before)
    stat[0:1, :] = before - (me * (OWN * 64)).astype(f32)
    step = COURANT / best
    for g in range(1, 7):
        combine(8 + 8 * g, step, qt, r1, r2, st)


def wave_rate(depth, grads):
    gx, gy, hx, hy = grads
    lengths = [jnp.sqrt(vx * vx + vy * vy) for vx, vy in ((hx, hy), (gx + hx, gy + hy), (gx, gy))]
    return jnp.sqrt(GRAVITY * depth) * jnp.maximum(jnp.maximum(lengths[0], lengths[1]), lengths[2])


def lay_state(qt, m, s, t):
    for n in range(10):
        qt[m * QP + 4 * n : m * QP + 4 * n + 3, :] = s[n, :, t * 128 : (t + 1) * 128]


def lay_metric(mt, m, g, t):
    mt[m * MP : m * MP + 4, :] = g[:, t * 128 : (t + 1) * 128]


def load_rims(left, right, qt, mt, cv, pv, ends):
    ls, lm, ld, lp = left
    rs, rm, rd, rp = right

    def lay(m, s, g, t):
        lay_state(qt, m, s, t)
        lay_metric(mt, m, g, t)

    for t in range(HALO):
        lay(BASE - HALO + t, ls, lm, t)
        if t < HALO - 1:
            lay(BASE + OWN + t, rs, rm, t)
    lay(8, rs, rm, HALO - 1)
    lay(64, rs, rm, HALO - 1)
    lay(7, rs, rm, HALO - 2)
    for into, before, after, scale in ((cv, ld, rd, GRAVITY), (pv, lp, rp, 1)):
        into[BASE - HALO : BASE, :] = scale * before[16 - HALO : 16, :]
        into[BASE + OWN : BASE + OWN + 8, :] = scale * after[0:8, :]
        into[7:8, :] = scale * after[7:8, :]
        into[8:9, :] = scale * after[8:9, :]
        into[64:65, :] = scale * after[8:9, :]
    first, last = ends

    @pl.when(first)
    def _():
        cv[BASE - 1 : BASE, :] = pltpu.roll(cv[BASE : BASE + 1, :], 127, 1)

    @pl.when(last)
    def _():
        cv[BASE + OWN : BASE + OWN + 1, :] = pltpu.roll(cv[BASE + OWN - 1 : BASE + OWN, :], 1, 1)


def mirror(src, pitch, at, mt, ends):
    lane = lanes_of((1, 128))

    def row(tile, v):
        return src[tile * pitch + v : tile * pitch + v + 1, :]

    def grads(tile):
        return [mt[tile * MP + k : tile * MP + k + 1, :] for k in range(4)]

    def write(tile, rim, nodes, meet, gx, gy, shift, target):
        length = jnp.sqrt(gx * gx + gy * gy)
        nx, ny = gx / length, gy / length
        for j in range(4):
            eta, mx, my = (row(tile, at(f, nodes[j])) for f in range(3))
            normal = mx * nx + my * ny
            for f, value in enumerate((eta, mx - 2.0 * normal * nx, my - 2.0 * normal * ny)):
                v = at(f, meet[j])
                old = row(rim, v)
                src[rim * pitch + v : rim * pitch + v + 1, :] = jnp.where(
                    lane == target, pltpu.roll(value, shift, 1), old)

    first, last = ends

    @pl.when(first)
    def _():
        _, _, sx, sy = grads(BASE)
        write(BASE, BASE - 1, FACES[0], MEET[0], -sx, -sy, 127, 127)

    @pl.when(last)
    def _():
        rx, ry, sx, sy = grads(BASE + OWN - 1)
        write(BASE + OWN - 1, BASE + OWN, FACES[1], MEET[1], rx + sx, ry + sy, 1, 0)


def shifts(partner):
    lane = lanes_of((8, 128))
    j = lane + partner
    idx, inside = j & 127, (j >= 0) & (j < 128)

    def before(own, prv, nxt):
        return pltpu.roll(jnp.where(lane == 127, prv, own), 1, 1)

    def after(own, prv, nxt):
        return pltpu.roll(jnp.where(lane == 0, nxt, own), 127, 1)

    def across(own, prv, nxt):
        return jnp.where(inside, pick(own, idx), pick(jnp.where(lane < 64, nxt, prv), idx))

    return before, after, across


def coefficients(m, mt, cv, pv, co):
    rx, ry, sx, sy = (spread(mt, k, m, MP) for k in range(4))
    partner = pv[m : m + 8, :]
    three = [cv[m + s : m + s + 8, :] for s in (0, -1, 1)]
    c = three[0]
    outer = [move(*three) for move in shifts(partner)]
    outer[2] = jnp.where(partner == 0, c, outer[2])
    for k, (gx, gy) in enumerate(((sx, sy), (rx + sx, ry + sy), (rx, ry))):
        length = jnp.sqrt(gx * gx + gy * gy)
        co[k, m : m + 8, :] = outer[k]
        co[3 + k, m : m + 8, :] = length * jnp.sqrt(jnp.maximum(c, outer[k]))
        if k == 2:
            co[6, m : m + 8, :] = gx / length
            co[7, m : m + 8, :] = gy / length


def flux(m, src, pitch, at, mt, cv, pv, co, xt, slot):
    rx, ry, sx, sy = (spread(mt, k, m, MP) for k in range(4))
    c = cv[m : m + 8, :]
    partner = pv[m : m + 8, :]
    wall = partner == 0
    moves = shifts(partner)

    def value(f, n, step=0):
        return spread(src, at(f, n), m + step, pitch)

    def store(f, k, x):
        put(xt, f * 32 + k, slot, XS, x)

    crx, cry, csx, csy = -c * rx, -c * ry, -c * sx, -c * sy
    for n in range(10):
        eta, mx, my = (value(f, n) for f in range(3))
        store(0, n, -(rx * mx + ry * my))
        store(0, 10 + n, -(sx * mx + sy * my))
        store(1, n, crx * eta)
        store(1, 10 + n, csx * eta)
        store(2, n, cry * eta)
        store(2, 10 + n, csy * eta)
    vectors = ((-sx, -sy), (rx + sx, ry + sy), (-rx, -ry))
    for k in range(3):
        gx, gy = vectors[k]
        ce = co[k, m : m + 8, :]
        scale = co[3 + k, m : m + 8, :]
        for j in range(4):
            inner = [value(f, FACES[k][j]) for f in range(3)]
            outer = []
            for f in range(3):
                node = MEET[k][j]
                own = value(f, node)
                prv = value(f, node, -1) if k != 1 else None
                nxt = value(f, node, 1) if k != 0 else None
                outer.append(moves[k](own, prv, nxt))
            if k == 2:
                outer[0] = jnp.where(wall, inner[0], outer[0])
            d_eta, d_mx, d_my = (b - a for a, b in zip(inner, outer))
            if k == 2:
                nx, ny = co[6, m : m + 8, :], co[7, m : m + 8, :]
                twice = -2.0 * (inner[1] * nx + inner[2] * ny)
                d_mx = jnp.where(wall, twice * nx, d_mx)
                d_my = jnp.where(wall, twice * ny, d_my)
            drop = c * inner[0] - ce * outer[0]
            row = 20 + 4 * k + j
            store(0, row, scale * d_eta - gx * d_mx - gy * d_my)
            store(1, row, gx * drop + scale * d_mx)
            store(2, row, gy * drop + scale * d_my)


def product(m, slot, xt, wl, out):
    for pair in range(4):
        parts = []
        for t in (2 * pair, 2 * pair + 1):
            hi, lo = split(xt[(slot + t) * XS : (slot + t) * XS + XP, :])
            parts.append(jnp.concatenate([hi, lo], axis=0))
        both = jnp.concatenate(parts, axis=1)
        res = jnp.dot(wl[:, 0 : 2 * XP], both, preferred_element_type=f32)
        res = res[0:32] + res[32:64]
        tile = m + 2 * pair
        out[tile * RP : tile * RP + RR, :] = res[:, 0:128]
        out[(tile + 1) * RP : (tile + 1) * RP + RR, :] = res[:, 128:256]


def weights(diff_ops, lift, wl, tmp, wf):
    wf[...] = jnp.zeros_like(wf)
    base = jnp.zeros((16, 128), f32)
    for i, shift in ((0, 0), (1, 10), (2, 20)):
        tmp[...] = jnp.zeros_like(tmp)
        if i == 2:
            tmp[0:10, 0:12] = 0.5 * lift[...]
        else:
            for n in range(10):
                tmp[n : n + 1, 0:10] = diff_ops[n, i : i + 1, :]
        base = base + (tmp[...] if shift == 0 else pltpu.roll(tmp[...], shift, 1))
    for f in range(3):
        turned = base if f == 0 else pltpu.roll(base, 32 * f, 1)
        wf[f * 10 : f * 10 + 10, :] = turned[0:10]
    w = wf[0:32, :]
    hi = w.astype(bf16).astype(f32)
    low = w - hi
    turned = pltpu.roll(hi, XP, 1)
    lane = lanes_of((32, 128))
    wl[0:32, 0:128] = (hi + jnp.where(lane >= XP, turned, 0.0)).astype(bf16)
    wl[0:32, 128:256] = jnp.where(lane < 64, turned, 0.0).astype(bf16)
    wl[32:64, 0:128] = low.astype(bf16)
    wl[32:64, 128:256] = jnp.zeros((32, 128), bf16)


def child_weights(prolong, pw, tmp, wf):
    for i in range(3):
        wf[...] = jnp.zeros_like(wf)
        tmp[...] = jnp.zeros_like(tmp)
        if i == 0:
            eye = lax.broadcasted_iota(i32, (16, 128), 0) == lanes_of((16, 128))
            tmp[0:10, :] = jnp.where(eye, 1.0, 0.0)[0:10]
        else:
            for n in range(10):
                tmp[n : n + 1, 0:10] = prolong[n, i - 1 : i, :]
        for f in range(3):
            turned = tmp[...] if f == 0 else pltpu.roll(tmp[...], 10 * f, 1)
            wf[pl.ds(f, 10, stride=4), :] = turned[0:10]
        w = wf[...]
        hi = w.astype(bf16).astype(f32)
        low = w - hi
        pw[i * 48 : i * 48 + 48, :] = (hi + pltpu.roll(hi, 32, 1) + pltpu.roll(low, 64, 1)).astype(bf16)


def combine(m, step, qt, r1, r2, st):
    half = 0.5 * step * step
    for f in range(3):
        for n in range(10):
            v = f * 10 + n
            x = spread(qt, state_row(f, n), m, QP) + (step * spread(r1, v, m, RP) + half * spread(r2, v, m, RP))
            put(st, v, m - 16, RP, x)
    put(st, 30, m - 16, RP, jnp.zeros((8, 128), f32))
    put(st, 31, m - 16, RP, jnp.zeros((8, 128), f32))


def prefix(lr, refine, rr, rv, pk):
    rv[0:8, :] = lr[8:16, :]
    rv[8:40, :] = refine[...]
    rv[40:48, :] = rr[0:8, :]
    bits = rv[...]
    counts = (1 + bits).astype(f32)
    upper = lax.broadcasted_iota(i32, (128, 128), 0) <= lanes_of((128, 128))
    within = jnp.dot(counts.astype(bf16), upper.astype(f32).astype(bf16), preferred_element_type=f32)
    sums = jnp.broadcast_to(within[:, 127:128], (48, 128))
    lower = lanes_of((48, 48)) < lax.broadcasted_iota(i32, (48, 48), 0)
    before = jnp.dot(lower.astype(f32).astype(bf16), sums.astype(bf16), preferred_element_type=f32)
    ends = (within + before - before[8:9, :]).astype(i32)
    pk[0:48, :] = 2 * (ends - 1 - bits) + bits
    pk[48:56, :] = jnp.full((8, 128), 1 << 21, i32)


def tables(offset, rel, pk, near, code, lidx, pkw):
    pk[...] = rel[...] + 2 * offset.astype(i32)
    ends = (pk[0:48, :] >> 1) + 1 + (pk[0:48, :] & 1)
    last = jnp.broadcast_to(ends[:, 127:128], (48, 128))
    reached = (last <= lanes_of((48, 128)) * 128).astype(f32)
    first = jnp.sum(reached, axis=0, keepdims=True).astype(i32)
    near[...] = jnp.broadcast_to(first, (8, 128))
    tiles = [near[0, r] for r in range(48)]
    for r in range(48):
        pkw[0, r : r + 1, :] = pk[pl.ds(tiles[r], 1), :]
        pkw[1, r : r + 1, :] = pk[pl.ds(tiles[r] + 1, 1), :]
    for g in range(6):
        rows = slice(8 * g, 8 * g + 8)
        p0, p1 = pkw[0, rows, :], pkw[1, rows, :]
        e0 = (p0 >> 1) + 1 + (p0 & 1)
        e1 = (p1 >> 1) + 1 + (p1 & 1)
        slot = (8 * g + lax.broadcasted_iota(i32, (8, 128), 0)) * 128 + lanes_of((8, 128))
        over = jnp.broadcast_to(e0[:, 127:128], (8, 128)) <= slot
        pos = jnp.zeros((8, 128), i32)
        for s in (64, 32, 16, 8, 4, 2, 1):
            probe = pos + (s - 1)
            e = jnp.where(over, pick(e1, probe), pick(e0, probe))
            pos = jnp.where(e <= slot, pos + s, pos)
        got = jnp.where(over, pick(p1, pos), pick(p0, pos))
        which = slot - (got >> 1)
        lidx[rows, :] = jnp.where(over, pos + 128, pos)
        code[rows, :] = jnp.where((got & 1) == 0, 0, 1 + which)
    return tiles


def place(rel, pw, stat, st, out, new_tiles, pk, near, code, lidx, pkw, sems):
    tiles = tables(stat[0:1, :], rel, pk, near, code, lidx, pkw)
    weight = pw[:, 0:96]
    stores = []
    for pair in range(24):
        parts = []
        for r in (2 * pair, 2 * pair + 1):
            begin = tiles[r] * RP
            near_tile = st[pl.ds(begin, RR), :]
            far_tile = st[pl.ds(begin + RP, RR), :]
            idx = jnp.broadcast_to(lidx[r : r + 1, :], (RR, 128))
            low = idx & 127
            s = jnp.where(idx < 128, pick(near_tile, low), pick(far_tile, low))
            hi, lo = split(s)
            parts.append(jnp.concatenate([hi, lo, hi], axis=0))
        res = jnp.dot(weight, jnp.concatenate(parts, axis=1), preferred_element_type=f32)
        for i in range(2):
            r = 2 * pair + i
            one = res[:, 128 * i : 128 * i + 128]
            kind = jnp.broadcast_to(code[r : r + 1, :], (48, 128))
            new = jnp.where(kind == 0, one[0:48], jnp.where(kind == 1, one[48:96], one[96:144]))
            for n in range(10):
                new_tiles[n, :, r * 128 : (r + 1) * 128] = new[4 * n : 4 * n + 3]
        if pair % 6 == 5:
            part = pl.ds((pair // 6) * 1536, 1536)
            store = pltpu.make_async_copy(new_tiles.at[:, :, part], out.at[:, :, part], sems.at[pair // 6])
            store.start()
            stores.append(store)
    for store in stores:
        store.wait()


def solution(mesh):
    rows, cols = mesh.shape["row"], mesh.shape["col"]
    total = rows * cols
    low = min(16, cols // 2)
    high = total // low
    placed = OWN + OWN // 2

    def shards(state, depth, metric, partner, refine, diff_ops, lift, prolong):
        depth, partner, refine = (a.reshape(OWN, 128) for a in (depth, partner, refine))
        state, diff_ops, prolong = (a.transpose(1, 0, 2) for a in (state, diff_ops, prolong))
        args = (state, metric, depth, partner, refine, diff_ops, lift, prolong)
        vm, hbm = pl.BlockSpec(memory_space=pltpu.VMEM), pl.BlockSpec(memory_space=pl.ANY)
        side = [
            pltpu.VMEM((10, 3, WIDE), f32),
            pltpu.VMEM((4, WIDE), f32),
            pltpu.VMEM((16, 128), f32),
            pltpu.VMEM((16, 128), i32),
            pltpu.VMEM((16, 128), i32),
        ]
        st, pk, pw, stat = pl.pallas_call(
            functools.partial(advance, rows, cols, low),
            out_shape=[
                pltpu.VMEM((((placed + 1) * RP + 7) // 8 * 8, 128), f32),
                pltpu.VMEM((56, 128), i32),
                pltpu.VMEM((144, 128), bf16),
                pltpu.VMEM((8, 128), f32),
            ],
            in_specs=[hbm] * 8,
            out_specs=[vm] * 4,
            scratch_shapes=[pltpu.VMEM(a.shape, a.dtype) for a in args]
            + side
            + side
            + [
                pltpu.VMEM((MEM * QP, 128), f32),
                pltpu.VMEM((MEM * MP, 128), f32),
                pltpu.VMEM((MEM, 128), f32),
                pltpu.VMEM((MEM, 128), i32),
                pltpu.VMEM((8, MEM, 128), f32),
                pltpu.VMEM((16 * XS, 128), f32),
                pltpu.VMEM((MEM * RP, 128), f32),
                pltpu.VMEM((MEM * RP, 128), f32),
                pltpu.VMEM((64, 256), bf16),
                pltpu.VMEM((16, 128), f32),
                pltpu.VMEM((48, 128), f32),
                pltpu.VMEM((48, 128), i32),
                pltpu.VMEM((8, 128), f32),
                pltpu.VMEM((low, 128), f32),
                pltpu.VMEM((8, 128), f32),
                pltpu.VMEM((high, 128), f32),
                pltpu.SemaphoreType.DMA((8,)),
                pltpu.SemaphoreType.DMA((10,)),
                pltpu.SemaphoreType.DMA((10,)),
                pltpu.SemaphoreType.DMA((low - 1,)),
                pltpu.SemaphoreType.DMA((low - 1,)),
                pltpu.SemaphoreType.DMA((high - 1,)),
                pltpu.SemaphoreType.DMA((high - 1,)),
            ],
            compiler_params=pltpu.CompilerParams(collective_id=0, has_side_effects=True),
            name="advance",
        )(*args)
        new = pl.pallas_call(
            place,
            out_shape=jax.ShapeDtypeStruct((10, 3, placed * 128), f32),
            in_specs=[vm] * 4,
            out_specs=hbm,
            scratch_shapes=[
                pltpu.VMEM((10, 3, placed * 128), f32),
                pltpu.VMEM((56, 128), i32),
                pltpu.VMEM((8, 128), i32),
                pltpu.VMEM((48, 128), i32),
                pltpu.VMEM((48, 128), i32),
                pltpu.VMEM((2, 48, 128), i32),
                pltpu.SemaphoreType.DMA((4,)),
            ],
            name="place",
        )(*(pltpu.with_memory_space_constraint(a, pltpu.VMEM) for a in (pk, pw, stat, st)))
        return new.transpose(1, 0, 2)

    halves = ("row", "col")
    return jax.shard_map(
        shards,
        mesh=mesh,
        in_specs=(P(None, None, halves), P(halves), P(None, halves), P(halves), P(halves), P(), P(), P()),
        out_specs=P(None, None, halves),
        check_vma=False,
    )
```

```python
import functools

import jax
import jax.numpy as jnp
from jax import lax
from jax.experimental import pallas as pl
from jax.experimental.pallas import tpu as pltpu
from jax.sharding import PartitionSpec as P

GRAVITY = 9.81
COURANT = 0.5
MESH = pl.DeviceIdType.MESH

OWN = 32
HALO = 9
WIDE = HALO * 128
BASE = 24
MEM = 72
QP = 41
RR = 32
RP = 33
MP = 9
XP = 96
XS = 97

FACES = ((0, 1, 2, 3), (3, 6, 8, 9), (9, 7, 4, 0))
MEET = ((9, 8, 6, 3), (3, 2, 1, 0), (0, 4, 7, 9))

f32 = jnp.float32
bf16 = jnp.bfloat16
i32 = jnp.int32


def lanes_of(shape):
    return lax.broadcasted_iota(i32, shape, len(shape) - 1)


def state_row(f, n):
    return 4 * n + f


def result_row(f, n):
    return 10 * f + n


def spread(ref, v, tile, pitch):
    return ref[pl.ds(tile * pitch + v, 8, stride=pitch), :]


def put(ref, v, tile, pitch, value):
    ref[pl.ds(tile * pitch + v, 8, stride=pitch), :] = value


def pick(x, idx):
    return jnp.take_along_axis(x, idx, axis=1, mode="promise_in_bounds")


def split(x):
    hi = x.astype(bf16)
    return hi, (x - hi.astype(f32)).astype(bf16)


def joined(own, box, members, earlier):
    part = box[0:members, :]
    best = jnp.maximum(own, jnp.max(part, axis=0, keepdims=True))
    both = own + jnp.sum(part, axis=0, keepdims=True)
    d = lax.broadcasted_iota(i32, part.shape, 0) + 1
    before = jnp.sum(jnp.where(earlier(d), part, 0.0), axis=0, keepdims=True)
    return jnp.where(lanes_of((1, 128)) < 64, best, both), before


def advance(
    rows, cols, low,
    state, metric, depth, partner, refine, diff_ops, lift, prolong,
    st, tab, pw, stat,
    sv, gv, dv, av, bv, wd, wt, wc,
    ls, lm, ld, lp, lr, rs, rm, rd, rp, rr,
    qt, mt, cv, pv, co, xt, r1, r2, wl, tmp, wf, rv, pk, pkw,
    mine, box1, mine2, box2,
    here, send, recv, send1, recv1, send2, recv2,
):
    total = rows * cols
    part, deep = cols // low, rows * (cols // low)
    row, col = lax.axis_index("row"), lax.axis_index("col")
    me = row * cols + col
    block, lo = col // low, lax.rem(col, low)

    def wrapped(x, n):
        return jnp.where(x >= n, x - n, x)

    def hops(d, n):
        return min(d, n - d)

    over = wrapped(col + 1, cols)
    under = wrapped(col + cols - 1, cols)
    right = (jnp.where(over == 0, wrapped(row + 1, rows), row), over)
    left = (jnp.where(col == 0, wrapped(row + rows - 1, rows), row), under)
    close = sorted(range(1, low), key=lambda d: -hops(d // 2, low // 2))
    peers1 = {d: (row, block * low + wrapped(lo + d, low)) for d in close}
    row_at = [wrapped(row + d, rows) for d in range(rows)]
    col_at = [wrapped(block + d, part) * low + lo for d in range(part)]
    far = sorted(range(1, deep), key=lambda d: -hops(d // part, rows) - hops(d % part, part))
    peers2 = {d: (row_at[d // part], col_at[d % part]) for d in far}
    everyone = [peers1[d] for d in close] + [peers2[d] for d in far] + [left, right]

    pairs = (
        (metric, gv), (depth, dv), (refine, bv), (state, sv), (partner, av), (diff_ops, wd), (lift, wt), (prolong, wc))
    loads = [pltpu.make_async_copy(a, b, here.at[k]) for k, (a, b) in enumerate(pairs)]
    for load in loads[:3]:
        load.start()
    barrier = pltpu.get_barrier_semaphore()
    for peer in everyone:
        pl.semaphore_signal(barrier, inc=1, device_id=peer, device_id_type=MESH)
    for load in loads[3:]:
        load.start()
    for load in loads[:3]:
        load.wait()
    for t in range(OWN):
        lay_metric(mt, BASE + t, gv, t)
    grads = [mt[pl.ds(BASE * MP + k, OWN, stride=MP), :] for k in range(4)]
    rate = wave_rate(dv[...], grads)
    top = jnp.max(jnp.max(rate, axis=0, keepdims=True), axis=1, keepdims=True)
    count = jnp.sum(bv[...].astype(f32), axis=0, keepdims=True)
    count = jnp.sum(count, axis=1, keepdims=True)
    half = lanes_of((1, 128)) < 64
    own = jnp.where(half, top, count)
    mine[0:1, :] = own

    def round_of(source, box, peers, sems, rems):
        return [
            pltpu.make_async_remote_copy(
                src_ref=source.at[pl.ds(0, 1)], dst_ref=box.at[pl.ds(d - 1, 1)],
                send_sem=sems.at[d - 1], recv_sem=rems.at[d - 1], device_id=peer, device_id_type=MESH)
            for d, peer in peers.items()
        ]

    round1 = round_of(mine, box1, peers1, send1, recv1)
    round2 = round_of(mine2, box2, peers2, send2, recv2)
    tail, head = pl.ds((OWN - HALO) * 128, WIDE), pl.ds(0, WIDE)
    copies = []
    for peer, wide, short, targets in (
        (right, tail, pl.ds(16, 16), (ls, lm, ld, lp, lr)),
        (left, head, pl.ds(0, 16), (rs, rm, rd, rp, rr)),
    ):
        sources = (state.at[:, :, wide], metric.at[:, wide], depth.at[short], partner.at[short], refine.at[short])
        for source, target in zip(sources, targets):
            k = len(copies)
            copies.append(pltpu.make_async_remote_copy(
                src_ref=source, dst_ref=target, send_sem=send.at[k], recv_sem=recv.at[k],
                device_id=peer, device_id_type=MESH))

    pl.semaphore_wait(barrier, len(everyone))
    for copy in round1 + copies:
        copy.start()

    for load in loads[3:]:
        load.wait()
    ends = (me == 0, me == total - 1)
    weights(wd, wt, wl, tmp, wf)
    for t in range(OWN):
        lay_state(qt, BASE + t, sv, t)
    cv[BASE : BASE + OWN, :] = GRAVITY * dv[...]
    pv[BASE : BASE + OWN, :] = av[...]

    def first_rate(g):
        m = 8 + 8 * g
        coefficients(m, mt, cv, pv, co)
        flux(m, qt, QP, state_row, mt, cv, pv, co, xt, 8 * (g % 2))
        product(m, 8 * (g % 2), xt, wl, r1)

    for g in (3, 4):
        first_rate(g)
    child_weights(wc, pw, tmp, wf)

    def earlier2(d):
        r, b = row - d // part, block - d % part
        r, b = jnp.where(r < 0, r + rows, r), jnp.where(b < 0, b + part, b)
        return r * part + b < row * part + block

    for copy in round1:
        copy.wait_recv()
    own, before1 = joined(own, box1, low - 1, lambda d: d <= lo)
    mine2[0:1, :] = own
    for copy in round2:
        copy.start()
    for copy in copies:
        copy.wait_recv()
    load_rims((ls, lm, ld, lp), (rs, rm, rd, rp), qt, mt, cv, pv, ends)
    mirror(qt, QP, state_row, mt, ends)
    for g in (2, 5, 6, 1, 0):
        first_rate(g)
    r1[64 * RP : 65 * RP, :] = r1[8 * RP : 9 * RP, :]
    mirror(r1, RP, result_row, mt, ends)
    for g in range(1, 7):
        m = 8 + 8 * g
        flux(m, r1, RP, result_row, mt, cv, pv, co, xt, 8 * (g % 2))
        product(m, 8 * (g % 2), xt, wl, r2)
    prefix(lr, bv, rr, rv, pk)
    tables(pk, pkw, tab)
    for copy in round1 + round2 + copies:
        copy.wait_send()
    for copy in round2:
        copy.wait_recv()
    own, before2 = joined(own, box2, deep - 1, earlier2)
    best = jnp.where(half, own, pltpu.roll(own, 64, 1))
    before = before1 + before2
    before = jnp.where(half, pltpu.roll(before, 64, 1), before)
    stat[0:1, :] = before - (me * (OWN * 64)).astype(f32)
    step = COURANT / best
    for g in range(1, 7):
        combine(8 + 8 * g, step, qt, r1, r2, st)


def wave_rate(depth, grads):
    gx, gy, hx, hy = grads
    lengths = [jnp.sqrt(vx * vx + vy * vy) for vx, vy in ((hx, hy), (gx + hx, gy + hy), (gx, gy))]
    return jnp.sqrt(GRAVITY * depth) * jnp.maximum(jnp.maximum(lengths[0], lengths[1]), lengths[2])


def lay_state(qt, m, s, t):
    for n in range(10):
        qt[m * QP + 4 * n : m * QP + 4 * n + 3, :] = s[n, :, t * 128 : (t + 1) * 128]


def lay_metric(mt, m, g, t):
    mt[m * MP : m * MP + 4, :] = g[:, t * 128 : (t + 1) * 128]


def load_rims(left, right, qt, mt, cv, pv, ends):
    ls, lm, ld, lp = left
    rs, rm, rd, rp = right

    def lay(m, s, g, t):
        lay_state(qt, m, s, t)
        lay_metric(mt, m, g, t)

    for t in range(HALO):
        lay(BASE - HALO + t, ls, lm, t)
        if t < HALO - 1:
            lay(BASE + OWN + t, rs, rm, t)
    lay(8, rs, rm, HALO - 1)
    lay(64, rs, rm, HALO - 1)
    lay(7, rs, rm, HALO - 2)
    for into, before, after, scale in ((cv, ld, rd, GRAVITY), (pv, lp, rp, 1)):
        into[BASE - HALO : BASE, :] = scale * before[16 - HALO : 16, :]
        into[BASE + OWN : BASE + OWN + 8, :] = scale * after[0:8, :]
        into[7:8, :] = scale * after[7:8, :]
        into[8:9, :] = scale * after[8:9, :]
        into[64:65, :] = scale * after[8:9, :]
    first, last = ends

    @pl.when(first)
    def _():
        cv[BASE - 1 : BASE, :] = pltpu.roll(cv[BASE : BASE + 1, :], 127, 1)

    @pl.when(last)
    def _():
        cv[BASE + OWN : BASE + OWN + 1, :] = pltpu.roll(cv[BASE + OWN - 1 : BASE + OWN, :], 1, 1)


def mirror(src, pitch, at, mt, ends):
    lane = lanes_of((1, 128))

    def row(tile, v):
        return src[tile * pitch + v : tile * pitch + v + 1, :]

    def grads(tile):
        return [mt[tile * MP + k : tile * MP + k + 1, :] for k in range(4)]

    def write(tile, rim, nodes, meet, gx, gy, shift, target):
        length = jnp.sqrt(gx * gx + gy * gy)
        nx, ny = gx / length, gy / length
        for j in range(4):
            eta, mx, my = (row(tile, at(f, nodes[j])) for f in range(3))
            normal = mx * nx + my * ny
            for f, value in enumerate((eta, mx - 2.0 * normal * nx, my - 2.0 * normal * ny)):
                v = at(f, meet[j])
                old = row(rim, v)
                src[rim * pitch + v : rim * pitch + v + 1, :] = jnp.where(
                    lane == target, pltpu.roll(value, shift, 1), old)

    first, last = ends

    @pl.when(first)
    def _():
        _, _, sx, sy = grads(BASE)
        write(BASE, BASE - 1, FACES[0], MEET[0], -sx, -sy, 127, 127)

    @pl.when(last)
    def _():
        rx, ry, sx, sy = grads(BASE + OWN - 1)
        write(BASE + OWN - 1, BASE + OWN, FACES[1], MEET[1], rx + sx, ry + sy, 1, 0)


def shifts(partner):
    lane = lanes_of((8, 128))
    j = lane + partner
    idx, inside = j & 127, (j >= 0) & (j < 128)

    def before(own, prv, nxt):
        return pltpu.roll(jnp.where(lane == 127, prv, own), 1, 1)

    def after(own, prv, nxt):
        return pltpu.roll(jnp.where(lane == 0, nxt, own), 127, 1)

    def across(own, prv, nxt):
        return jnp.where(inside, pick(own, idx), pick(jnp.where(lane < 64, nxt, prv), idx))

    return before, after, across


def coefficients(m, mt, cv, pv, co):
    rx, ry, sx, sy = (spread(mt, k, m, MP) for k in range(4))
    partner = pv[m : m + 8, :]
    three = [cv[m + s : m + s + 8, :] for s in (0, -1, 1)]
    c = three[0]
    outer = [move(*three) for move in shifts(partner)]
    outer[2] = jnp.where(partner == 0, c, outer[2])
    for k, (gx, gy) in enumerate(((sx, sy), (rx + sx, ry + sy), (rx, ry))):
        length = jnp.sqrt(gx * gx + gy * gy)
        co[k, m : m + 8, :] = outer[k]
        co[3 + k, m : m + 8, :] = length * jnp.sqrt(jnp.maximum(c, outer[k]))
        if k == 2:
            co[6, m : m + 8, :] = gx / length
            co[7, m : m + 8, :] = gy / length


def flux(m, src, pitch, at, mt, cv, pv, co, xt, slot):
    rx, ry, sx, sy = (spread(mt, k, m, MP) for k in range(4))
    c = cv[m : m + 8, :]
    partner = pv[m : m + 8, :]
    wall = partner == 0
    moves = shifts(partner)

    def value(f, n, step=0):
        return spread(src, at(f, n), m + step, pitch)

    def store(f, k, x):
        put(xt, f * 32 + k, slot, XS, x)

    crx, cry, csx, csy = -c * rx, -c * ry, -c * sx, -c * sy
    for n in range(10):
        eta, mx, my = (value(f, n) for f in range(3))
        store(0, n, -(rx * mx + ry * my))
        store(0, 10 + n, -(sx * mx + sy * my))
        store(1, n, crx * eta)
        store(1, 10 + n, csx * eta)
        store(2, n, cry * eta)
        store(2, 10 + n, csy * eta)
    vectors = ((-sx, -sy), (rx + sx, ry + sy), (-rx, -ry))
    for k in range(3):
        gx, gy = vectors[k]
        ce = co[k, m : m + 8, :]
        scale = co[3 + k, m : m + 8, :]
        for j in range(4):
            inner = [value(f, FACES[k][j]) for f in range(3)]
            outer = []
            for f in range(3):
                node = MEET[k][j]
                own = value(f, node)
                prv = value(f, node, -1) if k != 1 else None
                nxt = value(f, node, 1) if k != 0 else None
                outer.append(moves[k](own, prv, nxt))
            if k == 2:
                outer[0] = jnp.where(wall, inner[0], outer[0])
            d_eta, d_mx, d_my = (b - a for a, b in zip(inner, outer))
            if k == 2:
                nx, ny = co[6, m : m + 8, :], co[7, m : m + 8, :]
                twice = -2.0 * (inner[1] * nx + inner[2] * ny)
                d_mx = jnp.where(wall, twice * nx, d_mx)
                d_my = jnp.where(wall, twice * ny, d_my)
            drop = c * inner[0] - ce * outer[0]
            row = 20 + 4 * k + j
            store(0, row, scale * d_eta - gx * d_mx - gy * d_my)
            store(1, row, gx * drop + scale * d_mx)
            store(2, row, gy * drop + scale * d_my)


def product(m, slot, xt, wl, out):
    for pair in range(4):
        parts = []
        for t in (2 * pair, 2 * pair + 1):
            hi, lo = split(xt[(slot + t) * XS : (slot + t) * XS + XP, :])
            parts.append(jnp.concatenate([hi, lo], axis=0))
        both = jnp.concatenate(parts, axis=1)
        res = jnp.dot(wl[:, 0 : 2 * XP], both, preferred_element_type=f32)
        res = res[0:32] + res[32:64]
        tile = m + 2 * pair
        out[tile * RP : tile * RP + RR, :] = res[:, 0:128]
        out[(tile + 1) * RP : (tile + 1) * RP + RR, :] = res[:, 128:256]


def weights(diff_ops, lift, wl, tmp, wf):
    wf[...] = jnp.zeros_like(wf)
    base = jnp.zeros((16, 128), f32)
    for i, shift in ((0, 0), (1, 10), (2, 20)):
        tmp[...] = jnp.zeros_like(tmp)
        if i == 2:
            tmp[0:10, 0:12] = 0.5 * lift[...]
        else:
            for n in range(10):
                tmp[n : n + 1, 0:10] = diff_ops[n, i : i + 1, :]
        base = base + (tmp[...] if shift == 0 else pltpu.roll(tmp[...], shift, 1))
    for f in range(3):
        turned = base if f == 0 else pltpu.roll(base, 32 * f, 1)
        wf[f * 10 : f * 10 + 10, :] = turned[0:10]
    w = wf[0:32, :]
    hi = w.astype(bf16).astype(f32)
    low = w - hi
    turned = pltpu.roll(hi, XP, 1)
    lane = lanes_of((32, 128))
    wl[0:32, 0:128] = (hi + jnp.where(lane >= XP, turned, 0.0)).astype(bf16)
    wl[0:32, 128:256] = jnp.where(lane < 64, turned, 0.0).astype(bf16)
    wl[32:64, 0:128] = low.astype(bf16)
    wl[32:64, 128:256] = jnp.zeros((32, 128), bf16)


def child_weights(prolong, pw, tmp, wf):
    for i in range(3):
        wf[...] = jnp.zeros_like(wf)
        tmp[...] = jnp.zeros_like(tmp)
        if i == 0:
            eye = lax.broadcasted_iota(i32, (16, 128), 0) == lanes_of((16, 128))
            tmp[0:10, :] = jnp.where(eye, 1.0, 0.0)[0:10]
        else:
            for n in range(10):
                tmp[n : n + 1, 0:10] = prolong[n, i - 1 : i, :]
        for f in range(3):
            turned = tmp[...] if f == 0 else pltpu.roll(tmp[...], 10 * f, 1)
            wf[pl.ds(f, 10, stride=4), :] = turned[0:10]
        w = wf[...]
        hi = w.astype(bf16).astype(f32)
        low = w - hi
        pw[i * 48 : i * 48 + 48, :] = (hi + pltpu.roll(hi, 32, 1) + pltpu.roll(low, 64, 1)).astype(bf16)


def combine(m, step, qt, r1, r2, st):
    half = 0.5 * step * step
    for f in range(3):
        for n in range(10):
            v = f * 10 + n
            x = spread(qt, state_row(f, n), m, QP) + (step * spread(r1, v, m, RP) + half * spread(r2, v, m, RP))
            put(st, v, m - 16, RP, x)
    put(st, 30, m - 16, RP, jnp.zeros((8, 128), f32))
    put(st, 31, m - 16, RP, jnp.zeros((8, 128), f32))


def prefix(lr, refine, rr, rv, pk):
    rv[0:8, :] = lr[8:16, :]
    rv[8:40, :] = refine[...]
    rv[40:48, :] = rr[0:8, :]
    bits = rv[...]
    counts = (1 + bits).astype(f32)
    upper = lax.broadcasted_iota(i32, (128, 128), 0) <= lanes_of((128, 128))
    within = jnp.dot(counts.astype(bf16), upper.astype(f32).astype(bf16), preferred_element_type=f32)
    sums = jnp.broadcast_to(within[:, 127:128], (48, 128))
    lower = lanes_of((48, 48)) < lax.broadcasted_iota(i32, (48, 48), 0)
    before = jnp.dot(lower.astype(f32).astype(bf16), sums.astype(bf16), preferred_element_type=f32)
    ends = (within + before - before[8:9, :]).astype(i32)
    pk[...] = 2 * (ends - 1 - bits) + bits


def tables(pk, pkw, tab):
    row = lax.broadcasted_iota(i32, (48, 128), 0)
    ends = (pk[...] >> 1) + 1 + (pk[...] & 1)
    last = jnp.broadcast_to(ends[:, 127:128], (48, 128))
    reached = jnp.where(last <= lanes_of((48, 128)) * 128 - 1024, 1.0, 0.0)
    here = jnp.where(row == 0, 1.0, pltpu.roll(reached, 1, 0)) - reached
    after = jnp.where(row == 0, 0.0, pltpu.roll(here, 1, 0))
    shifted = pk[...] + 8192
    tiles = [(shifted >> 8), shifted & 255, row]
    tiles = jnp.concatenate([t.astype(f32).astype(bf16) for t in tiles], axis=1)
    for i, mark in enumerate((here, after)):
        found = jnp.dot(mark.T[0:64].astype(bf16), tiles, preferred_element_type=f32).astype(i32)
        pkw[i, :, :] = found[:, 0:128] * 256 + found[:, 128:256] - 8192
        if i == 0:
            pkw[2, :, :] = found[:, 256:384] * 128
    for g in range(8):
        rows = slice(8 * g, 8 * g + 8)
        p0, p1 = pkw[0, rows, :], pkw[1, rows, :]
        e0 = (p0 >> 1) + 1 + (p0 & 1)
        e1 = (p1 >> 1) + 1 + (p1 & 1)
        slot = (8 * g - 8 + lax.broadcasted_iota(i32, (8, 128), 0)) * 128 + lanes_of((8, 128))
        over = jnp.broadcast_to(e0[:, 127:128], (8, 128)) <= slot
        pos = jnp.zeros((8, 128), i32)
        for s in (64, 32, 16, 8, 4, 2, 1):
            probe = pos + (s - 1)
            e = jnp.where(over, pick(e1, probe), pick(e0, probe))
            pos = jnp.where(e <= slot, pos + s, pos)
        pos = jnp.minimum(pos, 127)
        got = jnp.where(over, pick(p1, pos), pick(p0, pos))
        which = slot - (got >> 1)
        parent = pkw[2, rows, :] + jnp.where(over, pos + 128, pos)
        tab[rows, :] = 4 * parent + jnp.where((got & 1) == 0, 0, 1 + which)


def aligned(offset, tab, near, code, lidx):
    near[0:8, :] = jnp.broadcast_to(1024 - offset.astype(i32), (8, 128))
    begin = near[0, 0]
    row, turn = jnp.clip(begin >> 7, 0, 16), begin & 127
    back = (128 - turn) & 127
    keep = lanes_of((8, 128)) >= turn
    for g in range(6):
        rows = slice(8 * g, 8 * g + 8)
        both = jnp.where(keep, tab[pl.ds(row + 8 * g, 8), :], tab[pl.ds(row + 8 * g + 1, 8), :])
        both = pltpu.roll(both, back, 1)
        tile = jnp.clip(jnp.broadcast_to(both[:, 0:1], (8, 128)) >> 9, 0, 47)
        lidx[rows, :] = (both >> 2) - tile * 128
        code[rows, :] = both & 3
        near[rows, :] = tile
    return [near[r, 0] for r in range(48)]


def place(tab, pw, stat, st, out, new_tiles, near, code, lidx, sems):
    tiles = aligned(stat[0:1, :], tab, near, code, lidx)
    weight = pw[:, 0:96]
    stores = []
    for pair in range(24):
        parts = []
        for r in (2 * pair, 2 * pair + 1):
            begin = tiles[r] * RP
            near_tile = st[pl.ds(begin, RR), :]
            far_tile = st[pl.ds(begin + RP, RR), :]
            idx = jnp.broadcast_to(lidx[r : r + 1, :], (RR, 128))
            low = idx & 127
            s = jnp.where(idx < 128, pick(near_tile, low), pick(far_tile, low))
            hi, lo = split(s)
            parts.append(jnp.concatenate([hi, lo, hi], axis=0))
        res = jnp.dot(weight, jnp.concatenate(parts, axis=1), preferred_element_type=f32)
        for i in range(2):
            r = 2 * pair + i
            one = res[:, 128 * i : 128 * i + 128]
            kind = jnp.broadcast_to(code[r : r + 1, :], (48, 128))
            new = jnp.where(kind == 0, one[0:48], jnp.where(kind == 1, one[48:96], one[96:144]))
            for n in range(10):
                new_tiles[n, :, r * 128 : (r + 1) * 128] = new[4 * n : 4 * n + 3]
        if pair in (7, 15, 20, 23):
            k = len(stores)
            begin = (0, 8, 16, 21)[k]
            part = pl.ds(begin * 256, (pair + 1 - begin) * 256)
            store = pltpu.make_async_copy(new_tiles.at[:, :, part], out.at[:, :, part], sems.at[k])
            store.start()
            stores.append(store)
    for store in stores:
        store.wait()


def solution(mesh):
    rows, cols = mesh.shape["row"], mesh.shape["col"]
    total = rows * cols
    low = min(16, cols // 2)
    high = total // low
    placed = OWN + OWN // 2

    def shards(state, depth, metric, partner, refine, diff_ops, lift, prolong):
        depth, partner, refine = (a.reshape(OWN, 128) for a in (depth, partner, refine))
        state, diff_ops, prolong = (a.transpose(1, 0, 2) for a in (state, diff_ops, prolong))
        args = (state, metric, depth, partner, refine, diff_ops, lift, prolong)
        vm, hbm = pl.BlockSpec(memory_space=pltpu.VMEM), pl.BlockSpec(memory_space=pl.ANY)
        side = [
            pltpu.VMEM((10, 3, WIDE), f32),
            pltpu.VMEM((4, WIDE), f32),
            pltpu.VMEM((16, 128), f32),
            pltpu.VMEM((16, 128), i32),
            pltpu.VMEM((16, 128), i32),
        ]
        st, tab, pw, stat = pl.pallas_call(
            functools.partial(advance, rows, cols, low),
            out_shape=[
                pltpu.VMEM((((placed + 1) * RP + 7) // 8 * 8, 128), f32),
                pltpu.VMEM((72, 128), i32),
                pltpu.VMEM((144, 128), bf16),
                pltpu.VMEM((8, 128), f32),
            ],
            in_specs=[hbm] * 8,
            out_specs=[vm] * 4,
            scratch_shapes=[pltpu.VMEM(a.shape, a.dtype) for a in args]
            + side
            + side
            + [
                pltpu.VMEM((MEM * QP, 128), f32),
                pltpu.VMEM((MEM * MP, 128), f32),
                pltpu.VMEM((MEM, 128), f32),
                pltpu.VMEM((MEM, 128), i32),
                pltpu.VMEM((8, MEM, 128), f32),
                pltpu.VMEM((16 * XS, 128), f32),
                pltpu.VMEM((MEM * RP, 128), f32),
                pltpu.VMEM((MEM * RP, 128), f32),
                pltpu.VMEM((64, 256), bf16),
                pltpu.VMEM((16, 128), f32),
                pltpu.VMEM((48, 128), f32),
                pltpu.VMEM((48, 128), i32),
                pltpu.VMEM((48, 128), i32),
                pltpu.VMEM((3, 64, 128), i32),
                pltpu.VMEM((8, 128), f32),
                pltpu.VMEM((low, 128), f32),
                pltpu.VMEM((8, 128), f32),
                pltpu.VMEM((high, 128), f32),
                pltpu.SemaphoreType.DMA((8,)),
                pltpu.SemaphoreType.DMA((10,)),
                pltpu.SemaphoreType.DMA((10,)),
                pltpu.SemaphoreType.DMA((low - 1,)),
                pltpu.SemaphoreType.DMA((low - 1,)),
                pltpu.SemaphoreType.DMA((high - 1,)),
                pltpu.SemaphoreType.DMA((high - 1,)),
            ],
            compiler_params=pltpu.CompilerParams(collective_id=0, has_side_effects=True),
            name="advance",
        )(*args)
        new = pl.pallas_call(
            place,
            out_shape=jax.ShapeDtypeStruct((10, 3, placed * 128), f32),
            in_specs=[vm] * 4,
            out_specs=hbm,
            scratch_shapes=[
                pltpu.VMEM((10, 3, placed * 128), f32),
                pltpu.VMEM((48, 128), i32),
                pltpu.VMEM((48, 128), i32),
                pltpu.VMEM((48, 128), i32),
                pltpu.SemaphoreType.DMA((4,)),
            ],
            name="place",
        )(*(pltpu.with_memory_space_constraint(a, pltpu.VMEM) for a in (tab, pw, stat, st)))
        return new.transpose(1, 0, 2)

    halves = ("row", "col")
    return jax.shard_map(
        shards,
        mesh=mesh,
        in_specs=(P(None, None, halves), P(halves), P(None, halves), P(halves), P(halves), P(), P(), P()),
        out_specs=P(None, None, halves),
        check_vma=False,
    )
```

```python
import functools

import jax
import jax.numpy as jnp
from jax import lax
from jax.experimental import pallas as pl
from jax.experimental.pallas import tpu as pltpu
from jax.sharding import PartitionSpec as P

GRAVITY = 9.81
COURANT = 0.5
MESH = pl.DeviceIdType.MESH

OWN = 32
HALO = 9
WIDE = HALO * 128
BASE = 2
RING = BASE + OWN + 2 * HALO
MEM = 64
QP = 41
RR = 32
RP = 33
MP = 9
XP = 96
XS = 97

FACES = ((0, 1, 2, 3), (3, 6, 8, 9), (9, 7, 4, 0))
MEET = ((9, 8, 6, 3), (3, 2, 1, 0), (0, 4, 7, 9))

f32 = jnp.float32
bf16 = jnp.bfloat16
i32 = jnp.int32


def lanes_of(shape):
    return lax.broadcasted_iota(i32, shape, len(shape) - 1)


def state_row(f, n):
    return 4 * n + f


def result_row(f, n):
    return 10 * f + n


def spread(ref, v, tile, pitch):
    return ref[pl.ds(tile * pitch + v, 8, stride=pitch), :]


def put(ref, v, tile, pitch, value):
    ref[pl.ds(tile * pitch + v, 8, stride=pitch), :] = value


def pick(x, idx):
    return jnp.take_along_axis(x, idx, axis=1, mode="promise_in_bounds")


def split(x):
    hi = x.astype(bf16)
    return hi, (x - hi.astype(f32)).astype(bf16)


def joined(own, box, members, earlier):
    part = box[0:members, :]
    best = jnp.maximum(own, jnp.max(part, axis=0, keepdims=True))
    both = own + jnp.sum(part, axis=0, keepdims=True)
    d = lax.broadcasted_iota(i32, part.shape, 0) + 1
    before = jnp.sum(jnp.where(earlier(d), part, 0.0), axis=0, keepdims=True)
    return jnp.where(lanes_of((1, 128)) < 64, best, both), before


def advance(
    rows, cols, low,
    state, metric, depth, partner, refine, diff_ops, lift, prolong,
    st, tab, pw, stat,
    sv, gv, dv, av, bv, wd, wt, wc,
    ls, lm, ld, lp, lr, rs, rm, rd, rp, rr,
    qt, mt, cv, pv, co, xt, r1, r2, wl, tmp, wf, rv, pk, pkw,
    mine, box1, mine2, box2,
    here, send, recv, send1, recv1, send2, recv2,
):
    total = rows * cols
    part, deep = cols // low, rows * (cols // low)
    row, col = lax.axis_index("row"), lax.axis_index("col")
    me = row * cols + col
    block, lo = col // low, lax.rem(col, low)

    def wrapped(x, n):
        return jnp.where(x >= n, x - n, x)

    def hops(d, n):
        return min(d, n - d)

    over = wrapped(col + 1, cols)
    under = wrapped(col + cols - 1, cols)
    right = (jnp.where(over == 0, wrapped(row + 1, rows), row), over)
    left = (jnp.where(col == 0, wrapped(row + rows - 1, rows), row), under)
    close = sorted(range(1, low), key=lambda d: -hops(d // 2, low // 2))
    peers1 = {d: (row, block * low + wrapped(lo + d, low)) for d in close}
    row_at = [wrapped(row + d, rows) for d in range(rows)]
    col_at = [wrapped(block + d, part) * low + lo for d in range(part)]
    far = sorted(range(1, deep), key=lambda d: -hops(d // part, rows) - hops(d % part, part))
    peers2 = {d: (row_at[d // part], col_at[d % part]) for d in far}
    everyone = [peers1[d] for d in close] + [peers2[d] for d in far] + [left, right]

    pairs = (
        (metric, gv), (depth, dv), (refine, bv), (state, sv), (partner, av), (diff_ops, wd), (lift, wt), (prolong, wc))
    loads = [pltpu.make_async_copy(a, b, here.at[k]) for k, (a, b) in enumerate(pairs)]
    for load in loads[:3]:
        load.start()
    barrier = pltpu.get_barrier_semaphore()
    for peer in everyone:
        pl.semaphore_signal(barrier, inc=1, device_id=peer, device_id_type=MESH)
    for load in loads[3:]:
        load.start()
    for load in loads[:3]:
        load.wait()
    for t in range(OWN):
        lay_metric(mt, BASE + t, gv, t)
    grads = [mt[pl.ds(BASE * MP + k, OWN, stride=MP), :] for k in range(4)]
    rate = wave_rate(dv[...], grads)
    top = jnp.max(jnp.max(rate, axis=0, keepdims=True), axis=1, keepdims=True)
    count = jnp.sum(bv[...].astype(f32), axis=0, keepdims=True)
    count = jnp.sum(count, axis=1, keepdims=True)
    half = lanes_of((1, 128)) < 64
    own = jnp.where(half, top, count)
    mine[0:1, :] = own

    def round_of(source, box, peers, sems, rems):
        return [
            pltpu.make_async_remote_copy(
                src_ref=source.at[pl.ds(0, 1)], dst_ref=box.at[pl.ds(d - 1, 1)],
                send_sem=sems.at[d - 1], recv_sem=rems.at[d - 1], device_id=peer, device_id_type=MESH)
            for d, peer in peers.items()
        ]

    round1 = round_of(mine, box1, peers1, send1, recv1)
    round2 = round_of(mine2, box2, peers2, send2, recv2)
    tail, head = pl.ds((OWN - HALO) * 128, WIDE), pl.ds(0, WIDE)
    copies = []
    for peer, wide, short, targets in (
        (right, tail, pl.ds(16, 16), (ls, lm, ld, lp, lr)),
        (left, head, pl.ds(0, 16), (rs, rm, rd, rp, rr)),
    ):
        sources = (state.at[:, :, wide], metric.at[:, wide], depth.at[short], partner.at[short], refine.at[short])
        for source, target in zip(sources, targets):
            k = len(copies)
            copies.append(pltpu.make_async_remote_copy(
                src_ref=source, dst_ref=target, send_sem=send.at[k], recv_sem=recv.at[k],
                device_id=peer, device_id_type=MESH))

    pl.semaphore_wait(barrier, len(everyone))
    for copy in round1 + copies:
        copy.start()

    for load in loads[3:]:
        load.wait()
    ends = (me == 0, me == total - 1)
    weights(wd, wt, wl, tmp, wf)
    for t in range(OWN):
        lay_state(qt, BASE + t, sv, t)
    cv[BASE : BASE + OWN, :] = GRAVITY * dv[...]
    pv[BASE : BASE + OWN, :] = av[...]
    for t in range(4):
        lay_state(qt, RING + t, sv, t)
        lay_metric(mt, RING + t, gv, t)
    cv[RING : RING + 4, :] = GRAVITY * dv[0:4, :]
    pv[RING : RING + 4, :] = av[0:4, :]

    def first_rates(tiles):
        for i, m in enumerate(tiles):
            coefficients(m, mt, cv, pv, co)
            flux(m, qt, QP, state_row, mt, cv, pv, co, xt, 8 * (i % 2))
            product(m, 8 * (i % 2), xt, wl, r1)

    def second_rates(tiles):
        for i, m in enumerate(tiles):
            flux(m, r1, RP, result_row, mt, cv, pv, co, xt, 8 * (i % 2))
            product(m, 8 * (i % 2), xt, wl, r2)

    first_rates((BASE + 1, BASE + 9, BASE + 17, BASE + 23))
    second_rates((BASE + 2, BASE + 10, BASE + 18, BASE + 22))
    child_weights(wc, pw, tmp, wf)

    def earlier2(d):
        r, b = row - d // part, block - d % part
        r, b = jnp.where(r < 0, r + rows, r), jnp.where(b < 0, b + part, b)
        return r * part + b < row * part + block

    for copy in round1:
        copy.wait_recv()
    own, before1 = joined(own, box1, low - 1, lambda d: d <= lo)
    mine2[0:1, :] = own
    for copy in round2:
        copy.start()
    for copy in copies:
        copy.wait_recv()
    load_rims((ls, lm, ld, lp), (rs, rm, rd, rp), qt, mt, cv, pv, ends)
    mirror(qt, QP, state_row, mt, ends)
    first_rates((BASE + 30, BASE + 38, BASE + 46))
    mirror(r1, RP, result_row, mt, ends)
    second_rates((BASE + 30, BASE + 38, BASE + 44))
    r1[BASE * RP : BASE * RP + RR, :] = r1[RING * RP : RING * RP + RR, :]
    for t in range(2):
        r2[(BASE + t) * RP : (BASE + t) * RP + RR, :] = r2[(RING + t) * RP : (RING + t) * RP + RR, :]
    prefix(lr, bv, rr, rv, pk)
    tables(pk, pkw, tab)
    for copy in round1 + round2 + copies:
        copy.wait_send()
    for copy in round2:
        copy.wait_recv()
    own, before2 = joined(own, box2, deep - 1, earlier2)
    best = jnp.where(half, own, pltpu.roll(own, 64, 1))
    before = before1 + before2
    before = jnp.where(half, pltpu.roll(before, 64, 1), before)
    stat[0:1, :] = before - (me * (OWN * 64)).astype(f32)
    step = COURANT / best
    combine(RING - 8, 0, step, qt, r1, r2, st)
    for g in range(5):
        combine(BASE + 8 * g, 8 + 8 * g, step, qt, r1, r2, st)


def wave_rate(depth, grads):
    gx, gy, hx, hy = grads
    lengths = [jnp.sqrt(vx * vx + vy * vy) for vx, vy in ((hx, hy), (gx + hx, gy + hy), (gx, gy))]
    return jnp.sqrt(GRAVITY * depth) * jnp.maximum(jnp.maximum(lengths[0], lengths[1]), lengths[2])


def lay_state(qt, m, s, t):
    for n in range(10):
        qt[m * QP + 4 * n : m * QP + 4 * n + 3, :] = s[n, :, t * 128 : (t + 1) * 128]


def lay_metric(mt, m, g, t):
    mt[m * MP : m * MP + 4, :] = g[:, t * 128 : (t + 1) * 128]


def load_rims(left, right, qt, mt, cv, pv, ends):
    ls, lm, ld, lp = left
    rs, rm, rd, rp = right

    def lay(m, s, g, t):
        lay_state(qt, m, s, t)
        lay_metric(mt, m, g, t)

    for t in range(HALO):
        lay(RING - HALO + t, ls, lm, t)
        lay(BASE + OWN + t, rs, rm, t)
    for into, before, after, scale in ((cv, ld, rd, GRAVITY), (pv, lp, rp, 1)):
        into[RING - HALO : RING, :] = scale * before[16 - HALO : 16, :]
        into[BASE + OWN : BASE + OWN + HALO, :] = scale * after[0:HALO, :]
    first, last = ends

    @pl.when(first)
    def _():
        cv[RING - 1 : RING, :] = pltpu.roll(cv[RING : RING + 1, :], 127, 1)

    @pl.when(last)
    def _():
        cv[BASE + OWN : BASE + OWN + 1, :] = pltpu.roll(cv[BASE + OWN - 1 : BASE + OWN, :], 1, 1)


def mirror(src, pitch, at, mt, ends):
    lane = lanes_of((1, 128))

    def row(tile, v):
        return src[tile * pitch + v : tile * pitch + v + 1, :]

    def grads(tile):
        return [mt[tile * MP + k : tile * MP + k + 1, :] for k in range(4)]

    def write(tile, rim, nodes, meet, gx, gy, shift, target):
        length = jnp.sqrt(gx * gx + gy * gy)
        nx, ny = gx / length, gy / length
        for j in range(4):
            eta, mx, my = (row(tile, at(f, nodes[j])) for f in range(3))
            normal = mx * nx + my * ny
            for f, value in enumerate((eta, mx - 2.0 * normal * nx, my - 2.0 * normal * ny)):
                v = at(f, meet[j])
                old = row(rim, v)
                src[rim * pitch + v : rim * pitch + v + 1, :] = jnp.where(
                    lane == target, pltpu.roll(value, shift, 1), old)

    first, last = ends

    @pl.when(first)
    def _():
        _, _, sx, sy = grads(RING)
        write(RING, RING - 1, FACES[0], MEET[0], -sx, -sy, 127, 127)

    @pl.when(last)
    def _():
        rx, ry, sx, sy = grads(BASE + OWN - 1)
        write(BASE + OWN - 1, BASE + OWN, FACES[1], MEET[1], rx + sx, ry + sy, 1, 0)


def shifts(partner):
    lane = lanes_of((8, 128))
    j = lane + partner
    idx, inside = j & 127, (j >= 0) & (j < 128)

    def before(own, prv, nxt):
        return pltpu.roll(jnp.where(lane == 127, prv, own), 1, 1)

    def after(own, prv, nxt):
        return pltpu.roll(jnp.where(lane == 0, nxt, own), 127, 1)

    def across(own, prv, nxt):
        return jnp.where(inside, pick(own, idx), pick(jnp.where(lane < 64, nxt, prv), idx))

    return before, after, across


def coefficients(m, mt, cv, pv, co):
    rx, ry, sx, sy = (spread(mt, k, m, MP) for k in range(4))
    partner = pv[m : m + 8, :]
    three = [cv[m + s : m + s + 8, :] for s in (0, -1, 1)]
    c = three[0]
    outer = [move(*three) for move in shifts(partner)]
    outer[2] = jnp.where(partner == 0, c, outer[2])
    for k, (gx, gy) in enumerate(((sx, sy), (rx + sx, ry + sy), (rx, ry))):
        length = jnp.sqrt(gx * gx + gy * gy)
        co[k, m : m + 8, :] = outer[k]
        co[3 + k, m : m + 8, :] = length * jnp.sqrt(jnp.maximum(c, outer[k]))
        if k == 2:
            co[6, m : m + 8, :] = gx / length
            co[7, m : m + 8, :] = gy / length


def flux(m, src, pitch, at, mt, cv, pv, co, xt, slot):
    rx, ry, sx, sy = (spread(mt, k, m, MP) for k in range(4))
    c = cv[m : m + 8, :]
    partner = pv[m : m + 8, :]
    wall = partner == 0
    moves = shifts(partner)

    def value(f, n, step=0):
        return spread(src, at(f, n), m + step, pitch)

    def store(f, k, x):
        put(xt, f * 32 + k, slot, XS, x)

    crx, cry, csx, csy = -c * rx, -c * ry, -c * sx, -c * sy
    for n in range(10):
        eta, mx, my = (value(f, n) for f in range(3))
        store(0, n, -(rx * mx + ry * my))
        store(0, 10 + n, -(sx * mx + sy * my))
        store(1, n, crx * eta)
        store(1, 10 + n, csx * eta)
        store(2, n, cry * eta)
        store(2, 10 + n, csy * eta)
    vectors = ((-sx, -sy), (rx + sx, ry + sy), (-rx, -ry))
    for k in range(3):
        gx, gy = vectors[k]
        ce = co[k, m : m + 8, :]
        scale = co[3 + k, m : m + 8, :]
        for j in range(4):
            inner = [value(f, FACES[k][j]) for f in range(3)]
            outer = []
            for f in range(3):
                node = MEET[k][j]
                own = value(f, node)
                prv = value(f, node, -1) if k != 1 else None
                nxt = value(f, node, 1) if k != 0 else None
                outer.append(moves[k](own, prv, nxt))
            if k == 2:
                outer[0] = jnp.where(wall, inner[0], outer[0])
            d_eta, d_mx, d_my = (b - a for a, b in zip(inner, outer))
            if k == 2:
                nx, ny = co[6, m : m + 8, :], co[7, m : m + 8, :]
                twice = -2.0 * (inner[1] * nx + inner[2] * ny)
                d_mx = jnp.where(wall, twice * nx, d_mx)
                d_my = jnp.where(wall, twice * ny, d_my)
            drop = c * inner[0] - ce * outer[0]
            row = 20 + 4 * k + j
            store(0, row, scale * d_eta - gx * d_mx - gy * d_my)
            store(1, row, gx * drop + scale * d_mx)
            store(2, row, gy * drop + scale * d_my)


def product(m, slot, xt, wl, out):
    for pair in range(4):
        parts = []
        for t in (2 * pair, 2 * pair + 1):
            hi, lo = split(xt[(slot + t) * XS : (slot + t) * XS + XP, :])
            parts.append(jnp.concatenate([hi, lo], axis=0))
        both = jnp.concatenate(parts, axis=1)
        res = jnp.dot(wl[:, 0 : 2 * XP], both, preferred_element_type=f32)
        res = res[0:32] + res[32:64]
        tile = m + 2 * pair
        out[tile * RP : tile * RP + RR, :] = res[:, 0:128]
        out[(tile + 1) * RP : (tile + 1) * RP + RR, :] = res[:, 128:256]


def weights(diff_ops, lift, wl, tmp, wf):
    wf[...] = jnp.zeros_like(wf)
    base = jnp.zeros((16, 128), f32)
    for i, shift in ((0, 0), (1, 10), (2, 20)):
        tmp[...] = jnp.zeros_like(tmp)
        if i == 2:
            tmp[0:10, 0:12] = 0.5 * lift[...]
        else:
            for n in range(10):
                tmp[n : n + 1, 0:10] = diff_ops[n, i : i + 1, :]
        base = base + (tmp[...] if shift == 0 else pltpu.roll(tmp[...], shift, 1))
    for f in range(3):
        turned = base if f == 0 else pltpu.roll(base, 32 * f, 1)
        wf[f * 10 : f * 10 + 10, :] = turned[0:10]
    w = wf[0:32, :]
    hi = w.astype(bf16).astype(f32)
    low = w - hi
    turned = pltpu.roll(hi, XP, 1)
    lane = lanes_of((32, 128))
    wl[0:32, 0:128] = (hi + jnp.where(lane >= XP, turned, 0.0)).astype(bf16)
    wl[0:32, 128:256] = jnp.where(lane < 64, turned, 0.0).astype(bf16)
    wl[32:64, 0:128] = low.astype(bf16)
    wl[32:64, 128:256] = jnp.zeros((32, 128), bf16)


def child_weights(prolong, pw, tmp, wf):
    for i in range(3):
        wf[...] = jnp.zeros_like(wf)
        tmp[...] = jnp.zeros_like(tmp)
        if i == 0:
            eye = lax.broadcasted_iota(i32, (16, 128), 0) == lanes_of((16, 128))
            tmp[0:10, :] = jnp.where(eye, 1.0, 0.0)[0:10]
        else:
            for n in range(10):
                tmp[n : n + 1, 0:10] = prolong[n, i - 1 : i, :]
        for f in range(3):
            turned = tmp[...] if f == 0 else pltpu.roll(tmp[...], 10 * f, 1)
            wf[pl.ds(f, 10, stride=4), :] = turned[0:10]
        w = wf[...]
        hi = w.astype(bf16).astype(f32)
        low = w - hi
        pw[i * 48 : i * 48 + 48, :] = (hi + pltpu.roll(hi, 32, 1) + pltpu.roll(low, 64, 1)).astype(bf16)


def combine(m, to, step, qt, r1, r2, st):
    half = 0.5 * step * step
    for f in range(3):
        for n in range(10):
            v = f * 10 + n
            x = spread(qt, state_row(f, n), m, QP) + (step * spread(r1, v, m, RP) + half * spread(r2, v, m, RP))
            put(st, v, to, RP, x)
    put(st, 30, to, RP, jnp.zeros((8, 128), f32))
    put(st, 31, to, RP, jnp.zeros((8, 128), f32))


def prefix(lr, refine, rr, rv, pk):
    rv[0:8, :] = lr[8:16, :]
    rv[8:40, :] = refine[...]
    rv[40:48, :] = rr[0:8, :]
    bits = rv[...]
    counts = (1 + bits).astype(f32)
    upper = lax.broadcasted_iota(i32, (128, 128), 0) <= lanes_of((128, 128))
    within = jnp.dot(counts.astype(bf16), upper.astype(f32).astype(bf16), preferred_element_type=f32)
    sums = jnp.broadcast_to(within[:, 127:128], (48, 128))
    lower = lanes_of((48, 48)) < lax.broadcasted_iota(i32, (48, 48), 0)
    before = jnp.dot(lower.astype(f32).astype(bf16), sums.astype(bf16), preferred_element_type=f32)
    ends = (within + before - before[8:9, :]).astype(i32)
    pk[...] = 2 * (ends - 1 - bits) + bits


def tables(pk, pkw, tab):
    row = lax.broadcasted_iota(i32, (48, 128), 0)
    ends = (pk[...] >> 1) + 1 + (pk[...] & 1)
    last = jnp.broadcast_to(ends[:, 127:128], (48, 128))
    reached = jnp.where(last <= lanes_of((48, 128)) * 128 - 1024, 1.0, 0.0)
    here = jnp.where(row == 0, 1.0, pltpu.roll(reached, 1, 0)) - reached
    after = jnp.where(row == 0, 0.0, pltpu.roll(here, 1, 0))
    shifted = pk[...] + 8192
    tiles = [(shifted >> 8), shifted & 255, row]
    tiles = jnp.concatenate([t.astype(f32).astype(bf16) for t in tiles], axis=1)
    for i, mark in enumerate((here, after)):
        found = jnp.dot(mark.T[0:64].astype(bf16), tiles, preferred_element_type=f32).astype(i32)
        pkw[i, :, :] = found[:, 0:128] * 256 + found[:, 128:256] - 8192
        if i == 0:
            pkw[2, :, :] = found[:, 256:384] * 128
    for g in range(8):
        rows = slice(8 * g, 8 * g + 8)
        p0, p1 = pkw[0, rows, :], pkw[1, rows, :]
        e0 = (p0 >> 1) + 1 + (p0 & 1)
        e1 = (p1 >> 1) + 1 + (p1 & 1)
        slot = (8 * g - 8 + lax.broadcasted_iota(i32, (8, 128), 0)) * 128 + lanes_of((8, 128))
        over = jnp.broadcast_to(e0[:, 127:128], (8, 128)) <= slot
        pos = jnp.zeros((8, 128), i32)
        for s in (64, 32, 16, 8, 4, 2, 1):
            probe = pos + (s - 1)
            e = jnp.where(over, pick(e1, probe), pick(e0, probe))
            pos = jnp.where(e <= slot, pos + s, pos)
        pos = jnp.minimum(pos, 127)
        got = jnp.where(over, pick(p1, pos), pick(p0, pos))
        which = slot - (got >> 1)
        parent = pkw[2, rows, :] + jnp.where(over, pos + 128, pos)
        tab[rows, :] = 4 * parent + jnp.where((got & 1) == 0, 0, 1 + which)


def aligned(offset, tab, near, code, lidx):
    near[0:8, :] = jnp.broadcast_to(1024 - offset.astype(i32), (8, 128))
    begin = near[0, 0]
    row, turn = jnp.clip(begin >> 7, 0, 16), begin & 127
    back = (128 - turn) & 127
    keep = lanes_of((8, 128)) >= turn
    for g in range(6):
        rows = slice(8 * g, 8 * g + 8)
        both = jnp.where(keep, tab[pl.ds(row + 8 * g, 8), :], tab[pl.ds(row + 8 * g + 1, 8), :])
        both = pltpu.roll(both, back, 1)
        tile = jnp.clip(jnp.broadcast_to(both[:, 0:1], (8, 128)) >> 9, 0, 47)
        lidx[rows, :] = (both >> 2) - tile * 128
        code[rows, :] = both & 3
        near[rows, :] = tile
    return [near[r, 0] for r in range(48)]


def place(tab, pw, stat, st, out, new_tiles, near, code, lidx, sems):
    tiles = aligned(stat[0:1, :], tab, near, code, lidx)
    weight = pw[:, 0:96]
    stores = []
    for pair in range(24):
        parts = []
        for r in (2 * pair, 2 * pair + 1):
            begin = tiles[r] * RP
            near_tile = st[pl.ds(begin, RR), :]
            far_tile = st[pl.ds(begin + RP, RR), :]
            idx = jnp.broadcast_to(lidx[r : r + 1, :], (RR, 128))
            low = idx & 127
            s = jnp.where(idx < 128, pick(near_tile, low), pick(far_tile, low))
            hi, lo = split(s)
            parts.append(jnp.concatenate([hi, lo, hi], axis=0))
        res = jnp.dot(weight, jnp.concatenate(parts, axis=1), preferred_element_type=f32)
        for i in range(2):
            r = 2 * pair + i
            one = res[:, 128 * i : 128 * i + 128]
            kind = jnp.broadcast_to(code[r : r + 1, :], (48, 128))
            new = jnp.where(kind == 0, one[0:48], jnp.where(kind == 1, one[48:96], one[96:144]))
            for n in range(10):
                new_tiles[n, :, r * 128 : (r + 1) * 128] = new[4 * n : 4 * n + 3]
        if pair in (7, 15, 20, 23):
            k = len(stores)
            begin = (0, 8, 16, 21)[k]
            part = pl.ds(begin * 256, (pair + 1 - begin) * 256)
            store = pltpu.make_async_copy(new_tiles.at[:, :, part], out.at[:, :, part], sems.at[k])
            store.start()
            stores.append(store)
    for store in stores:
        store.wait()


def solution(mesh):
    rows, cols = mesh.shape["row"], mesh.shape["col"]
    total = rows * cols
    low = min(16, cols // 2)
    high = total // low
    placed = OWN + OWN // 2

    def shards(state, depth, metric, partner, refine, diff_ops, lift, prolong):
        depth, partner, refine = (a.reshape(OWN, 128) for a in (depth, partner, refine))
        state, diff_ops, prolong = (a.transpose(1, 0, 2) for a in (state, diff_ops, prolong))
        args = (state, metric, depth, partner, refine, diff_ops, lift, prolong)
        vm, hbm = pl.BlockSpec(memory_space=pltpu.VMEM), pl.BlockSpec(memory_space=pl.ANY)
        side = [
            pltpu.VMEM((10, 3, WIDE), f32),
            pltpu.VMEM((4, WIDE), f32),
            pltpu.VMEM((16, 128), f32),
            pltpu.VMEM((16, 128), i32),
            pltpu.VMEM((16, 128), i32),
        ]
        st, tab, pw, stat = pl.pallas_call(
            functools.partial(advance, rows, cols, low),
            out_shape=[
                pltpu.VMEM((((placed + 1) * RP + 7) // 8 * 8, 128), f32),
                pltpu.VMEM((72, 128), i32),
                pltpu.VMEM((144, 128), bf16),
                pltpu.VMEM((8, 128), f32),
            ],
            in_specs=[hbm] * 8,
            out_specs=[vm] * 4,
            scratch_shapes=[pltpu.VMEM(a.shape, a.dtype) for a in args]
            + side
            + side
            + [
                pltpu.VMEM((MEM * QP, 128), f32),
                pltpu.VMEM((MEM * MP, 128), f32),
                pltpu.VMEM((MEM, 128), f32),
                pltpu.VMEM((MEM, 128), i32),
                pltpu.VMEM((8, MEM, 128), f32),
                pltpu.VMEM((16 * XS, 128), f32),
                pltpu.VMEM((MEM * RP, 128), f32),
                pltpu.VMEM((MEM * RP, 128), f32),
                pltpu.VMEM((64, 256), bf16),
                pltpu.VMEM((16, 128), f32),
                pltpu.VMEM((48, 128), f32),
                pltpu.VMEM((48, 128), i32),
                pltpu.VMEM((48, 128), i32),
                pltpu.VMEM((3, 64, 128), i32),
                pltpu.VMEM((8, 128), f32),
                pltpu.VMEM((low, 128), f32),
                pltpu.VMEM((8, 128), f32),
                pltpu.VMEM((high, 128), f32),
                pltpu.SemaphoreType.DMA((8,)),
                pltpu.SemaphoreType.DMA((10,)),
                pltpu.SemaphoreType.DMA((10,)),
                pltpu.SemaphoreType.DMA((low - 1,)),
                pltpu.SemaphoreType.DMA((low - 1,)),
                pltpu.SemaphoreType.DMA((high - 1,)),
                pltpu.SemaphoreType.DMA((high - 1,)),
            ],
            compiler_params=pltpu.CompilerParams(collective_id=0, has_side_effects=True),
            name="advance",
        )(*args)
        new = pl.pallas_call(
            place,
            out_shape=jax.ShapeDtypeStruct((10, 3, placed * 128), f32),
            in_specs=[vm] * 4,
            out_specs=hbm,
            scratch_shapes=[
                pltpu.VMEM((10, 3, placed * 128), f32),
                pltpu.VMEM((48, 128), i32),
                pltpu.VMEM((48, 128), i32),
                pltpu.VMEM((48, 128), i32),
                pltpu.SemaphoreType.DMA((4,)),
            ],
            name="place",
        )(*(pltpu.with_memory_space_constraint(a, pltpu.VMEM) for a in (tab, pw, stat, st)))
        return new.transpose(1, 0, 2)

    halves = ("row", "col")
    return jax.shard_map(
        shards,
        mesh=mesh,
        in_specs=(P(None, None, halves), P(halves), P(None, halves), P(halves), P(halves), P(), P(), P()),
        out_specs=P(None, None, halves),
        check_vma=False,
    )
```

```python
import functools

import jax
import jax.numpy as jnp
from jax import lax
from jax.experimental import pallas as pl
from jax.experimental.pallas import tpu as pltpu
from jax.sharding import PartitionSpec as P

GRAVITY = 9.81
COURANT = 0.5
MESH = pl.DeviceIdType.MESH

OWN = 32
HALO = 9
WIDE = HALO * 128
BASE = 2
RING = BASE + OWN + 2 * HALO
MEM = 64
QP = 41
RR = 32
RP = 33
MP = 9
XP = 96
XS = 97

FACES = ((0, 1, 2, 3), (3, 6, 8, 9), (9, 7, 4, 0))
MEET = ((9, 8, 6, 3), (3, 2, 1, 0), (0, 4, 7, 9))

f32 = jnp.float32
bf16 = jnp.bfloat16
i32 = jnp.int32


def lanes_of(shape):
    return lax.broadcasted_iota(i32, shape, len(shape) - 1)


def state_row(f, n):
    return 4 * n + f


def result_row(f, n):
    return 10 * f + n


def spread(ref, v, tile, pitch):
    return ref[pl.ds(tile * pitch + v, 8, stride=pitch), :]


def put(ref, v, tile, pitch, value):
    ref[pl.ds(tile * pitch + v, 8, stride=pitch), :] = value


def pick(x, idx):
    return jnp.take_along_axis(x, idx, axis=1, mode="promise_in_bounds")


def split(x):
    hi = x.astype(bf16)
    return hi, (x - hi.astype(f32)).astype(bf16)


def joined(own, box, members, earlier):
    part = box[0:members, :]
    best = jnp.maximum(own, jnp.max(part, axis=0, keepdims=True))
    both = own + jnp.sum(part, axis=0, keepdims=True)
    d = lax.broadcasted_iota(i32, part.shape, 0) + 1
    before = jnp.sum(jnp.where(earlier(d), part, 0.0), axis=0, keepdims=True)
    return jnp.where(lanes_of((1, 128)) < 64, best, both), before


def advance(
    rows, cols, low,
    state, metric, depth, partner, refine, diff_ops, lift, prolong,
    st, tab, pw, stat,
    sv, gv, dv, av, bv, wd, wt, wc,
    ls, lm, ld, lp, lr, rs, rm, rd, rp, rr,
    qt, mt, cv, pv, co, xt, r1, r2, wl, tmp, wf, rv, pk, pkw,
    mine, box1, mine2, box2,
    here, send, recv, send1, recv1, send2, recv2,
):
    total = rows * cols
    part, deep = cols // low, rows * (cols // low)
    row, col = lax.axis_index("row"), lax.axis_index("col")
    me = row * cols + col
    block, lo = col // low, lax.rem(col, low)

    def wrapped(x, n):
        return jnp.where(x >= n, x - n, x)

    def hops(d, n):
        return min(d, n - d)

    over = wrapped(col + 1, cols)
    under = wrapped(col + cols - 1, cols)
    right = (jnp.where(over == 0, wrapped(row + 1, rows), row), over)
    left = (jnp.where(col == 0, wrapped(row + rows - 1, rows), row), under)
    has_left, has_right = me != 0, me != total - 1
    close = sorted(range(1, low), key=lambda d: -hops(d // 2, low // 2))
    peers1 = {d: (row, block * low + wrapped(lo + d, low)) for d in close}
    row_at = [wrapped(row + d, rows) for d in range(rows)]
    col_at = [wrapped(block + d, part) * low + lo for d in range(part)]
    far = sorted(range(1, deep), key=lambda d: -hops(d // part, rows) - hops(d % part, part))
    peers2 = {d: (row_at[d // part], col_at[d % part]) for d in far}
    everyone = [peers1[d] for d in close] + [peers2[d] for d in far]

    pairs = (
        (metric, gv), (depth, dv), (refine, bv), (state, sv), (partner, av), (diff_ops, wd), (lift, wt), (prolong, wc))
    loads = [pltpu.make_async_copy(a, b, here.at[k]) for k, (a, b) in enumerate(pairs)]
    for load in loads[:3]:
        load.start()
    barrier = pltpu.get_barrier_semaphore()
    for peer in everyone:
        pl.semaphore_signal(barrier, inc=1, device_id=peer, device_id_type=MESH)

    @pl.when(has_left)
    def _():
        pl.semaphore_signal(barrier, inc=1, device_id=left, device_id_type=MESH)

    @pl.when(has_right)
    def _():
        pl.semaphore_signal(barrier, inc=1, device_id=right, device_id_type=MESH)

    for load in loads[3:]:
        load.start()
    for load in loads[:3]:
        load.wait()
    for t in range(OWN):
        lay_metric(mt, BASE + t, gv, t)
    grads = [mt[pl.ds(BASE * MP + k, OWN, stride=MP), :] for k in range(4)]
    rate = wave_rate(dv[...], grads)
    top = jnp.max(jnp.max(rate, axis=0, keepdims=True), axis=1, keepdims=True)
    count = jnp.sum(bv[...].astype(f32), axis=0, keepdims=True)
    count = jnp.sum(count, axis=1, keepdims=True)
    half = lanes_of((1, 128)) < 64
    own = jnp.where(half, top, count)
    mine[0:1, :] = own

    def round_of(source, box, peers, sems, rems):
        return [
            pltpu.make_async_remote_copy(
                src_ref=source.at[pl.ds(0, 1)], dst_ref=box.at[pl.ds(d - 1, 1)],
                send_sem=sems.at[d - 1], recv_sem=rems.at[d - 1], device_id=peer, device_id_type=MESH)
            for d, peer in peers.items()
        ]

    round1 = round_of(mine, box1, peers1, send1, recv1)
    round2 = round_of(mine2, box2, peers2, send2, recv2)
    tail, head = pl.ds((OWN - HALO) * 128, WIDE), pl.ds(0, WIDE)
    copies = []
    for peer, wide, short, targets in (
        (right, tail, pl.ds(16, 16), (ls, lm, ld, lp, lr)),
        (left, head, pl.ds(0, 16), (rs, rm, rd, rp, rr)),
    ):
        sources = (state.at[:, :, wide], metric.at[:, wide], depth.at[short], partner.at[short], refine.at[short])
        for source, target in zip(sources, targets):
            k = len(copies)
            copies.append(pltpu.make_async_remote_copy(
                src_ref=source, dst_ref=target, send_sem=send.at[k], recv_sem=recv.at[k],
                device_id=peer, device_id_type=MESH))

    onward, back = copies[:5], copies[5:]

    def each(batch, act):
        for copy in batch:
            act(copy)

    pl.semaphore_wait(barrier, len(everyone) + has_left.astype(i32) + has_right.astype(i32))
    for copy in round1:
        copy.start()
    pl.when(has_right)(lambda: each(onward, lambda copy: copy.start()))
    pl.when(has_left)(lambda: each(back, lambda copy: copy.start()))

    for load in loads[3:]:
        load.wait()
    ends = (me == 0, me == total - 1)
    weights(wd, wt, wl, tmp, wf)
    for t in range(OWN):
        lay_state(qt, BASE + t, sv, t)
    cv[BASE : BASE + OWN, :] = GRAVITY * dv[...]
    pv[BASE : BASE + OWN, :] = av[...]
    for t in range(4):
        lay_state(qt, RING + t, sv, t)
        lay_metric(mt, RING + t, gv, t)
    cv[RING : RING + 4, :] = GRAVITY * dv[0:4, :]
    pv[RING : RING + 4, :] = av[0:4, :]

    def first_rates(tiles):
        for i, m in enumerate(tiles):
            coefficients(m, mt, cv, pv, co)
            flux(m, qt, QP, state_row, mt, cv, pv, co, xt, 8 * (i % 2))
            product(m, 8 * (i % 2), xt, wl, r1)

    def second_rates(tiles):
        for i, m in enumerate(tiles):
            flux(m, r1, RP, result_row, mt, cv, pv, co, xt, 8 * (i % 2))
            product(m, 8 * (i % 2), xt, wl, r2)

    first_rates((BASE + 1, BASE + 9, BASE + 17, BASE + 23))
    second_rates((BASE + 2, BASE + 10, BASE + 18, BASE + 22))
    child_weights(wc, pw, tmp, wf)

    def earlier2(d):
        r, b = row - d // part, block - d % part
        r, b = jnp.where(r < 0, r + rows, r), jnp.where(b < 0, b + part, b)
        return r * part + b < row * part + block

    for copy in round1:
        copy.wait_recv()
    own, before1 = joined(own, box1, low - 1, lambda d: d <= lo)
    mine2[0:1, :] = own
    for copy in round2:
        copy.start()
    pl.when(has_left)(lambda: each(onward, lambda copy: copy.wait_recv()))
    pl.when(has_right)(lambda: each(back, lambda copy: copy.wait_recv()))

    @pl.when(~has_left)
    def _():
        lr[...] = jnp.zeros_like(lr)

    @pl.when(~has_right)
    def _():
        rr[...] = jnp.zeros_like(rr)

    load_rims((ls, lm, ld, lp), (rs, rm, rd, rp), qt, mt, cv, pv, ends)
    mirror(qt, QP, state_row, mt, ends)
    first_rates((BASE + 30, BASE + 38, BASE + 46))
    mirror(r1, RP, result_row, mt, ends)
    second_rates((BASE + 30, BASE + 38, BASE + 44))
    r1[BASE * RP : BASE * RP + RR, :] = r1[RING * RP : RING * RP + RR, :]
    for t in range(2):
        r2[(BASE + t) * RP : (BASE + t) * RP + RR, :] = r2[(RING + t) * RP : (RING + t) * RP + RR, :]
    prefix(lr, bv, rr, rv, pk)
    tables(pk, pkw, tab)
    for copy in round1 + round2:
        copy.wait_send()
    pl.when(has_right)(lambda: each(onward, lambda copy: copy.wait_send()))
    pl.when(has_left)(lambda: each(back, lambda copy: copy.wait_send()))
    for copy in round2:
        copy.wait_recv()
    own, before2 = joined(own, box2, deep - 1, earlier2)
    best = jnp.where(half, own, pltpu.roll(own, 64, 1))
    before = before1 + before2
    before = jnp.where(half, pltpu.roll(before, 64, 1), before)
    stat[0:1, :] = before - (me * (OWN * 64)).astype(f32)
    step = COURANT / best
    combine(RING - 8, 0, step, qt, r1, r2, st)
    for g in range(5):
        combine(BASE + 8 * g, 8 + 8 * g, step, qt, r1, r2, st)


def wave_rate(depth, grads):
    gx, gy, hx, hy = grads
    lengths = [jnp.sqrt(vx * vx + vy * vy) for vx, vy in ((hx, hy), (gx + hx, gy + hy), (gx, gy))]
    return jnp.sqrt(GRAVITY * depth) * jnp.maximum(jnp.maximum(lengths[0], lengths[1]), lengths[2])


def lay_state(qt, m, s, t):
    for n in range(10):
        qt[m * QP + 4 * n : m * QP + 4 * n + 3, :] = s[n, :, t * 128 : (t + 1) * 128]


def lay_metric(mt, m, g, t):
    mt[m * MP : m * MP + 4, :] = g[:, t * 128 : (t + 1) * 128]


def load_rims(left, right, qt, mt, cv, pv, ends):
    ls, lm, ld, lp = left
    rs, rm, rd, rp = right

    def lay(m, s, g, t):
        lay_state(qt, m, s, t)
        lay_metric(mt, m, g, t)

    for t in range(HALO):
        lay(RING - HALO + t, ls, lm, t)
        lay(BASE + OWN + t, rs, rm, t)
    for into, before, after, scale in ((cv, ld, rd, GRAVITY), (pv, lp, rp, 1)):
        into[RING - HALO : RING, :] = scale * before[16 - HALO : 16, :]
        into[BASE + OWN : BASE + OWN + HALO, :] = scale * after[0:HALO, :]
    first, last = ends

    @pl.when(first)
    def _():
        cv[RING - 1 : RING, :] = pltpu.roll(cv[RING : RING + 1, :], 127, 1)

    @pl.when(last)
    def _():
        cv[BASE + OWN : BASE + OWN + 1, :] = pltpu.roll(cv[BASE + OWN - 1 : BASE + OWN, :], 1, 1)


def mirror(src, pitch, at, mt, ends):
    lane = lanes_of((1, 128))

    def row(tile, v):
        return src[tile * pitch + v : tile * pitch + v + 1, :]

    def grads(tile):
        return [mt[tile * MP + k : tile * MP + k + 1, :] for k in range(4)]

    def write(tile, rim, nodes, meet, gx, gy, shift, target):
        length = jnp.sqrt(gx * gx + gy * gy)
        nx, ny = gx / length, gy / length
        for j in range(4):
            eta, mx, my = (row(tile, at(f, nodes[j])) for f in range(3))
            normal = mx * nx + my * ny
            for f, value in enumerate((eta, mx - 2.0 * normal * nx, my - 2.0 * normal * ny)):
                v = at(f, meet[j])
                old = row(rim, v)
                src[rim * pitch + v : rim * pitch + v + 1, :] = jnp.where(
                    lane == target, pltpu.roll(value, shift, 1), old)

    first, last = ends

    @pl.when(first)
    def _():
        _, _, sx, sy = grads(RING)
        write(RING, RING - 1, FACES[0], MEET[0], -sx, -sy, 127, 127)

    @pl.when(last)
    def _():
        rx, ry, sx, sy = grads(BASE + OWN - 1)
        write(BASE + OWN - 1, BASE + OWN, FACES[1], MEET[1], rx + sx, ry + sy, 1, 0)


def shifts(partner):
    lane = lanes_of((8, 128))
    j = lane + partner
    idx, inside = j & 127, (j >= 0) & (j < 128)

    def before(own, prv, nxt):
        return pltpu.roll(jnp.where(lane == 127, prv, own), 1, 1)

    def after(own, prv, nxt):
        return pltpu.roll(jnp.where(lane == 0, nxt, own), 127, 1)

    def across(own, prv, nxt):
        return jnp.where(inside, pick(own, idx), pick(jnp.where(lane < 64, nxt, prv), idx))

    return before, after, across


def coefficients(m, mt, cv, pv, co):
    rx, ry, sx, sy = (spread(mt, k, m, MP) for k in range(4))
    partner = pv[m : m + 8, :]
    three = [cv[m + s : m + s + 8, :] for s in (0, -1, 1)]
    c = three[0]
    outer = [move(*three) for move in shifts(partner)]
    outer[2] = jnp.where(partner == 0, c, outer[2])
    for k, (gx, gy) in enumerate(((sx, sy), (rx + sx, ry + sy), (rx, ry))):
        length = jnp.sqrt(gx * gx + gy * gy)
        co[k, m : m + 8, :] = outer[k]
        co[3 + k, m : m + 8, :] = length * jnp.sqrt(jnp.maximum(c, outer[k]))
        if k == 2:
            co[6, m : m + 8, :] = gx / length
            co[7, m : m + 8, :] = gy / length


def flux(m, src, pitch, at, mt, cv, pv, co, xt, slot):
    rx, ry, sx, sy = (spread(mt, k, m, MP) for k in range(4))
    c = cv[m : m + 8, :]
    partner = pv[m : m + 8, :]
    wall = partner == 0
    moves = shifts(partner)

    def value(f, n, step=0):
        return spread(src, at(f, n), m + step, pitch)

    def store(f, k, x):
        put(xt, f * 32 + k, slot, XS, x)

    crx, cry, csx, csy = -c * rx, -c * ry, -c * sx, -c * sy
    for n in range(10):
        eta, mx, my = (value(f, n) for f in range(3))
        store(0, n, -(rx * mx + ry * my))
        store(0, 10 + n, -(sx * mx + sy * my))
        store(1, n, crx * eta)
        store(1, 10 + n, csx * eta)
        store(2, n, cry * eta)
        store(2, 10 + n, csy * eta)
    vectors = ((-sx, -sy), (rx + sx, ry + sy), (-rx, -ry))
    for k in range(3):
        gx, gy = vectors[k]
        ce = co[k, m : m + 8, :]
        scale = co[3 + k, m : m + 8, :]
        for j in range(4):
            inner = [value(f, FACES[k][j]) for f in range(3)]
            outer = []
            for f in range(3):
                node = MEET[k][j]
                own = value(f, node)
                prv = value(f, node, -1) if k != 1 else None
                nxt = value(f, node, 1) if k != 0 else None
                outer.append(moves[k](own, prv, nxt))
            if k == 2:
                outer[0] = jnp.where(wall, inner[0], outer[0])
            d_eta, d_mx, d_my = (b - a for a, b in zip(inner, outer))
            if k == 2:
                nx, ny = co[6, m : m + 8, :], co[7, m : m + 8, :]
                twice = -2.0 * (inner[1] * nx + inner[2] * ny)
                d_mx = jnp.where(wall, twice * nx, d_mx)
                d_my = jnp.where(wall, twice * ny, d_my)
            drop = c * inner[0] - ce * outer[0]
            row = 20 + 4 * k + j
            store(0, row, scale * d_eta - gx * d_mx - gy * d_my)
            store(1, row, gx * drop + scale * d_mx)
            store(2, row, gy * drop + scale * d_my)


def product(m, slot, xt, wl, out):
    for pair in range(4):
        parts = []
        for t in (2 * pair, 2 * pair + 1):
            hi, lo = split(xt[(slot + t) * XS : (slot + t) * XS + XP, :])
            parts.append(jnp.concatenate([hi, lo], axis=0))
        both = jnp.concatenate(parts, axis=1)
        res = jnp.dot(wl[:, 0 : 2 * XP], both, preferred_element_type=f32)
        res = res[0:32] + res[32:64]
        tile = m + 2 * pair
        out[tile * RP : tile * RP + RR, :] = res[:, 0:128]
        out[(tile + 1) * RP : (tile + 1) * RP + RR, :] = res[:, 128:256]


def weights(diff_ops, lift, wl, tmp, wf):
    wf[...] = jnp.zeros_like(wf)
    base = jnp.zeros((16, 128), f32)
    for i, shift in ((0, 0), (1, 10), (2, 20)):
        tmp[...] = jnp.zeros_like(tmp)
        if i == 2:
            tmp[0:10, 0:12] = 0.5 * lift[...]
        else:
            for n in range(10):
                tmp[n : n + 1, 0:10] = diff_ops[n, i : i + 1, :]
        base = base + (tmp[...] if shift == 0 else pltpu.roll(tmp[...], shift, 1))
    for f in range(3):
        turned = base if f == 0 else pltpu.roll(base, 32 * f, 1)
        wf[f * 10 : f * 10 + 10, :] = turned[0:10]
    w = wf[0:32, :]
    hi = w.astype(bf16).astype(f32)
    low = w - hi
    turned = pltpu.roll(hi, XP, 1)
    lane = lanes_of((32, 128))
    wl[0:32, 0:128] = (hi + jnp.where(lane >= XP, turned, 0.0)).astype(bf16)
    wl[0:32, 128:256] = jnp.where(lane < 64, turned, 0.0).astype(bf16)
    wl[32:64, 0:128] = low.astype(bf16)
    wl[32:64, 128:256] = jnp.zeros((32, 128), bf16)


def child_weights(prolong, pw, tmp, wf):
    for i in range(3):
        wf[...] = jnp.zeros_like(wf)
        tmp[...] = jnp.zeros_like(tmp)
        if i == 0:
            eye = lax.broadcasted_iota(i32, (16, 128), 0) == lanes_of((16, 128))
            tmp[0:10, :] = jnp.where(eye, 1.0, 0.0)[0:10]
        else:
            for n in range(10):
                tmp[n : n + 1, 0:10] = prolong[n, i - 1 : i, :]
        for f in range(3):
            turned = tmp[...] if f == 0 else pltpu.roll(tmp[...], 10 * f, 1)
            wf[pl.ds(f, 10, stride=4), :] = turned[0:10]
        w = wf[...]
        hi = w.astype(bf16).astype(f32)
        low = w - hi
        pw[i * 48 : i * 48 + 48, :] = (hi + pltpu.roll(hi, 32, 1) + pltpu.roll(low, 64, 1)).astype(bf16)


def combine(m, to, step, qt, r1, r2, st):
    half = 0.5 * step * step
    for f in range(3):
        for n in range(10):
            v = f * 10 + n
            x = spread(qt, state_row(f, n), m, QP) + (step * spread(r1, v, m, RP) + half * spread(r2, v, m, RP))
            put(st, v, to, RP, x)
    put(st, 30, to, RP, jnp.zeros((8, 128), f32))
    put(st, 31, to, RP, jnp.zeros((8, 128), f32))


def prefix(lr, refine, rr, rv, pk):
    rv[0:8, :] = lr[8:16, :]
    rv[8:40, :] = refine[...]
    rv[40:48, :] = rr[0:8, :]
    bits = rv[...]
    counts = (1 + bits).astype(f32)
    upper = lax.broadcasted_iota(i32, (128, 128), 0) <= lanes_of((128, 128))
    within = jnp.dot(counts.astype(bf16), upper.astype(f32).astype(bf16), preferred_element_type=f32)
    sums = jnp.broadcast_to(within[:, 127:128], (48, 128))
    lower = lanes_of((48, 48)) < lax.broadcasted_iota(i32, (48, 48), 0)
    before = jnp.dot(lower.astype(f32).astype(bf16), sums.astype(bf16), preferred_element_type=f32)
    ends = (within + before - before[8:9, :]).astype(i32)
    pk[...] = 2 * (ends - 1 - bits) + bits


def tables(pk, pkw, tab):
    row = lax.broadcasted_iota(i32, (48, 128), 0)
    ends = (pk[...] >> 1) + 1 + (pk[...] & 1)
    last = jnp.broadcast_to(ends[:, 127:128], (48, 128))
    reached = jnp.where(last <= lanes_of((48, 128)) * 128 - 1024, 1.0, 0.0)
    here = jnp.where(row == 0, 1.0, pltpu.roll(reached, 1, 0)) - reached
    after = jnp.where(row == 0, 0.0, pltpu.roll(here, 1, 0))
    shifted = pk[...] + 8192
    tiles = [(shifted >> 8), shifted & 255, row]
    tiles = jnp.concatenate([t.astype(f32).astype(bf16) for t in tiles], axis=1)
    for i, mark in enumerate((here, after)):
        found = jnp.dot(mark.T[0:64].astype(bf16), tiles, preferred_element_type=f32).astype(i32)
        pkw[i, :, :] = found[:, 0:128] * 256 + found[:, 128:256] - 8192
        if i == 0:
            pkw[2, :, :] = found[:, 256:384] * 128
    for g in range(8):
        rows = slice(8 * g, 8 * g + 8)
        p0, p1 = pkw[0, rows, :], pkw[1, rows, :]
        e0 = (p0 >> 1) + 1 + (p0 & 1)
        e1 = (p1 >> 1) + 1 + (p1 & 1)
        slot = (8 * g - 8 + lax.broadcasted_iota(i32, (8, 128), 0)) * 128 + lanes_of((8, 128))
        over = jnp.broadcast_to(e0[:, 127:128], (8, 128)) <= slot
        pos = jnp.zeros((8, 128), i32)
        for s in (64, 32, 16, 8, 4, 2, 1):
            probe = pos + (s - 1)
            e = jnp.where(over, pick(e1, probe), pick(e0, probe))
            pos = jnp.where(e <= slot, pos + s, pos)
        pos = jnp.minimum(pos, 127)
        got = jnp.where(over, pick(p1, pos), pick(p0, pos))
        which = slot - (got >> 1)
        parent = pkw[2, rows, :] + jnp.where(over, pos + 128, pos)
        tab[rows, :] = 4 * parent + jnp.where((got & 1) == 0, 0, 1 + which)


def aligned(offset, tab, near, code, lidx):
    near[0:8, :] = jnp.broadcast_to(1024 - offset.astype(i32), (8, 128))
    begin = near[0, 0]
    row, turn = jnp.clip(begin >> 7, 0, 16), begin & 127
    back = (128 - turn) & 127
    keep = lanes_of((8, 128)) >= turn
    for g in range(6):
        rows = slice(8 * g, 8 * g + 8)
        both = jnp.where(keep, tab[pl.ds(row + 8 * g, 8), :], tab[pl.ds(row + 8 * g + 1, 8), :])
        both = pltpu.roll(both, back, 1)
        tile = jnp.clip(jnp.broadcast_to(both[:, 0:1], (8, 128)) >> 9, 0, 47)
        lidx[rows, :] = (both >> 2) - tile * 128
        code[rows, :] = both & 3
        near[rows, :] = tile
    return [near[r, 0] for r in range(48)]


def place(tab, pw, stat, st, out, new_tiles, near, code, lidx, sems):
    tiles = aligned(stat[0:1, :], tab, near, code, lidx)
    weight = pw[:, 0:96]
    stores = []
    for pair in range(24):
        parts = []
        for r in (2 * pair, 2 * pair + 1):
            begin = tiles[r] * RP
            near_tile = st[pl.ds(begin, RR), :]
            far_tile = st[pl.ds(begin + RP, RR), :]
            idx = jnp.broadcast_to(lidx[r : r + 1, :], (RR, 128))
            low = idx & 127
            s = jnp.where(idx < 128, pick(near_tile, low), pick(far_tile, low))
            hi, lo = split(s)
            parts.append(jnp.concatenate([hi, lo, hi], axis=0))
        res = jnp.dot(weight, jnp.concatenate(parts, axis=1), preferred_element_type=f32)
        for i in range(2):
            r = 2 * pair + i
            one = res[:, 128 * i : 128 * i + 128]
            kind = jnp.broadcast_to(code[r : r + 1, :], (48, 128))
            new = jnp.where(kind == 0, one[0:48], jnp.where(kind == 1, one[48:96], one[96:144]))
            for n in range(10):
                new_tiles[n, :, r * 128 : (r + 1) * 128] = new[4 * n : 4 * n + 3]
        if pair in (7, 15, 20, 23):
            k = len(stores)
            begin = (0, 8, 16, 21)[k]
            part = pl.ds(begin * 256, (pair + 1 - begin) * 256)
            store = pltpu.make_async_copy(new_tiles.at[:, :, part], out.at[:, :, part], sems.at[k])
            store.start()
            stores.append(store)
    for store in stores:
        store.wait()


def solution(mesh):
    rows, cols = mesh.shape["row"], mesh.shape["col"]
    total = rows * cols
    low = min(16, cols // 2)
    high = total // low
    placed = OWN + OWN // 2

    def shards(state, depth, metric, partner, refine, diff_ops, lift, prolong):
        depth, partner, refine = (a.reshape(OWN, 128) for a in (depth, partner, refine))
        state, diff_ops, prolong = (a.transpose(1, 0, 2) for a in (state, diff_ops, prolong))
        args = (state, metric, depth, partner, refine, diff_ops, lift, prolong)
        vm, hbm = pl.BlockSpec(memory_space=pltpu.VMEM), pl.BlockSpec(memory_space=pl.ANY)
        side = [
            pltpu.VMEM((10, 3, WIDE), f32),
            pltpu.VMEM((4, WIDE), f32),
            pltpu.VMEM((16, 128), f32),
            pltpu.VMEM((16, 128), i32),
            pltpu.VMEM((16, 128), i32),
        ]
        st, tab, pw, stat = pl.pallas_call(
            functools.partial(advance, rows, cols, low),
            out_shape=[
                pltpu.VMEM((((placed + 1) * RP + 7) // 8 * 8, 128), f32),
                pltpu.VMEM((72, 128), i32),
                pltpu.VMEM((144, 128), bf16),
                pltpu.VMEM((8, 128), f32),
            ],
            in_specs=[hbm] * 8,
            out_specs=[vm] * 4,
            scratch_shapes=[pltpu.VMEM(a.shape, a.dtype) for a in args]
            + side
            + side
            + [
                pltpu.VMEM((MEM * QP, 128), f32),
                pltpu.VMEM((MEM * MP, 128), f32),
                pltpu.VMEM((MEM, 128), f32),
                pltpu.VMEM((MEM, 128), i32),
                pltpu.VMEM((8, MEM, 128), f32),
                pltpu.VMEM((16 * XS, 128), f32),
                pltpu.VMEM((MEM * RP, 128), f32),
                pltpu.VMEM((MEM * RP, 128), f32),
                pltpu.VMEM((64, 256), bf16),
                pltpu.VMEM((16, 128), f32),
                pltpu.VMEM((48, 128), f32),
                pltpu.VMEM((48, 128), i32),
                pltpu.VMEM((48, 128), i32),
                pltpu.VMEM((3, 64, 128), i32),
                pltpu.VMEM((8, 128), f32),
                pltpu.VMEM((low, 128), f32),
                pltpu.VMEM((8, 128), f32),
                pltpu.VMEM((high, 128), f32),
                pltpu.SemaphoreType.DMA((8,)),
                pltpu.SemaphoreType.DMA((10,)),
                pltpu.SemaphoreType.DMA((10,)),
                pltpu.SemaphoreType.DMA((low - 1,)),
                pltpu.SemaphoreType.DMA((low - 1,)),
                pltpu.SemaphoreType.DMA((high - 1,)),
                pltpu.SemaphoreType.DMA((high - 1,)),
            ],
            compiler_params=pltpu.CompilerParams(collective_id=0, has_side_effects=True),
            name="advance",
        )(*args)
        new = pl.pallas_call(
            place,
            out_shape=jax.ShapeDtypeStruct((10, 3, placed * 128), f32),
            in_specs=[vm] * 4,
            out_specs=hbm,
            scratch_shapes=[
                pltpu.VMEM((10, 3, placed * 128), f32),
                pltpu.VMEM((48, 128), i32),
                pltpu.VMEM((48, 128), i32),
                pltpu.VMEM((48, 128), i32),
                pltpu.SemaphoreType.DMA((4,)),
            ],
            name="place",
        )(*(pltpu.with_memory_space_constraint(a, pltpu.VMEM) for a in (tab, pw, stat, st)))
        return new.transpose(1, 0, 2)

    halves = ("row", "col")
    return jax.shard_map(
        shards,
        mesh=mesh,
        in_specs=(P(None, None, halves), P(halves), P(None, halves), P(halves), P(halves), P(), P(), P()),
        out_specs=P(None, None, halves),
        check_vma=False,
    )
```

```python
import functools

import jax
import jax.numpy as jnp
from jax import lax
from jax.experimental import pallas as pl
from jax.experimental.pallas import tpu as pltpu
from jax.sharding import PartitionSpec as P

GRAVITY = 9.81
COURANT = 0.5
MESH = pl.DeviceIdType.MESH

OWN = 32
HALO = 9
WIDE = HALO * 128
BASE = 2
RING = BASE + OWN + 2 * HALO
MEM = 64
QP = 41
RR = 32
RP = 33
MP = 9
XP = 96
XS = 97

FACES = ((0, 1, 2, 3), (3, 6, 8, 9), (9, 7, 4, 0))
MEET = ((9, 8, 6, 3), (3, 2, 1, 0), (0, 4, 7, 9))

f32 = jnp.float32
bf16 = jnp.bfloat16
i32 = jnp.int32


def lanes_of(shape):
    return lax.broadcasted_iota(i32, shape, len(shape) - 1)


def state_row(f, n):
    return 4 * n + f


def result_row(f, n):
    return 10 * f + n


def spread(ref, v, tile, pitch):
    return ref[pl.ds(tile * pitch + v, 8, stride=pitch), :]


def put(ref, v, tile, pitch, value):
    ref[pl.ds(tile * pitch + v, 8, stride=pitch), :] = value


def pick(x, idx):
    return jnp.take_along_axis(x, idx, axis=1, mode="promise_in_bounds")


def split(x):
    hi = x.astype(bf16)
    return hi, (x - hi.astype(f32)).astype(bf16)


def joined(own, box, members, earlier):
    part = box[0:members, :]
    best = jnp.maximum(own, jnp.max(part, axis=0, keepdims=True))
    both = own + jnp.sum(part, axis=0, keepdims=True)
    d = lax.broadcasted_iota(i32, part.shape, 0) + 1
    before = jnp.sum(jnp.where(earlier(d), part, 0.0), axis=0, keepdims=True)
    return jnp.where(lanes_of((1, 128)) < 64, best, both), before


def advance(
    rows, cols, low,
    state, metric, depth, partner, refine, diff_ops, lift, prolong,
    st, tab, pw, stat,
    sv, gv, dv, av, bv, wd, wt, wc,
    ls, lm, ld, lp, lr, rs, rm, rd, rp, rr,
    qt, mt, cv, pv, co, xt, r1, r2, wl, tmp, wf, rv, pk, pkw,
    mine, box1, mine2, box2,
    here, send, recv, send1, recv1, send2, recv2,
):
    total = rows * cols
    part, deep = cols // low, rows * (cols // low)
    row, col = lax.axis_index("row"), lax.axis_index("col")
    me = row * cols + col
    block, lo = col // low, lax.rem(col, low)

    def wrapped(x, n):
        return jnp.where(x >= n, x - n, x)

    def hops(d, n):
        return min(d, n - d)

    over = wrapped(col + 1, cols)
    under = wrapped(col + cols - 1, cols)
    right = (jnp.where(over == 0, wrapped(row + 1, rows), row), over)
    left = (jnp.where(col == 0, wrapped(row + rows - 1, rows), row), under)
    has_left, has_right = me != 0, me != total - 1
    close = sorted(range(1, low), key=lambda d: -hops(d // 2, low // 2))
    peers1 = {d: (row, block * low + wrapped(lo + d, low)) for d in close}
    row_at = [wrapped(row + d, rows) for d in range(rows)]
    col_at = [wrapped(block + d, part) * low + lo for d in range(part)]
    far = sorted(range(1, deep), key=lambda d: -hops(d // part, rows) - hops(d % part, part))
    peers2 = {d: (row_at[d // part], col_at[d % part]) for d in far}
    everyone = [peers1[d] for d in close] + [peers2[d] for d in far]

    pairs = (
        (metric, gv), (depth, dv), (refine, bv), (state, sv), (partner, av), (diff_ops, wd), (lift, wt), (prolong, wc))
    loads = [pltpu.make_async_copy(a, b, here.at[k]) for k, (a, b) in enumerate(pairs)]
    for load in loads[:3]:
        load.start()
    barrier = pltpu.get_barrier_semaphore()
    for peer in everyone:
        pl.semaphore_signal(barrier, inc=1, device_id=peer, device_id_type=MESH)

    @pl.when(has_left)
    def _():
        pl.semaphore_signal(barrier, inc=1, device_id=left, device_id_type=MESH)

    @pl.when(has_right)
    def _():
        pl.semaphore_signal(barrier, inc=1, device_id=right, device_id_type=MESH)

    for load in loads[3:]:
        load.start()
    for load in loads[:3]:
        load.wait()
    for t in range(OWN):
        lay_metric(mt, BASE + t, gv, t)
    grads = [mt[pl.ds(BASE * MP + k, OWN, stride=MP), :] for k in range(4)]
    rate = wave_rate(dv[...], grads)
    top = jnp.max(jnp.max(rate, axis=0, keepdims=True), axis=1, keepdims=True)
    count = jnp.sum(bv[...].astype(f32), axis=0, keepdims=True)
    count = jnp.sum(count, axis=1, keepdims=True)
    half = lanes_of((1, 128)) < 64
    own = jnp.where(half, top, count)
    mine[0:1, :] = own

    def round_of(source, box, peers, sems, rems):
        return [
            pltpu.make_async_remote_copy(
                src_ref=source.at[pl.ds(0, 1)], dst_ref=box.at[pl.ds(d - 1, 1)],
                send_sem=sems.at[0], recv_sem=rems.at[0], device_id=peer, device_id_type=MESH)
            for d, peer in peers.items()
        ]

    def whole(box, peers, sems, rems):
        rows_in = box.at[pl.ds(0, len(peers))]
        return pltpu.make_async_remote_copy(
            src_ref=rows_in, dst_ref=rows_in, send_sem=sems.at[0], recv_sem=rems.at[0],
            device_id=peers[1], device_id_type=MESH)

    level1 = whole(box1, peers1, send1, recv1)
    level2 = whole(box2, peers2, send2, recv2)
    round1 = round_of(mine, box1, peers1, send1, recv1)
    round2 = round_of(mine2, box2, peers2, send2, recv2)
    tail, head = pl.ds((OWN - HALO) * 128, WIDE), pl.ds(0, WIDE)
    copies = []
    for peer, wide, short, targets in (
        (right, tail, pl.ds(16, 16), (ls, lm, ld, lp, lr)),
        (left, head, pl.ds(0, 16), (rs, rm, rd, rp, rr)),
    ):
        sources = (state.at[:, :, wide], metric.at[:, wide], depth.at[short], partner.at[short], refine.at[short])
        for source, target in zip(sources, targets):
            k = len(copies)
            copies.append(pltpu.make_async_remote_copy(
                src_ref=source, dst_ref=target, send_sem=send.at[k], recv_sem=recv.at[k],
                device_id=peer, device_id_type=MESH))

    onward, back = copies[:5], copies[5:]

    def each(batch, act):
        for copy in batch:
            act(copy)

    pl.semaphore_wait(barrier, len(everyone) + has_left.astype(i32) + has_right.astype(i32))
    for copy in round1:
        copy.start()
    pl.when(has_right)(lambda: each(onward, lambda copy: copy.start()))
    pl.when(has_left)(lambda: each(back, lambda copy: copy.start()))

    for load in loads[3:]:
        load.wait()
    ends = (me == 0, me == total - 1)
    weights(wd, wt, wl, tmp, wf)
    for t in range(OWN):
        lay_state(qt, BASE + t, sv, t)
    cv[BASE : BASE + OWN, :] = GRAVITY * dv[...]
    pv[BASE : BASE + OWN, :] = av[...]
    for t in range(4):
        lay_state(qt, RING + t, sv, t)
        lay_metric(mt, RING + t, gv, t)
    cv[RING : RING + 4, :] = GRAVITY * dv[0:4, :]
    pv[RING : RING + 4, :] = av[0:4, :]

    def first_rates(tiles):
        for i, m in enumerate(tiles):
            coefficients(m, mt, cv, pv, co)
            flux(m, qt, QP, state_row, mt, cv, pv, co, xt, 8 * (i % 2))
            product(m, 8 * (i % 2), xt, wl, r1)

    def second_rates(tiles):
        for i, m in enumerate(tiles):
            flux(m, r1, RP, result_row, mt, cv, pv, co, xt, 8 * (i % 2))
            product(m, 8 * (i % 2), xt, wl, r2)

    first_rates((BASE + 1, BASE + 9, BASE + 17, BASE + 23))
    second_rates((BASE + 2, BASE + 10, BASE + 18, BASE + 22))
    child_weights(wc, pw, tmp, wf)

    def earlier2(d):
        r, b = row - d // part, block - d % part
        r, b = jnp.where(r < 0, r + rows, r), jnp.where(b < 0, b + part, b)
        return r * part + b < row * part + block

    level1.wait_recv()
    own, before1 = joined(own, box1, low - 1, lambda d: d <= lo)
    mine2[0:1, :] = own
    for copy in round2:
        copy.start()
    pl.when(has_left)(lambda: each(onward, lambda copy: copy.wait_recv()))
    pl.when(has_right)(lambda: each(back, lambda copy: copy.wait_recv()))

    @pl.when(~has_left)
    def _():
        lr[...] = jnp.zeros_like(lr)

    @pl.when(~has_right)
    def _():
        rr[...] = jnp.zeros_like(rr)

    load_rims((ls, lm, ld, lp), (rs, rm, rd, rp), qt, mt, cv, pv, ends)
    mirror(qt, QP, state_row, mt, ends)
    first_rates((BASE + 30, BASE + 38, BASE + 46))
    mirror(r1, RP, result_row, mt, ends)
    second_rates((BASE + 30, BASE + 38, BASE + 44))
    r1[BASE * RP : BASE * RP + RR, :] = r1[RING * RP : RING * RP + RR, :]
    for t in range(2):
        r2[(BASE + t) * RP : (BASE + t) * RP + RR, :] = r2[(RING + t) * RP : (RING + t) * RP + RR, :]
    prefix(lr, bv, rr, rv, pk)
    tables(pk, pkw, tab)
    level1.wait_send()
    level2.wait_send()
    pl.when(has_right)(lambda: each(onward, lambda copy: copy.wait_send()))
    pl.when(has_left)(lambda: each(back, lambda copy: copy.wait_send()))
    level2.wait_recv()
    own, before2 = joined(own, box2, deep - 1, earlier2)
    best = jnp.where(half, own, pltpu.roll(own, 64, 1))
    before = before1 + before2
    before = jnp.where(half, pltpu.roll(before, 64, 1), before)
    stat[0:1, :] = before - (me * (OWN * 64)).astype(f32)
    step = COURANT / best
    combine(RING - 8, 0, step, qt, r1, r2, st)
    for g in range(5):
        combine(BASE + 8 * g, 8 + 8 * g, step, qt, r1, r2, st)


def wave_rate(depth, grads):
    gx, gy, hx, hy = grads
    lengths = [jnp.sqrt(vx * vx + vy * vy) for vx, vy in ((hx, hy), (gx + hx, gy + hy), (gx, gy))]
    return jnp.sqrt(GRAVITY * depth) * jnp.maximum(jnp.maximum(lengths[0], lengths[1]), lengths[2])


def lay_state(qt, m, s, t):
    for n in range(10):
        qt[m * QP + 4 * n : m * QP + 4 * n + 3, :] = s[n, :, t * 128 : (t + 1) * 128]


def lay_metric(mt, m, g, t):
    mt[m * MP : m * MP + 4, :] = g[:, t * 128 : (t + 1) * 128]


def load_rims(left, right, qt, mt, cv, pv, ends):
    ls, lm, ld, lp = left
    rs, rm, rd, rp = right

    def lay(m, s, g, t):
        lay_state(qt, m, s, t)
        lay_metric(mt, m, g, t)

    for t in range(HALO):
        lay(RING - HALO + t, ls, lm, t)
        lay(BASE + OWN + t, rs, rm, t)
    for into, before, after, scale in ((cv, ld, rd, GRAVITY), (pv, lp, rp, 1)):
        into[RING - HALO : RING, :] = scale * before[16 - HALO : 16, :]
        into[BASE + OWN : BASE + OWN + HALO, :] = scale * after[0:HALO, :]
    first, last = ends

    @pl.when(first)
    def _():
        cv[RING - 1 : RING, :] = pltpu.roll(cv[RING : RING + 1, :], 127, 1)

    @pl.when(last)
    def _():
        cv[BASE + OWN : BASE + OWN + 1, :] = pltpu.roll(cv[BASE + OWN - 1 : BASE + OWN, :], 1, 1)


def mirror(src, pitch, at, mt, ends):
    lane = lanes_of((1, 128))

    def row(tile, v):
        return src[tile * pitch + v : tile * pitch + v + 1, :]

    def grads(tile):
        return [mt[tile * MP + k : tile * MP + k + 1, :] for k in range(4)]

    def write(tile, rim, nodes, meet, gx, gy, shift, target):
        length = jnp.sqrt(gx * gx + gy * gy)
        nx, ny = gx / length, gy / length
        for j in range(4):
            eta, mx, my = (row(tile, at(f, nodes[j])) for f in range(3))
            normal = mx * nx + my * ny
            for f, value in enumerate((eta, mx - 2.0 * normal * nx, my - 2.0 * normal * ny)):
                v = at(f, meet[j])
                old = row(rim, v)
                src[rim * pitch + v : rim * pitch + v + 1, :] = jnp.where(
                    lane == target, pltpu.roll(value, shift, 1), old)

    first, last = ends

    @pl.when(first)
    def _():
        _, _, sx, sy = grads(RING)
        write(RING, RING - 1, FACES[0], MEET[0], -sx, -sy, 127, 127)

    @pl.when(last)
    def _():
        rx, ry, sx, sy = grads(BASE + OWN - 1)
        write(BASE + OWN - 1, BASE + OWN, FACES[1], MEET[1], rx + sx, ry + sy, 1, 0)


def shifts(partner):
    lane = lanes_of((8, 128))
    j = lane + partner
    idx, inside = j & 127, (j >= 0) & (j < 128)

    def before(own, prv, nxt):
        return pltpu.roll(jnp.where(lane == 127, prv, own), 1, 1)

    def after(own, prv, nxt):
        return pltpu.roll(jnp.where(lane == 0, nxt, own), 127, 1)

    def across(own, prv, nxt):
        return jnp.where(inside, pick(own, idx), pick(jnp.where(lane < 64, nxt, prv), idx))

    return before, after, across


def coefficients(m, mt, cv, pv, co):
    rx, ry, sx, sy = (spread(mt, k, m, MP) for k in range(4))
    partner = pv[m : m + 8, :]
    three = [cv[m + s : m + s + 8, :] for s in (0, -1, 1)]
    c = three[0]
    outer = [move(*three) for move in shifts(partner)]
    outer[2] = jnp.where(partner == 0, c, outer[2])
    for k, (gx, gy) in enumerate(((sx, sy), (rx + sx, ry + sy), (rx, ry))):
        length = jnp.sqrt(gx * gx + gy * gy)
        co[k, m : m + 8, :] = outer[k]
        co[3 + k, m : m + 8, :] = length * jnp.sqrt(jnp.maximum(c, outer[k]))
        if k == 2:
            co[6, m : m + 8, :] = gx / length
            co[7, m : m + 8, :] = gy / length


def flux(m, src, pitch, at, mt, cv, pv, co, xt, slot):
    rx, ry, sx, sy = (spread(mt, k, m, MP) for k in range(4))
    c = cv[m : m + 8, :]
    partner = pv[m : m + 8, :]
    wall = partner == 0
    moves = shifts(partner)

    def value(f, n, step=0):
        return spread(src, at(f, n), m + step, pitch)

    def store(f, k, x):
        put(xt, f * 32 + k, slot, XS, x)

    crx, cry, csx, csy = -c * rx, -c * ry, -c * sx, -c * sy
    for n in range(10):
        eta, mx, my = (value(f, n) for f in range(3))
        store(0, n, -(rx * mx + ry * my))
        store(0, 10 + n, -(sx * mx + sy * my))
        store(1, n, crx * eta)
        store(1, 10 + n, csx * eta)
        store(2, n, cry * eta)
        store(2, 10 + n, csy * eta)
    vectors = ((-sx, -sy), (rx + sx, ry + sy), (-rx, -ry))
    for k in range(3):
        gx, gy = vectors[k]
        ce = co[k, m : m + 8, :]
        scale = co[3 + k, m : m + 8, :]
        for j in range(4):
            inner = [value(f, FACES[k][j]) for f in range(3)]
            outer = []
            for f in range(3):
                node = MEET[k][j]
                own = value(f, node)
                prv = value(f, node, -1) if k != 1 else None
                nxt = value(f, node, 1) if k != 0 else None
                outer.append(moves[k](own, prv, nxt))
            if k == 2:
                outer[0] = jnp.where(wall, inner[0], outer[0])
            d_eta, d_mx, d_my = (b - a for a, b in zip(inner, outer))
            if k == 2:
                nx, ny = co[6, m : m + 8, :], co[7, m : m + 8, :]
                twice = -2.0 * (inner[1] * nx + inner[2] * ny)
                d_mx = jnp.where(wall, twice * nx, d_mx)
                d_my = jnp.where(wall, twice * ny, d_my)
            drop = c * inner[0] - ce * outer[0]
            row = 20 + 4 * k + j
            store(0, row, scale * d_eta - gx * d_mx - gy * d_my)
            store(1, row, gx * drop + scale * d_mx)
            store(2, row, gy * drop + scale * d_my)


def product(m, slot, xt, wl, out):
    for pair in range(4):
        parts = []
        for t in (2 * pair, 2 * pair + 1):
            hi, lo = split(xt[(slot + t) * XS : (slot + t) * XS + XP, :])
            parts.append(jnp.concatenate([hi, lo], axis=0))
        both = jnp.concatenate(parts, axis=1)
        res = jnp.dot(wl[:, 0 : 2 * XP], both, preferred_element_type=f32)
        res = res[0:32] + res[32:64]
        tile = m + 2 * pair
        out[tile * RP : tile * RP + RR, :] = res[:, 0:128]
        out[(tile + 1) * RP : (tile + 1) * RP + RR, :] = res[:, 128:256]


def weights(diff_ops, lift, wl, tmp, wf):
    wf[...] = jnp.zeros_like(wf)
    base = jnp.zeros((16, 128), f32)
    for i, shift in ((0, 0), (1, 10), (2, 20)):
        tmp[...] = jnp.zeros_like(tmp)
        if i == 2:
            tmp[0:10, 0:12] = 0.5 * lift[...]
        else:
            for n in range(10):
                tmp[n : n + 1, 0:10] = diff_ops[n, i : i + 1, :]
        base = base + (tmp[...] if shift == 0 else pltpu.roll(tmp[...], shift, 1))
    for f in range(3):
        turned = base if f == 0 else pltpu.roll(base, 32 * f, 1)
        wf[f * 10 : f * 10 + 10, :] = turned[0:10]
    w = wf[0:32, :]
    hi = w.astype(bf16).astype(f32)
    low = w - hi
    turned = pltpu.roll(hi, XP, 1)
    lane = lanes_of((32, 128))
    wl[0:32, 0:128] = (hi + jnp.where(lane >= XP, turned, 0.0)).astype(bf16)
    wl[0:32, 128:256] = jnp.where(lane < 64, turned, 0.0).astype(bf16)
    wl[32:64, 0:128] = low.astype(bf16)
    wl[32:64, 128:256] = jnp.zeros((32, 128), bf16)


def child_weights(prolong, pw, tmp, wf):
    for i in range(3):
        wf[...] = jnp.zeros_like(wf)
        tmp[...] = jnp.zeros_like(tmp)
        if i == 0:
            eye = lax.broadcasted_iota(i32, (16, 128), 0) == lanes_of((16, 128))
            tmp[0:10, :] = jnp.where(eye, 1.0, 0.0)[0:10]
        else:
            for n in range(10):
                tmp[n : n + 1, 0:10] = prolong[n, i - 1 : i, :]
        for f in range(3):
            turned = tmp[...] if f == 0 else pltpu.roll(tmp[...], 10 * f, 1)
            wf[pl.ds(f, 10, stride=4), :] = turned[0:10]
        w = wf[...]
        hi = w.astype(bf16).astype(f32)
        low = w - hi
        pw[i * 48 : i * 48 + 48, :] = (hi + pltpu.roll(hi, 32, 1) + pltpu.roll(low, 64, 1)).astype(bf16)


def combine(m, to, step, qt, r1, r2, st):
    half = 0.5 * step * step
    for f in range(3):
        for n in range(10):
            v = f * 10 + n
            x = spread(qt, state_row(f, n), m, QP) + (step * spread(r1, v, m, RP) + half * spread(r2, v, m, RP))
            put(st, v, to, RP, x)
    put(st, 30, to, RP, jnp.zeros((8, 128), f32))
    put(st, 31, to, RP, jnp.zeros((8, 128), f32))


def prefix(lr, refine, rr, rv, pk):
    rv[0:8, :] = lr[8:16, :]
    rv[8:40, :] = refine[...]
    rv[40:48, :] = rr[0:8, :]
    bits = rv[...]
    counts = (1 + bits).astype(f32)
    upper = lax.broadcasted_iota(i32, (128, 128), 0) <= lanes_of((128, 128))
    within = jnp.dot(counts.astype(bf16), upper.astype(f32).astype(bf16), preferred_element_type=f32)
    sums = jnp.broadcast_to(within[:, 127:128], (48, 128))
    lower = lanes_of((48, 48)) < lax.broadcasted_iota(i32, (48, 48), 0)
    before = jnp.dot(lower.astype(f32).astype(bf16), sums.astype(bf16), preferred_element_type=f32)
    ends = (within + before - before[8:9, :]).astype(i32)
    pk[...] = 2 * (ends - 1 - bits) + bits


def tables(pk, pkw, tab):
    row = lax.broadcasted_iota(i32, (48, 128), 0)
    ends = (pk[...] >> 1) + 1 + (pk[...] & 1)
    last = jnp.broadcast_to(ends[:, 127:128], (48, 128))
    reached = jnp.where(last <= lanes_of((48, 128)) * 128 - 1024, 1.0, 0.0)
    here = jnp.where(row == 0, 1.0, pltpu.roll(reached, 1, 0)) - reached
    after = jnp.where(row == 0, 0.0, pltpu.roll(here, 1, 0))
    shifted = pk[...] + 8192
    tiles = [(shifted >> 8), shifted & 255, row]
    tiles = jnp.concatenate([t.astype(f32).astype(bf16) for t in tiles], axis=1)
    for i, mark in enumerate((here, after)):
        found = jnp.dot(mark.T[0:64].astype(bf16), tiles, preferred_element_type=f32).astype(i32)
        pkw[i, :, :] = found[:, 0:128] * 256 + found[:, 128:256] - 8192
        if i == 0:
            pkw[2, :, :] = found[:, 256:384] * 128
    for g in range(8):
        rows = slice(8 * g, 8 * g + 8)
        p0, p1 = pkw[0, rows, :], pkw[1, rows, :]
        e0 = (p0 >> 1) + 1 + (p0 & 1)
        e1 = (p1 >> 1) + 1 + (p1 & 1)
        slot = (8 * g - 8 + lax.broadcasted_iota(i32, (8, 128), 0)) * 128 + lanes_of((8, 128))
        over = jnp.broadcast_to(e0[:, 127:128], (8, 128)) <= slot
        pos = jnp.zeros((8, 128), i32)
        for s in (64, 32, 16, 8, 4, 2, 1):
            probe = pos + (s - 1)
            e = jnp.where(over, pick(e1, probe), pick(e0, probe))
            pos = jnp.where(e <= slot, pos + s, pos)
        pos = jnp.minimum(pos, 127)
        got = jnp.where(over, pick(p1, pos), pick(p0, pos))
        which = slot - (got >> 1)
        parent = pkw[2, rows, :] + jnp.where(over, pos + 128, pos)
        tab[rows, :] = 4 * parent + jnp.where((got & 1) == 0, 0, 1 + which)


def aligned(offset, tab, near, code, lidx):
    near[0:8, :] = jnp.broadcast_to(1024 - offset.astype(i32), (8, 128))
    begin = near[0, 0]
    row, turn = jnp.clip(begin >> 7, 0, 16), begin & 127
    back = (128 - turn) & 127
    keep = lanes_of((8, 128)) >= turn
    for g in range(6):
        rows = slice(8 * g, 8 * g + 8)
        both = jnp.where(keep, tab[pl.ds(row + 8 * g, 8), :], tab[pl.ds(row + 8 * g + 1, 8), :])
        both = pltpu.roll(both, back, 1)
        tile = jnp.clip(jnp.broadcast_to(both[:, 0:1], (8, 128)) >> 9, 0, 47)
        lidx[rows, :] = (both >> 2) - tile * 128
        code[rows, :] = both & 3
        near[rows, :] = tile
    return [near[r, 0] for r in range(48)]


def place(tab, pw, stat, st, out, new_tiles, near, code, lidx, sems):
    tiles = aligned(stat[0:1, :], tab, near, code, lidx)
    weight = pw[:, 0:96]
    stores = []
    for pair in range(24):
        parts = []
        for r in (2 * pair, 2 * pair + 1):
            begin = tiles[r] * RP
            near_tile = st[pl.ds(begin, RR), :]
            far_tile = st[pl.ds(begin + RP, RR), :]
            idx = jnp.broadcast_to(lidx[r : r + 1, :], (RR, 128))
            low = idx & 127
            s = jnp.where(idx < 128, pick(near_tile, low), pick(far_tile, low))
            hi, lo = split(s)
            parts.append(jnp.concatenate([hi, lo, hi], axis=0))
        res = jnp.dot(weight, jnp.concatenate(parts, axis=1), preferred_element_type=f32)
        for i in range(2):
            r = 2 * pair + i
            one = res[:, 128 * i : 128 * i + 128]
            kind = jnp.broadcast_to(code[r : r + 1, :], (48, 128))
            new = jnp.where(kind == 0, one[0:48], jnp.where(kind == 1, one[48:96], one[96:144]))
            for n in range(10):
                new_tiles[n, :, r * 128 : (r + 1) * 128] = new[4 * n : 4 * n + 3]
        if pair in (7, 15, 20, 23):
            k = len(stores)
            begin = (0, 8, 16, 21)[k]
            part = pl.ds(begin * 256, (pair + 1 - begin) * 256)
            store = pltpu.make_async_copy(new_tiles.at[:, :, part], out.at[:, :, part], sems.at[k])
            store.start()
            stores.append(store)
    for store in stores:
        store.wait()


def solution(mesh):
    rows, cols = mesh.shape["row"], mesh.shape["col"]
    total = rows * cols
    low = min(16, cols // 2)
    high = total // low
    placed = OWN + OWN // 2

    def shards(state, depth, metric, partner, refine, diff_ops, lift, prolong):
        depth, partner, refine = (a.reshape(OWN, 128) for a in (depth, partner, refine))
        state, diff_ops, prolong = (a.transpose(1, 0, 2) for a in (state, diff_ops, prolong))
        args = (state, metric, depth, partner, refine, diff_ops, lift, prolong)
        vm, hbm = pl.BlockSpec(memory_space=pltpu.VMEM), pl.BlockSpec(memory_space=pl.ANY)
        side = [
            pltpu.VMEM((10, 3, WIDE), f32),
            pltpu.VMEM((4, WIDE), f32),
            pltpu.VMEM((16, 128), f32),
            pltpu.VMEM((16, 128), i32),
            pltpu.VMEM((16, 128), i32),
        ]
        st, tab, pw, stat = pl.pallas_call(
            functools.partial(advance, rows, cols, low),
            out_shape=[
                pltpu.VMEM((((placed + 1) * RP + 7) // 8 * 8, 128), f32),
                pltpu.VMEM((72, 128), i32),
                pltpu.VMEM((144, 128), bf16),
                pltpu.VMEM((8, 128), f32),
            ],
            in_specs=[hbm] * 8,
            out_specs=[vm] * 4,
            scratch_shapes=[pltpu.VMEM(a.shape, a.dtype) for a in args]
            + side
            + side
            + [
                pltpu.VMEM((MEM * QP, 128), f32),
                pltpu.VMEM((MEM * MP, 128), f32),
                pltpu.VMEM((MEM, 128), f32),
                pltpu.VMEM((MEM, 128), i32),
                pltpu.VMEM((8, MEM, 128), f32),
                pltpu.VMEM((16 * XS, 128), f32),
                pltpu.VMEM((MEM * RP, 128), f32),
                pltpu.VMEM((MEM * RP, 128), f32),
                pltpu.VMEM((64, 256), bf16),
                pltpu.VMEM((16, 128), f32),
                pltpu.VMEM((48, 128), f32),
                pltpu.VMEM((48, 128), i32),
                pltpu.VMEM((48, 128), i32),
                pltpu.VMEM((3, 64, 128), i32),
                pltpu.VMEM((8, 128), f32),
                pltpu.VMEM((low, 128), f32),
                pltpu.VMEM((8, 128), f32),
                pltpu.VMEM((high, 128), f32),
                pltpu.SemaphoreType.DMA((8,)),
                pltpu.SemaphoreType.DMA((10,)),
                pltpu.SemaphoreType.DMA((10,)),
                pltpu.SemaphoreType.DMA((1,)),
                pltpu.SemaphoreType.DMA((1,)),
                pltpu.SemaphoreType.DMA((1,)),
                pltpu.SemaphoreType.DMA((1,)),
            ],
            compiler_params=pltpu.CompilerParams(collective_id=0, has_side_effects=True),
            name="advance",
        )(*args)
        new = pl.pallas_call(
            place,
            out_shape=jax.ShapeDtypeStruct((10, 3, placed * 128), f32),
            in_specs=[vm] * 4,
            out_specs=hbm,
            scratch_shapes=[
                pltpu.VMEM((10, 3, placed * 128), f32),
                pltpu.VMEM((48, 128), i32),
                pltpu.VMEM((48, 128), i32),
                pltpu.VMEM((48, 128), i32),
                pltpu.SemaphoreType.DMA((4,)),
            ],
            name="place",
        )(*(pltpu.with_memory_space_constraint(a, pltpu.VMEM) for a in (tab, pw, stat, st)))
        return new.transpose(1, 0, 2)

    halves = ("row", "col")
    return jax.shard_map(
        shards,
        mesh=mesh,
        in_specs=(P(None, None, halves), P(halves), P(None, halves), P(halves), P(halves), P(), P(), P()),
        out_specs=P(None, None, halves),
        check_vma=False,
    )
```

```python
import functools

import jax
import jax.numpy as jnp
from jax import lax
from jax.experimental import pallas as pl
from jax.experimental.pallas import tpu as pltpu
from jax.sharding import PartitionSpec as P

GRAVITY = 9.81
COURANT = 0.5
MESH = pl.DeviceIdType.MESH

OWN = 32
HALO = 9
WIDE = HALO * 128
BASE = 2
RING = BASE + OWN + 2 * HALO
MEM = 64
QP = 41
RR = 32
RP = 33
MP = 9
XP = 96
XS = 97

FACES = ((0, 1, 2, 3), (3, 6, 8, 9), (9, 7, 4, 0))
MEET = ((9, 8, 6, 3), (3, 2, 1, 0), (0, 4, 7, 9))

f32 = jnp.float32
bf16 = jnp.bfloat16
i32 = jnp.int32


def lanes_of(shape):
    return lax.broadcasted_iota(i32, shape, len(shape) - 1)


def state_row(f, n):
    return 4 * n + f


def result_row(f, n):
    return 10 * f + n


def spread(ref, v, tile, pitch):
    return ref[pl.ds(tile * pitch + v, 8, stride=pitch), :]


def put(ref, v, tile, pitch, value):
    ref[pl.ds(tile * pitch + v, 8, stride=pitch), :] = value


def pick(x, idx):
    return jnp.take_along_axis(x, idx, axis=1, mode="promise_in_bounds")


def split(x):
    hi = x.astype(bf16)
    return hi, (x - hi.astype(f32)).astype(bf16)


def joined(own, box, members, earlier):
    part = box[0:members, :]
    best = jnp.maximum(own, jnp.max(part, axis=0, keepdims=True))
    both = own + jnp.sum(part, axis=0, keepdims=True)
    d = lax.broadcasted_iota(i32, part.shape, 0) + 1
    before = jnp.sum(jnp.where(earlier(d), part, 0.0), axis=0, keepdims=True)
    return jnp.where(lanes_of((1, 128)) < 64, best, both), before


def advance(
    rows, cols, low,
    state, metric, depth, partner, refine, diff_ops, lift, prolong,
    st, tab, pw, stat,
    sv, gv, dv, av, bv, wd, wt, wc,
    ls, lm, ld, lp, lr, rs, rm, rd, rp, rr,
    qt, mt, cv, pv, co, xt, r1, r2, wl, tmp, wf, rv, pk, pkw,
    mine, box1, mine2, box2,
    here, send, recv, send1, recv1, send2, recv2,
):
    total = rows * cols
    part, deep = cols // low, rows * (cols // low)
    row, col = lax.axis_index("row"), lax.axis_index("col")
    me = row * cols + col
    block, lo = col // low, lax.rem(col, low)

    def wrapped(x, n):
        return jnp.where(x >= n, x - n, x)

    def hops(d, n):
        return min(d, n - d)

    over = wrapped(col + 1, cols)
    under = wrapped(col + cols - 1, cols)
    right = (jnp.where(over == 0, wrapped(row + 1, rows), row), over)
    left = (jnp.where(col == 0, wrapped(row + rows - 1, rows), row), under)
    has_left, has_right = me != 0, me != total - 1
    close = sorted(range(1, low), key=lambda d: -hops(d // 2, low // 2))
    peers1 = {d: (row, block * low + wrapped(lo + d, low)) for d in close}
    row_at = [wrapped(row + d, rows) for d in range(rows)]
    col_at = [wrapped(block + d, part) * low + lo for d in range(part)]
    far = sorted(range(1, deep), key=lambda d: -hops(d // part, rows) - hops(d % part, part))
    peers2 = {d: (row_at[d // part], col_at[d % part]) for d in far}
    everyone = [peers1[d] for d in close] + [peers2[d] for d in far]

    pairs = (
        (metric, gv), (depth, dv), (refine, bv), (state, sv), (partner, av), (diff_ops, wd), (lift, wt), (prolong, wc))
    loads = [pltpu.make_async_copy(a, b, here.at[k]) for k, (a, b) in enumerate(pairs)]
    for load in loads[:3]:
        load.start()
    barrier = pltpu.get_barrier_semaphore()
    for peer in everyone:
        pl.semaphore_signal(barrier, inc=1, device_id=peer, device_id_type=MESH)

    @pl.when(has_left)
    def _():
        pl.semaphore_signal(barrier, inc=1, device_id=left, device_id_type=MESH)

    @pl.when(has_right)
    def _():
        pl.semaphore_signal(barrier, inc=1, device_id=right, device_id_type=MESH)

    for load in loads[3:]:
        load.start()
    for load in loads[:3]:
        load.wait()
    for t in range(OWN):
        lay_metric(mt, BASE + t, gv, t)
    grads = [mt[pl.ds(BASE * MP + k, OWN, stride=MP), :] for k in range(4)]
    rate = wave_rate(dv[...], grads)
    top = jnp.max(jnp.max(rate, axis=0, keepdims=True), axis=1, keepdims=True)
    count = jnp.sum(bv[...].astype(f32), axis=0, keepdims=True)
    count = jnp.sum(count, axis=1, keepdims=True)
    half = lanes_of((1, 128)) < 64
    own = jnp.where(half, top, count)
    mine[0:1, :] = own

    def round_of(source, box, peers, sems, rems):
        return [
            pltpu.make_async_remote_copy(
                src_ref=source.at[pl.ds(0, 1)], dst_ref=box.at[pl.ds(d - 1, 1)],
                send_sem=sems.at[0], recv_sem=rems.at[0], device_id=peer, device_id_type=MESH)
            for d, peer in peers.items()
        ]

    def whole(box, peers, sems, rems):
        rows_in = box.at[pl.ds(0, len(peers))]
        return pltpu.make_async_remote_copy(
            src_ref=rows_in, dst_ref=rows_in, send_sem=sems.at[0], recv_sem=rems.at[0],
            device_id=peers[1], device_id_type=MESH)

    level1 = whole(box1, peers1, send1, recv1)
    level2 = whole(box2, peers2, send2, recv2)
    round1 = round_of(mine, box1, peers1, send1, recv1)
    round2 = round_of(mine2, box2, peers2, send2, recv2)
    tail, head = pl.ds((OWN - HALO) * 128, WIDE), pl.ds(0, WIDE)
    copies = []
    for peer, wide, short, targets in (
        (right, tail, pl.ds(16, 16), (ls, lm, ld, lp, lr)),
        (left, head, pl.ds(0, 16), (rs, rm, rd, rp, rr)),
    ):
        sources = (state.at[:, :, wide], metric.at[:, wide], depth.at[short], partner.at[short], refine.at[short])
        for source, target in zip(sources, targets):
            k = len(copies)
            copies.append(pltpu.make_async_remote_copy(
                src_ref=source, dst_ref=target, send_sem=send.at[k], recv_sem=recv.at[k],
                device_id=peer, device_id_type=MESH))

    onward, back = copies[:5], copies[5:]

    def each(batch, act):
        for copy in batch:
            act(copy)

    pl.semaphore_wait(barrier, len(everyone) + has_left.astype(i32) + has_right.astype(i32))
    for copy in round1:
        copy.start()
    pl.when(has_right)(lambda: each(onward, lambda copy: copy.start()))
    pl.when(has_left)(lambda: each(back, lambda copy: copy.start()))

    for load in loads[3:]:
        load.wait()
    ends = (me == 0, me == total - 1)
    weights(wd, wt, wl, tmp, wf)
    for t in range(OWN):
        lay_state(qt, BASE + t, sv, t)
    cv[BASE : BASE + OWN, :] = GRAVITY * dv[...]
    pv[BASE : BASE + OWN, :] = av[...]
    for t in range(4):
        lay_state(qt, RING + t, sv, t)
        lay_metric(mt, RING + t, gv, t)
    cv[RING : RING + 4, :] = GRAVITY * dv[0:4, :]
    pv[RING : RING + 4, :] = av[0:4, :]

    def first_rates(tiles):
        for i, m in enumerate(tiles):
            coefficients(m, mt, cv, pv, co)
            flux(m, qt, QP, state_row, mt, cv, pv, co, xt, 8 * (i % 2))
            product(m, 8 * (i % 2), xt, wl, r1)

    def second_rates(tiles):
        for i, m in enumerate(tiles):
            flux(m, r1, RP, result_row, mt, cv, pv, co, xt, 8 * (i % 2))
            product(m, 8 * (i % 2), xt, wl, r2)

    first_rates((BASE + 1, BASE + 9, BASE + 17, BASE + 23))
    second_rates((BASE + 2, BASE + 10, BASE + 18, BASE + 22))
    child_weights(wc, pw, tmp, wf)

    def earlier2(d):
        r, b = row - d // part, block - d % part
        r, b = jnp.where(r < 0, r + rows, r), jnp.where(b < 0, b + part, b)
        return r * part + b < row * part + block

    level1.wait_recv()
    own, before1 = joined(own, box1, low - 1, lambda d: d <= lo)
    mine2[0:1, :] = own
    for copy in round2:
        copy.start()
    pl.when(has_left)(lambda: each(onward, lambda copy: copy.wait_recv()))
    pl.when(has_right)(lambda: each(back, lambda copy: copy.wait_recv()))

    @pl.when(~has_left)
    def _():
        lr[...] = jnp.zeros_like(lr)

    @pl.when(~has_right)
    def _():
        rr[...] = jnp.zeros_like(rr)

    load_rims((ls, lm, ld, lp), (rs, rm, rd, rp), qt, mt, cv, pv, ends)
    mirror(qt, QP, state_row, mt, ends)
    first_rates((BASE + 30, BASE + 38, BASE + 46))
    mirror(r1, RP, result_row, mt, ends)
    second_rates((BASE + 30, BASE + 38, BASE + 44))
    r1[BASE * RP : BASE * RP + RR, :] = r1[RING * RP : RING * RP + RR, :]
    for t in range(2):
        r2[(BASE + t) * RP : (BASE + t) * RP + RR, :] = r2[(RING + t) * RP : (RING + t) * RP + RR, :]
    prefix(lr, bv, rr, rv, pk)
    tables(pk, pkw, tab)
    level1.wait_send()
    level2.wait_send()
    pl.when(has_right)(lambda: each(onward, lambda copy: copy.wait_send()))
    pl.when(has_left)(lambda: each(back, lambda copy: copy.wait_send()))
    level2.wait_recv()
    own, before2 = joined(own, box2, deep - 1, earlier2)
    best = jnp.where(half, own, pltpu.roll(own, 64, 1))
    before = before1 + before2
    before = jnp.where(half, pltpu.roll(before, 64, 1), before)
    stat[0:1, :] = before - (me * (OWN * 64)).astype(f32)
    step = COURANT / best
    combine(RING - 8, 0, step, qt, r1, r2, st)
    for g in range(5):
        combine(BASE + 8 * g, 8 + 8 * g, step, qt, r1, r2, st)


def wave_rate(depth, grads):
    gx, gy, hx, hy = grads
    lengths = [jnp.sqrt(vx * vx + vy * vy) for vx, vy in ((hx, hy), (gx + hx, gy + hy), (gx, gy))]
    return jnp.sqrt(GRAVITY * depth) * jnp.maximum(jnp.maximum(lengths[0], lengths[1]), lengths[2])


def lay_state(qt, m, s, t):
    for n in range(10):
        qt[m * QP + 4 * n : m * QP + 4 * n + 3, :] = s[n, :, t * 128 : (t + 1) * 128]


def lay_metric(mt, m, g, t):
    mt[m * MP : m * MP + 4, :] = g[:, t * 128 : (t + 1) * 128]


def load_rims(left, right, qt, mt, cv, pv, ends):
    ls, lm, ld, lp = left
    rs, rm, rd, rp = right

    def lay(m, s, g, t):
        lay_state(qt, m, s, t)
        lay_metric(mt, m, g, t)

    for t in range(HALO):
        lay(RING - HALO + t, ls, lm, t)
        lay(BASE + OWN + t, rs, rm, t)
    for into, before, after, scale in ((cv, ld, rd, GRAVITY), (pv, lp, rp, 1)):
        into[RING - HALO : RING, :] = scale * before[16 - HALO : 16, :]
        into[BASE + OWN : BASE + OWN + HALO, :] = scale * after[0:HALO, :]
    first, last = ends

    @pl.when(first)
    def _():
        cv[RING - 1 : RING, :] = pltpu.roll(cv[RING : RING + 1, :], 127, 1)

    @pl.when(last)
    def _():
        cv[BASE + OWN : BASE + OWN + 1, :] = pltpu.roll(cv[BASE + OWN - 1 : BASE + OWN, :], 1, 1)


def mirror(src, pitch, at, mt, ends):
    lane = lanes_of((1, 128))

    def row(tile, v):
        return src[tile * pitch + v : tile * pitch + v + 1, :]

    def grads(tile):
        return [mt[tile * MP + k : tile * MP + k + 1, :] for k in range(4)]

    def write(tile, rim, nodes, meet, gx, gy, shift, target):
        length = jnp.sqrt(gx * gx + gy * gy)
        nx, ny = gx / length, gy / length
        for j in range(4):
            eta, mx, my = (row(tile, at(f, nodes[j])) for f in range(3))
            normal = mx * nx + my * ny
            for f, value in enumerate((eta, mx - 2.0 * normal * nx, my - 2.0 * normal * ny)):
                v = at(f, meet[j])
                old = row(rim, v)
                src[rim * pitch + v : rim * pitch + v + 1, :] = jnp.where(
                    lane == target, pltpu.roll(value, shift, 1), old)

    first, last = ends

    @pl.when(first)
    def _():
        _, _, sx, sy = grads(RING)
        write(RING, RING - 1, FACES[0], MEET[0], -sx, -sy, 127, 127)

    @pl.when(last)
    def _():
        rx, ry, sx, sy = grads(BASE + OWN - 1)
        write(BASE + OWN - 1, BASE + OWN, FACES[1], MEET[1], rx + sx, ry + sy, 1, 0)


def shifts(partner):
    lane = lanes_of((8, 128))
    j = lane + partner
    idx, inside = j & 127, (j >= 0) & (j < 128)

    def before(own, prv, nxt):
        return pltpu.roll(jnp.where(lane == 127, prv, own), 1, 1)

    def after(own, prv, nxt):
        return pltpu.roll(jnp.where(lane == 0, nxt, own), 127, 1)

    def across(own, prv, nxt):
        return jnp.where(inside, pick(own, idx), pick(jnp.where(lane < 64, nxt, prv), idx))

    return before, after, across


def coefficients(m, mt, cv, pv, co):
    rx, ry, sx, sy = (spread(mt, k, m, MP) for k in range(4))
    partner = pv[m : m + 8, :]
    three = [cv[m + s : m + s + 8, :] for s in (0, -1, 1)]
    c = three[0]
    outer = [move(*three) for move in shifts(partner)]
    outer[2] = jnp.where(partner == 0, c, outer[2])
    for k, (gx, gy) in enumerate(((sx, sy), (rx + sx, ry + sy), (rx, ry))):
        length = jnp.sqrt(gx * gx + gy * gy)
        co[k, m : m + 8, :] = outer[k]
        co[3 + k, m : m + 8, :] = length * jnp.sqrt(jnp.maximum(c, outer[k]))
        if k == 2:
            co[6, m : m + 8, :] = gx / length
            co[7, m : m + 8, :] = gy / length


def flux(m, src, pitch, at, mt, cv, pv, co, xt, slot):
    rx, ry, sx, sy = (spread(mt, k, m, MP) for k in range(4))
    c = cv[m : m + 8, :]
    partner = pv[m : m + 8, :]
    wall = partner == 0
    moves = shifts(partner)

    def value(f, n, step=0):
        return spread(src, at(f, n), m + step, pitch)

    def store(f, k, x):
        put(xt, f * 32 + k, slot, XS, x)

    crx, cry, csx, csy = -c * rx, -c * ry, -c * sx, -c * sy
    for n in range(10):
        eta, mx, my = (value(f, n) for f in range(3))
        store(0, n, -(rx * mx + ry * my))
        store(0, 10 + n, -(sx * mx + sy * my))
        store(1, n, crx * eta)
        store(1, 10 + n, csx * eta)
        store(2, n, cry * eta)
        store(2, 10 + n, csy * eta)
    vectors = ((-sx, -sy), (rx + sx, ry + sy), (-rx, -ry))
    for k in range(3):
        gx, gy = vectors[k]
        ce = co[k, m : m + 8, :]
        scale = co[3 + k, m : m + 8, :]
        for j in range(4):
            inner = [value(f, FACES[k][j]) for f in range(3)]
            outer = []
            for f in range(3):
                node = MEET[k][j]
                own = value(f, node)
                prv = value(f, node, -1) if k != 1 else None
                nxt = value(f, node, 1) if k != 0 else None
                outer.append(moves[k](own, prv, nxt))
            if k == 2:
                outer[0] = jnp.where(wall, inner[0], outer[0])
            d_eta, d_mx, d_my = (b - a for a, b in zip(inner, outer))
            if k == 2:
                nx, ny = co[6, m : m + 8, :], co[7, m : m + 8, :]
                twice = -2.0 * (inner[1] * nx + inner[2] * ny)
                d_mx = jnp.where(wall, twice * nx, d_mx)
                d_my = jnp.where(wall, twice * ny, d_my)
            drop = c * inner[0] - ce * outer[0]
            row = 20 + 4 * k + j
            store(0, row, scale * d_eta - gx * d_mx - gy * d_my)
            store(1, row, gx * drop + scale * d_mx)
            store(2, row, gy * drop + scale * d_my)


def product(m, slot, xt, wl, out):
    for pair in range(4):
        parts = []
        for t in (2 * pair, 2 * pair + 1):
            hi, lo = split(xt[(slot + t) * XS : (slot + t) * XS + XP, :])
            parts.append(jnp.concatenate([hi, lo], axis=0))
        both = jnp.concatenate(parts, axis=1)
        res = jnp.dot(wl[:, 0 : 2 * XP], both, preferred_element_type=f32)
        res = res[0:32] + res[32:64]
        tile = m + 2 * pair
        out[tile * RP : tile * RP + RR, :] = res[:, 0:128]
        out[(tile + 1) * RP : (tile + 1) * RP + RR, :] = res[:, 128:256]


def weights(diff_ops, lift, wl, tmp, wf):
    wf[...] = jnp.zeros_like(wf)
    base = jnp.zeros((16, 128), f32)
    for i, shift in ((0, 0), (1, 10), (2, 20)):
        tmp[...] = jnp.zeros_like(tmp)
        if i == 2:
            tmp[0:10, 0:12] = 0.5 * lift[...]
        else:
            for n in range(10):
                tmp[n : n + 1, 0:10] = diff_ops[n, i : i + 1, :]
        base = base + (tmp[...] if shift == 0 else pltpu.roll(tmp[...], shift, 1))
    for f in range(3):
        turned = base if f == 0 else pltpu.roll(base, 32 * f, 1)
        wf[f * 10 : f * 10 + 10, :] = turned[0:10]
    w = wf[0:32, :]
    hi = w.astype(bf16).astype(f32)
    low = w - hi
    turned = pltpu.roll(hi, XP, 1)
    lane = lanes_of((32, 128))
    wl[0:32, 0:128] = (hi + jnp.where(lane >= XP, turned, 0.0)).astype(bf16)
    wl[0:32, 128:256] = jnp.where(lane < 64, turned, 0.0).astype(bf16)
    wl[32:64, 0:128] = low.astype(bf16)
    wl[32:64, 128:256] = jnp.zeros((32, 128), bf16)


def child_weights(prolong, pw, tmp, wf):
    halves = []
    for i in range(3):
        wf[...] = jnp.zeros_like(wf)
        tmp[...] = jnp.zeros_like(tmp)
        if i == 0:
            eye = lax.broadcasted_iota(i32, (16, 128), 0) == lanes_of((16, 128))
            tmp[0:10, :] = jnp.where(eye, 1.0, 0.0)[0:10]
        else:
            for n in range(10):
                tmp[n : n + 1, 0:10] = prolong[n, i - 1 : i, :]
        for f in range(3):
            turned = tmp[...] if f == 0 else pltpu.roll(tmp[...], 10 * f, 1)
            wf[pl.ds(f, 10, stride=4), :] = turned[0:10]
        w = wf[...]
        hi = w.astype(bf16).astype(f32)
        low = w - hi
        halves += [hi, low]
    eye, _, one, one_low, two, two_low = halves
    first = (eye, eye, one, one)
    rest = (one_low, two, two, two_low)
    for k, four in enumerate((first, rest)):
        total = four[0]
        for j in range(1, 4):
            total = total + pltpu.roll(four[j], 32 * j, 1)
        pw[:, 128 * k : 128 * k + 128] = total.astype(bf16)


def combine(m, to, step, qt, r1, r2, st):
    half = 0.5 * step * step
    for f in range(3):
        for n in range(10):
            v = f * 10 + n
            x = spread(qt, state_row(f, n), m, QP) + (step * spread(r1, v, m, RP) + half * spread(r2, v, m, RP))
            put(st, v, to, RP, x)
    put(st, 30, to, RP, jnp.zeros((8, 128), f32))
    put(st, 31, to, RP, jnp.zeros((8, 128), f32))


def prefix(lr, refine, rr, rv, pk):
    rv[0:8, :] = lr[8:16, :]
    rv[8:40, :] = refine[...]
    rv[40:48, :] = rr[0:8, :]
    bits = rv[...]
    counts = (1 + bits).astype(f32)
    upper = lax.broadcasted_iota(i32, (128, 128), 0) <= lanes_of((128, 128))
    within = jnp.dot(counts.astype(bf16), upper.astype(f32).astype(bf16), preferred_element_type=f32)
    sums = jnp.broadcast_to(within[:, 127:128], (48, 128))
    lower = lanes_of((48, 48)) < lax.broadcasted_iota(i32, (48, 48), 0)
    before = jnp.dot(lower.astype(f32).astype(bf16), sums.astype(bf16), preferred_element_type=f32)
    ends = (within + before - before[8:9, :]).astype(i32)
    pk[...] = 2 * (ends - 1 - bits) + bits


def tables(pk, pkw, tab):
    row = lax.broadcasted_iota(i32, (48, 128), 0)
    ends = (pk[...] >> 1) + 1 + (pk[...] & 1)
    last = jnp.broadcast_to(ends[:, 127:128], (48, 128))
    reached = jnp.where(last <= lanes_of((48, 128)) * 128 - 1024, 1.0, 0.0)
    here = jnp.where(row == 0, 1.0, pltpu.roll(reached, 1, 0)) - reached
    after = jnp.where(row == 0, 0.0, pltpu.roll(here, 1, 0))
    shifted = pk[...] + 8192
    tiles = [(shifted >> 8), shifted & 255, row]
    tiles = jnp.concatenate([t.astype(f32).astype(bf16) for t in tiles], axis=1)
    for i, mark in enumerate((here, after)):
        found = jnp.dot(mark.T[0:64].astype(bf16), tiles, preferred_element_type=f32).astype(i32)
        pkw[i, :, :] = found[:, 0:128] * 256 + found[:, 128:256] - 8192
        if i == 0:
            pkw[2, :, :] = found[:, 256:384] * 128
    for g in range(8):
        rows = slice(8 * g, 8 * g + 8)
        p0, p1 = pkw[0, rows, :], pkw[1, rows, :]
        e0 = (p0 >> 1) + 1 + (p0 & 1)
        e1 = (p1 >> 1) + 1 + (p1 & 1)
        slot = (8 * g - 8 + lax.broadcasted_iota(i32, (8, 128), 0)) * 128 + lanes_of((8, 128))
        over = jnp.broadcast_to(e0[:, 127:128], (8, 128)) <= slot
        pos = jnp.zeros((8, 128), i32)
        for s in (64, 32, 16, 8, 4, 2, 1):
            probe = pos + (s - 1)
            e = jnp.where(over, pick(e1, probe), pick(e0, probe))
            pos = jnp.where(e <= slot, pos + s, pos)
        pos = jnp.minimum(pos, 127)
        got = jnp.where(over, pick(p1, pos), pick(p0, pos))
        which = slot - (got >> 1)
        parent = pkw[2, rows, :] + jnp.where(over, pos + 128, pos)
        tab[rows, :] = 4 * parent + jnp.where((got & 1) == 0, 0, 1 + which)


def aligned(offset, tab, near, code, lidx):
    near[0:8, :] = jnp.broadcast_to(1024 - offset.astype(i32), (8, 128))
    begin = near[0, 0]
    row, turn = jnp.clip(begin >> 7, 0, 16), begin & 127
    back = (128 - turn) & 127
    keep = lanes_of((8, 128)) >= turn
    for g in range(6):
        rows = slice(8 * g, 8 * g + 8)
        both = jnp.where(keep, tab[pl.ds(row + 8 * g, 8), :], tab[pl.ds(row + 8 * g + 1, 8), :])
        both = pltpu.roll(both, back, 1)
        tile = jnp.clip(jnp.broadcast_to(both[:, 0:1], (8, 128)) >> 9, 0, 47)
        lidx[rows, :] = (both >> 2) - tile * 128
        code[rows, :] = both & 3
        near[rows, :] = tile
    return [near[r, 0] for r in range(48)]


def place(tab, pw, stat, st, out, new_tiles, near, code, lidx, sems):
    tiles = aligned(stat[0:1, :], tab, near, code, lidx)
    weight = pw[...]
    stores = []
    for pair in range(24):
        parts = []
        for r in (2 * pair, 2 * pair + 1):
            begin = tiles[r] * RP
            near_tile = st[pl.ds(begin, RR), :]
            far_tile = st[pl.ds(begin + RP, RR), :]
            idx = jnp.broadcast_to(lidx[r : r + 1, :], (RR, 128))
            low = idx & 127
            s = jnp.where(idx < 128, pick(near_tile, low), pick(far_tile, low))
            hi, lo = split(s)
            kind = jnp.broadcast_to(code[r : r + 1, :], (16, 128))
            rows = []
            for j in range(3):
                only = jnp.where(kind == j, 1.0, 0.0).astype(bf16)
                only = jnp.concatenate([only, only], axis=0)
                rows += [hi * only, lo * only]
            rows = rows[0:4] + [rows[2]] + rows[4:6] + [rows[4]]
            parts.append(jnp.concatenate(rows, axis=0))
        res = jnp.dot(weight, jnp.concatenate(parts, axis=1), preferred_element_type=f32)
        for i in range(2):
            r = 2 * pair + i
            new = res[:, 128 * i : 128 * i + 128]
            for n in range(10):
                new_tiles[n, :, r * 128 : (r + 1) * 128] = new[4 * n : 4 * n + 3]
        if pair in (7, 15, 20, 23):
            k = len(stores)
            begin = (0, 8, 16, 21)[k]
            part = pl.ds(begin * 256, (pair + 1 - begin) * 256)
            store = pltpu.make_async_copy(new_tiles.at[:, :, part], out.at[:, :, part], sems.at[k])
            store.start()
            stores.append(store)
    for store in stores:
        store.wait()


def solution(mesh):
    rows, cols = mesh.shape["row"], mesh.shape["col"]
    total = rows * cols
    low = min(16, cols // 2)
    high = total // low
    placed = OWN + OWN // 2

    def shards(state, depth, metric, partner, refine, diff_ops, lift, prolong):
        depth, partner, refine = (a.reshape(OWN, 128) for a in (depth, partner, refine))
        state, diff_ops, prolong = (a.transpose(1, 0, 2) for a in (state, diff_ops, prolong))
        args = (state, metric, depth, partner, refine, diff_ops, lift, prolong)
        vm, hbm = pl.BlockSpec(memory_space=pltpu.VMEM), pl.BlockSpec(memory_space=pl.ANY)
        side = [
            pltpu.VMEM((10, 3, WIDE), f32),
            pltpu.VMEM((4, WIDE), f32),
            pltpu.VMEM((16, 128), f32),
            pltpu.VMEM((16, 128), i32),
            pltpu.VMEM((16, 128), i32),
        ]
        st, tab, pw, stat = pl.pallas_call(
            functools.partial(advance, rows, cols, low),
            out_shape=[
                pltpu.VMEM((((placed + 1) * RP + 7) // 8 * 8, 128), f32),
                pltpu.VMEM((72, 128), i32),
                pltpu.VMEM((48, 256), bf16),
                pltpu.VMEM((8, 128), f32),
            ],
            in_specs=[hbm] * 8,
            out_specs=[vm] * 4,
            scratch_shapes=[pltpu.VMEM(a.shape, a.dtype) for a in args]
            + side
            + side
            + [
                pltpu.VMEM((MEM * QP, 128), f32),
                pltpu.VMEM((MEM * MP, 128), f32),
                pltpu.VMEM((MEM, 128), f32),
                pltpu.VMEM((MEM, 128), i32),
                pltpu.VMEM((8, MEM, 128), f32),
                pltpu.VMEM((16 * XS, 128), f32),
                pltpu.VMEM((MEM * RP, 128), f32),
                pltpu.VMEM((MEM * RP, 128), f32),
                pltpu.VMEM((64, 256), bf16),
                pltpu.VMEM((16, 128), f32),
                pltpu.VMEM((48, 128), f32),
                pltpu.VMEM((48, 128), i32),
                pltpu.VMEM((48, 128), i32),
                pltpu.VMEM((3, 64, 128), i32),
                pltpu.VMEM((8, 128), f32),
                pltpu.VMEM((low, 128), f32),
                pltpu.VMEM((8, 128), f32),
                pltpu.VMEM((high, 128), f32),
                pltpu.SemaphoreType.DMA((8,)),
                pltpu.SemaphoreType.DMA((10,)),
                pltpu.SemaphoreType.DMA((10,)),
                pltpu.SemaphoreType.DMA((1,)),
                pltpu.SemaphoreType.DMA((1,)),
                pltpu.SemaphoreType.DMA((1,)),
                pltpu.SemaphoreType.DMA((1,)),
            ],
            compiler_params=pltpu.CompilerParams(collective_id=0, has_side_effects=True),
            name="advance",
        )(*args)
        new = pl.pallas_call(
            place,
            out_shape=jax.ShapeDtypeStruct((10, 3, placed * 128), f32),
            in_specs=[vm] * 4,
            out_specs=hbm,
            scratch_shapes=[
                pltpu.VMEM((10, 3, placed * 128), f32),
                pltpu.VMEM((48, 128), i32),
                pltpu.VMEM((48, 128), i32),
                pltpu.VMEM((48, 128), i32),
                pltpu.SemaphoreType.DMA((4,)),
            ],
            name="place",
        )(*(pltpu.with_memory_space_constraint(a, pltpu.VMEM) for a in (tab, pw, stat, st)))
        return new.transpose(1, 0, 2)

    halves = ("row", "col")
    return jax.shard_map(
        shards,
        mesh=mesh,
        in_specs=(P(None, None, halves), P(halves), P(None, halves), P(halves), P(halves), P(), P(), P()),
        out_specs=P(None, None, halves),
        check_vma=False,
    )
```
